32 devices in a mesh: space: 8 (over y, x, core), members: 4 (over z).
Axes of the slice: x: 2, y: 2, z: 4, core: 2. Of those that a mesh axis runs over, the one named last changes fastest.
Arguments:
- ensemble: bfloat16 [128, 65536], P('members', 'space'), may hold values from -6 to 6
- op_blocks: bfloat16 [512, 3, 128, 128], P('space'), may hold values from -0.3125 to 0.3125
- col_index: int32 [512, 2], P('space'), may hold values from 0 to 511, as said below
- weights: float32 [128, 512], P('members', 'space')
- innovations: float32 [2, 65536], P(None, 'space'), may hold values from -6 to 6
- obs_precision: float32 [2, 65536], P(None, 'space'), may hold values from 0.25 to 4
Outputs:
- grad_ens: float32 [128, 65536], P('members', 'space')
- direction: float32 [128, 512], P('members', 'space')
The draws below stay inside these ranges and needn't reach their ends.
Inputs may be any that keep to these rules, and one draw needn't show every extreme that they name: col_index[r, 0] lies in [r - 32, r - 1] and col_index[r, 1] in [r + 1, r + 32], each clipped to the grid; in every aligned run of 64 block-rows some row reaches back by exactly 32 and some row forward by exactly 32, before clipping.
All inputs are finite; a program needn't handle non-finite values.
Results may differ from the reference program's by a relative error of at most 0.011.
Values may be sent and summed in bfloat16 or wider, within the bound.
No kernel may reach another device: no remote copies, remote signals or barrier semaphores. Data moves between devices by JAX's collectives and lax.ppermute only.
A program may use at most 64 MiB of HBM per device.

```python
import math
import jax
import jax.numpy as jnp
from jax import lax

BS = 128
NNZ = 3
MEMBERS = 128
BLK_DEV = 64
REACH = 32
NBLK = 512
NROWS = 65536


def draw_col_index(key, part):
    row_ids = jnp.arange(NBLK, dtype=jnp.int32)
    tile_ids = row_ids // BLK_DEV
    within = row_ids % BLK_DEV
    left_reach = jax.random.randint(jax.random.fold_in(key, 1), (NBLK,), 1, REACH + 1)
    right_reach = jax.random.randint(jax.random.fold_in(key, 2), (NBLK,), 1, REACH + 1)
    left_pick = jax.random.randint(jax.random.fold_in(key, 3), (NBLK // BLK_DEV,), 0, BLK_DEV)
    right_pick = jax.random.randint(jax.random.fold_in(key, 4), (NBLK // BLK_DEV,), 0, BLK_DEV)
    left_reach = jnp.where(within == left_pick[tile_ids], REACH, left_reach)
    right_reach = jnp.where(within == right_pick[tile_ids], REACH, right_reach)
    left_cols = jnp.clip(row_ids - left_reach, 0, NBLK - 1)
    right_cols = jnp.clip(row_ids + right_reach, 0, NBLK - 1)
    return jnp.stack([left_cols, right_cols], axis=1).astype(jnp.int32)


def draw_weights(key, part):
    block_pos = jnp.arange(NBLK, dtype=jnp.float32) / max(NBLK - 1, 1)
    trend = jnp.exp(block_pos * math.log(3.0))[None, :]
    return jax.random.normal(jax.random.fold_in(key, 1), (MEMBERS, NBLK), jnp.float32) * trend


def level_of(own_key, dims, split, low, high):
    level, own = 1.0, jax.random.fold_in(own_key, 6)
    for dim, shards_of in split:
        steps = jnp.exp(jax.random.uniform(jax.random.fold_in(own, dim), (shards_of,), jnp.float32, low / len(split), high / len(split)))
        level = level * jnp.repeat(steps, dims[dim] // shards_of).reshape([-1 if axis == dim else 1 for axis in range(len(dims))])
    return level


def normal_values(own_key, extent, scale, limit, split=(), kind=jnp.bfloat16):
    array = jax.random.normal(own_key, extent, jnp.float32) * scale
    if len(split) > 0:
        array = level_of(own_key, extent, split, -0.22, 0.18) * array
    return jnp.clip(array, min=-limit, max=limit).astype(kind)


def setup_inputs(seed: int = 0) -> dict:
    keys = jax.random.split(jax.random.key(seed), 7)
    return {
        "ensemble": normal_values(keys[0], (MEMBERS, NROWS), 1.0, 6.0, ((0, 4), (1, 8))),
        "op_blocks": normal_values(keys[1], (NBLK, NNZ, BS, BS), (NNZ * BS) ** -0.5, 0.3125, ((0, 8),)),
        "col_index": draw_col_index(jax.random.fold_in(keys[6], 71), 0),
        "weights": draw_weights(jax.random.fold_in(keys[6], 71), 0),
        "innovations": normal_values(keys[4], (2, NROWS), 1.0, 6.0, ((1, 8),), jnp.float32),
        "obs_precision": jnp.clip(jnp.exp(math.log(4.0) - 2.7725887 * jax.random.uniform(keys[5], (2, NROWS), jnp.float32) ** level_of(keys[5], (2, NROWS), ((1, 8),), -0.2, 0.2)), 0.25, 4.0),
    }


def full_columns(col_index):
    row_ids = jnp.arange(NBLK, dtype=jnp.int32)[:, None]
    return jnp.concatenate([row_ids, col_index.astype(jnp.int32)], axis=1)

def apply_forward(op_blocks, columns, values_in):
    groups = NBLK // BLK_DEV
    grouped_ops = op_blocks.reshape(groups, BLK_DEV, NNZ, BS, BS)
    grouped_cols = columns.reshape(groups, BLK_DEV, NNZ)

    def apply_group(group_items):
        blocks, col_ids = group_items
        picked = values_in[:, col_ids, :]
        return jnp.einsum('rkij,mrkj->mri', blocks.astype(jnp.float32), picked.astype(jnp.float32))
    results = lax.map(apply_group, (grouped_ops, grouped_cols))
    return jnp.transpose(results, (1, 0, 2, 3)).reshape(MEMBERS, NBLK, BS)

def apply_adjoint(op_blocks, columns, cotangent):
    groups = NBLK // BLK_DEV
    grouped_ops = op_blocks.reshape(groups, BLK_DEV, NNZ, BS, BS)
    grouped_cols = columns.reshape(groups, BLK_DEV, NNZ)
    grouped_cot = jnp.transpose(cotangent.reshape(MEMBERS, groups, BLK_DEV, BS), (1, 0, 2, 3))

    def accumulate(summed, group_items):
        blocks, col_ids, cot_group = group_items
        contributions = jnp.einsum('rkij,mri->mrkj', blocks.astype(jnp.float32), cot_group.astype(jnp.float32))
        summed = summed.at[:, col_ids.reshape(-1), :].add(contributions.reshape(MEMBERS, BLK_DEV * NNZ, BS))
        return (summed, None)
    start_sum = jnp.zeros((MEMBERS, NBLK, BS), jnp.float32)
    summed, unused = lax.scan(accumulate, start_sum, (grouped_ops, grouped_cols, grouped_cot))
    return summed

def reference(ensemble, op_blocks, col_index, weights, innovations, obs_precision):
    columns = full_columns(col_index)
    states = ensemble.reshape(MEMBERS, NBLK, BS)
    prop_one = apply_forward(op_blocks, columns, states).astype(jnp.bfloat16)
    prop_two = apply_forward(op_blocks, columns, prop_one).astype(jnp.bfloat16)
    member_scale = (MEMBERS - 1) ** (-0.5)
    weight_col = weights[:, :, None]
    increments = jnp.stack([lax.optimization_barrier(jnp.sum(weight_col * prop_one.astype(jnp.float32), axis=0)), lax.optimization_barrier(jnp.sum(weight_col * prop_two.astype(jnp.float32), axis=0))]) * member_scale
    observed = innovations.reshape(2, NBLK, BS)
    precision = obs_precision.reshape(2, NBLK, BS)
    residual = precision * (increments - observed)
    cot_one = (member_scale * weight_col * residual[0][None]).astype(jnp.bfloat16)
    cot_two = (member_scale * weight_col * residual[1][None]).astype(jnp.bfloat16)
    adjoint_mid = (cot_one.astype(jnp.float32) + apply_adjoint(op_blocks, columns, cot_two)).astype(jnp.bfloat16)
    grad_ens = apply_adjoint(op_blocks, columns, adjoint_mid).reshape(MEMBERS, NROWS)
    products = prop_one.astype(jnp.float32) * residual[0][None] + prop_two.astype(jnp.float32) * residual[1][None]
    grad_weights = weights + member_scale * lax.optimization_barrier(jnp.sum(products, axis=2))
    mean_square = lax.optimization_barrier(jnp.mean(grad_weights * grad_weights, axis=1, keepdims=True))
    direction = grad_weights / jnp.sqrt(mean_square + 1e-06)
    return (grad_ens, direction)
```

```python
import jax
import jax.numpy as jnp
from jax import lax
from jax.experimental import pallas as pl
from jax.experimental.pallas import tpu as pltpu
from jax.sharding import PartitionSpec as P

MEMBERS = 128
REACH = 32
SCALE = (MEMBERS - 1) ** (-0.5)
F32 = jnp.float32
BF16 = jnp.bfloat16
ROWS_T = (((1,), (1,)), ((), ()))
ROWS_N = (((1,), (0,)), ((), ()))


def dot_t(x, a):
    return lax.dot_general(x, a, ROWS_T, preferred_element_type=F32)


def dot_n(x, a):
    return lax.dot_general(x, a, ROWS_N, preferred_element_type=F32)


def is_even():
    return lax.axis_index("space") % 2 == 0


def base_row(rows):
    return lax.axis_index("space") * rows


def block(ref, start, size):
    return ref[:, pl.ds(pl.multiple_of(start * size, size), size)]


def chunks(total, unroll, body):
    unroll = min(unroll, total)

    def step(i, carry):
        body([i * unroll + u for u in range(unroll)])
        return carry

    lax.fori_loop(0, total // unroll, step, 0)


def inner_pairs(rows):
    return ((2, 0, rows - REACH), (1, REACH, rows - REACH))


def rim_pairs(rows):
    return ((1, 0, REACH), (2, rows - REACH, REACH))


def forward_inner(cols, v, ops, acc):
    rows, _, size, _ = ops.shape
    base = base_row(rows)
    for k, low, count in inner_pairs(rows):

        def some(ids, k=k, low=low):
            outs = []
            for i in ids:
                r = low + i
                c = cols[k - 1, r] - base
                x = jnp.concatenate([block(v, r, size), block(v, c, size)], 1)
                outs.append((r, dot_t(x, jnp.concatenate([ops[r, 0], ops[r, k]], 1))))
            for r, o in outs:
                acc[r] = o

        chunks(count, 16, some)


def fill_wide(wide, v, mate, off, halo):
    length = v.shape[1]
    even = is_even()
    wide[:, halo : halo + length] = v[...]

    @pl.when(even)
    def _():
        wide[:, :halo] = off[...]
        wide[:, halo + length :] = mate[...]

    @pl.when(jnp.logical_not(even))
    def _():
        wide[:, :halo] = mate[...]
        wide[:, halo + length :] = off[...]


def pick(first, last):
    even = is_even()
    return jnp.where(even, last, first), jnp.where(even, first, last)


def forward_rim(cols, acc, v, mate, off, ops, out, wide):
    rows, _, size, _ = ops.shape
    base = base_row(rows)
    fill_wide(wide, v, mate, off, REACH * size)
    for k, low, count in rim_pairs(rows):

        def some(ids, k=k, low=low):
            outs = []
            for i in ids:
                r = low + i
                c = cols[k - 1, r] - base + REACH
                outs.append((r, acc[r] + dot_t(block(wide, c, size), ops[r, k])))
            for r, o in outs:
                out[:, pl.ds(pl.multiple_of(r * size, size), size)] = o.astype(BF16)

        chunks(count, 16, some)


def first_rim(cols, acc, v, mate, off, ops, out, to_mate, to_off, wide):
    forward_rim(cols, acc, v, mate, off, ops, out, wide)
    halo = REACH * ops.shape[2]
    length = out.shape[1]
    even = is_even()

    @pl.when(even)
    def _():
        to_mate[...] = out[:, length - halo :]
        to_off[...] = out[:, :halo]

    @pl.when(jnp.logical_not(even))
    def _():
        to_mate[...] = out[:, :halo]
        to_off[...] = out[:, length - halo :]


def member_sum(v, w, rows, size, store):
    for r in range(rows):
        x = v[:, r * size : (r + 1) * size].astype(F32)
        store(r, jnp.sum(x * w[:, r : r + 1], axis=0, keepdims=True))


def second_inner(cols, v, ops, w, acc, inc):
    forward_inner(cols, v, ops, acc)

    def store(r, s):
        inc[r : r + 1, :] = s

    member_sum(v, w, ops.shape[0], ops.shape[2], store)


def second_rim(cols, acc, v, mate, off, ops, w, inc_one, out, inc, inc_send, wide):
    rows = ops.shape[0]
    forward_rim(cols, acc, v, mate, off, ops, out, wide)
    inc[:rows, :] = inc_one[...]

    def store(r, s):
        inc[rows + r : rows + r + 1, :] = s

    member_sum(out, w, rows, ops.shape[2], store)
    inc_send[...] = inc[...].astype(BF16)


def cot_row(res, r):
    return jnp.broadcast_to(res[pl.ds(r, 1), :], (8, res.shape[1])).astype(BF16)


def residual_rim(inc, innov, prec, ops, cols, w, *rest):
    received = rest[:-4]
    res, to_mate, to_off, rim = rest[-4:]
    rows, _, size, _ = ops.shape
    total = inc[...]
    for other in received:
        total = total + other[...].astype(F32)
    res[...] = prec[...] * (total * SCALE - innov[...])
    res_two = res.at[pl.ds(rows, rows), :]
    start = 0
    for k, low, count in rim_pairs(rows):

        def some(ids, k=k, low=low, start=start):
            outs = [(i, dot_n(cot_row(res_two, low + i), ops[low + i, k])) for i in ids]
            for i, o in outs:
                rim[pl.ds(start + i, 1), :] = o[:1]

        chunks(count, 16, some)
        start += count
    members = w.shape[0]
    first, last = rim[:REACH, :], rim[REACH:, :]
    mate, off = pick(first, last)
    to_mate[:REACH, :] = mate
    to_off[:REACH, :] = off
    mate, off = pick(w[:, :REACH], w[:, rows - REACH :])
    to_mate[REACH : REACH + members, :REACH] = mate
    to_off[REACH : REACH + members, :REACH] = off
    col = cols[...].astype(F32)
    mate, off = pick(col[:1, :REACH], col[1:, rows - REACH :])
    to_mate[REACH : REACH + 1, REACH : 2 * REACH] = mate
    to_off[REACH : REACH + 1, REACH : 2 * REACH] = off


def residual_inner(res, ops, w, one, two, y, gw, squares):
    rows, _, size, _ = ops.shape
    members = w.shape[0]
    res_two = res.at[pl.ds(rows, rows), :]
    start = 0
    for k, low, count in inner_pairs(rows):

        def some(ids, k=k, low=low, start=start):
            outs = []
            for i in ids:
                r = low + i
                o = dot_n(cot_row(res_two, r), jnp.concatenate([ops[r, 0], ops[r, k]], 1))
                outs.append((r, i, o))
            for r, i, o in outs:
                y[pl.ds(r, 1), :] = o[:1, :size] + res[pl.ds(r, 1), :]
                y[pl.ds(rows + start + i, 1), :] = o[:1, size:]

        chunks(count, 16, some)
        start += count
    lanes = lax.broadcasted_iota(jnp.int32, (members, rows), 1)
    grown = jnp.zeros((members, rows), F32)
    for r in range(rows):
        part = slice(r * size, (r + 1) * size)
        prod = one[:, part].astype(F32) * res[r : r + 1, :] + two[:, part].astype(F32) * res[rows + r : rows + r + 1, :]
        grown = jnp.where(lanes == r, jnp.sum(prod, axis=1, keepdims=True), grown)
    grown = w[...] + SCALE * grown
    gw[...] = grown
    squares[...] = jnp.broadcast_to(jnp.sum(grown * grown, axis=1, keepdims=True), squares.shape)


def adjoint_rim(col_s, col_v, w, y, rim, mate, off, ops, mid, own, to_mate, to_off, vals, wp, tgt, wide):
    rows, _, size, _ = ops.shape
    members = w.shape[0]
    base = base_row(rows)
    even = is_even()
    inner = rows - REACH
    vals[:rows, :] = y[:rows, :].astype(BF16)
    vals[rows : rows + REACH, :] = rim[:REACH, :].astype(BF16)
    vals[rows + REACH : 2 * rows, :] = y[rows + inner : rows + 2 * inner, :].astype(BF16)
    vals[2 * rows : 2 * rows + inner, :] = y[rows : rows + inner, :].astype(BF16)
    vals[2 * rows + inner : 3 * rows, :] = rim[REACH:, :].astype(BF16)
    left = jnp.where(even, off[...], mate[...])
    right = jnp.where(even, mate[...], off[...])
    vals[3 * rows : 3 * rows + REACH, :] = left[:REACH, :].astype(BF16)
    vals[3 * rows + REACH :, :] = right[:REACH, :].astype(BF16)
    for k in range(3):
        wp[:, k * rows : (k + 1) * rows] = w[...] * SCALE
    wp[:, 3 * rows : 3 * rows + REACH] = left[REACH : REACH + members, :REACH] * SCALE
    wp[:, 3 * rows + REACH :] = right[REACH : REACH + members, :REACH] * SCALE
    shift = base.astype(F32)
    tgt[:, :rows] = lax.broadcasted_iota(jnp.int32, (8, rows), 1).astype(F32)
    for k in (1, 2):
        tgt[:, k * rows : (k + 1) * rows] = jnp.broadcast_to(col_v[k - 1 : k, :].astype(F32) - shift, (8, rows))
    for start, side in ((3 * rows, left), (3 * rows + REACH, right)):
        tgt[:, start : start + REACH] = jnp.broadcast_to(
            side[REACH : REACH + 1, REACH : 2 * REACH] - shift, (8, REACH)
        )
    weights = wp[...]
    target = tgt[:1, :]
    group = 8
    for g in range(rows // group):
        picked = [jnp.where(target == F32(g * group + c), weights, 0.0).astype(BF16) for c in range(group)]
        part = dot_n(jnp.concatenate(picked, 0), vals[...]).astype(BF16)
        mid[g * group * members : (g + 1) * group * members, :] = part
    wide[...] = jnp.zeros_like(wide)
    for k, low, count in rim_pairs(rows):

        def some(ids, k=k, low=low):
            outs = []
            for i in ids:
                r = low + i
                x = mid[pl.ds(pl.multiple_of(r * members, members), members), :]
                outs.append((col_s[k - 1, r] - base + REACH, dot_n(x, ops[r, k])))
            for c, o in outs:
                wide[c] = wide[c] + o

        chunks(count, 16, some)
    own[...] = wide[REACH : REACH + rows]

    @pl.when(even)
    def _():
        to_mate[...] = wide[REACH + rows :].astype(BF16)
        to_off[...] = wide[:REACH].astype(BF16)

    @pl.when(jnp.logical_not(even))
    def _():
        to_mate[...] = wide[:REACH].astype(BF16)
        to_off[...] = wide[REACH + rows :].astype(BF16)


def adjoint_inner(cols, mid, own, ops, out):
    rows, _, size, _ = ops.shape
    members = own.shape[1]
    base = base_row(rows)
    out[...] = own[...]
    for k, low, count in inner_pairs(rows):

        def some(ids, k=k, low=low):
            outs = []
            for i in ids:
                r = low + i
                x = mid[pl.ds(pl.multiple_of(r * members, members), members), :]
                o = dot_n(x, jnp.concatenate([ops[r, 0], ops[r, k]], 1))
                outs.append((r, o[:, :size]))
                outs.append((cols[k - 1, r] - base, o[:, size:]))
            for c, o in outs:
                out[c] = out[c] + o

        chunks(count, 16, some)


def finish(own, mate, off, out):
    rows, members, size = own.shape
    even = is_even()
    left = jnp.where(even, off[...], mate[...])
    right = jnp.where(even, mate[...], off[...])
    for c in range(rows):
        value = own[c]
        if c < REACH:
            value = value + left[c].astype(F32)
        if c >= rows - REACH:
            value = value + right[c - rows + REACH].astype(F32)
        out[:, c * size : (c + 1) * size] = value


SMEM = pl.BlockSpec(memory_space=pltpu.SMEM)
VMEM = pl.BlockSpec(memory_space=pltpu.VMEM)


def run(body, outs, args, scalars=0, scratch=()):
    return pl.pallas_call(
        body,
        out_shape=[jax.ShapeDtypeStruct(shape, kind) for shape, kind in outs],
        in_specs=[SMEM] * scalars + [VMEM] * (len(args) - scalars),
        out_specs=[VMEM] * len(outs),
        scratch_shapes=list(scratch),
        compiler_params=pltpu.CompilerParams(vmem_limit_bytes=40 * 1024 * 1024),
        name=body.__name__,
    )(*args)


def on_device(ensemble, op_blocks, col_index, weights, innovations, obs_precision):
    members = ensemble.shape[0]
    rows, _, size, _ = op_blocks.shape
    halo = REACH * size
    length = rows * size
    tiles = lax.axis_size("space")
    groups = lax.axis_size("members")
    mates = [(i, i ^ 1) for i in range(tiles)]
    offs = []
    for i in range(1, tiles - 1, 2):
        offs += [(i, i + 1), (i + 1, i)]

    def swap(to_mate, to_off):
        from_off = lax.ppermute(to_off, "space", offs)
        from_mate = lax.ppermute(to_mate, "space", mates)
        return from_mate, from_off

    even = is_even()
    cols = col_index.T
    wide = pltpu.VMEM((members, length + 2 * halo), BF16)
    acc_kind = ((rows, members, size), F32)
    flat_kind = ((members, length), BF16)
    rim_kind = ((members, halo), BF16)

    to_mate = lax.dynamic_slice_in_dim(ensemble, jnp.where(even, length - halo, 0), halo, 1)
    to_off = lax.dynamic_slice_in_dim(ensemble, jnp.where(even, 0, length - halo), halo, 1)
    mate, off = swap(to_mate, to_off)
    (acc,) = run(forward_inner, [acc_kind], (cols, ensemble, op_blocks), 1)
    one, to_mate, to_off = run(
        first_rim, [flat_kind, rim_kind, rim_kind], (cols, acc, ensemble, mate, off, op_blocks), 1, [wide]
    )
    mate, off = swap(to_mate, to_off)
    acc, inc_one = run(second_inner, [acc_kind, ((rows, size), F32)], (cols, one, op_blocks, weights), 1)
    two, inc, inc_send = run(
        second_rim,
        [flat_kind, ((2 * rows, size), F32), ((2 * rows, size), BF16)],
        (cols, acc, one, mate, off, op_blocks, weights, inc_one),
        1,
        [wide],
    )
    received = [
        lax.ppermute(inc_send, "members", [(i, (i + step) % groups) for i in range(groups)])
        for step in range(1, groups)
    ]
    pay_kind = ((REACH + members, size), F32)
    res, to_mate, to_off, rim = run(
        residual_rim,
        [((2 * rows, size), F32), pay_kind, pay_kind, ((2 * REACH, size), F32)],
        (
            inc,
            innovations.reshape(2 * rows, size),
            obs_precision.reshape(2 * rows, size),
            op_blocks,
            cols,
            weights,
            *received,
        ),
    )
    mate, off = swap(to_mate, to_off)
    y, grad_weights, squares = run(
        residual_inner,
        [((3 * rows - 2 * REACH, size), F32), ((members, rows), F32), ((members, size), F32)],
        (res, op_blocks, weights, one, two),
    )
    pairs = 3 * rows + 2 * REACH
    swap_kind = ((REACH, members, size), BF16)
    mid, own, to_mate, to_off = run(
        adjoint_rim,
        [((rows * members, size), BF16), acc_kind, swap_kind, swap_kind],
        (cols, cols, weights, y, rim, mate, off, op_blocks),
        1,
        [
            pltpu.VMEM((pairs, size), BF16),
            pltpu.VMEM((members, pairs), F32),
            pltpu.VMEM((8, pairs), F32),
            pltpu.VMEM((rows + 2 * REACH, members, size), F32),
        ],
    )
    mate, off = swap(to_mate, to_off)
    (own,) = run(adjoint_inner, [acc_kind], (cols, mid, own, op_blocks), 1)
    squares = lax.psum(squares[:, 0], "space")
    mean_square = squares / (rows * tiles)
    direction = grad_weights / jnp.sqrt(mean_square + 1e-06)[:, None]
    (grad_ens,) = run(finish, [((members, length), F32)], (own, mate, off))
    return (grad_ens, direction)


def solution(mesh):
    placed = (
        P("members", "space"),
        P("space", None, None, None),
        P("space", None),
        P("members", "space"),
        P(None, "space"),
        P(None, "space"),
    )
    return jax.shard_map(
        on_device,
        mesh=mesh,
        in_specs=placed,
        out_specs=(P("members", "space"), P("members", "space")),
        check_vma=False,
    )
```

```python
import jax
import jax.numpy as jnp
from jax import lax
from jax.experimental import pallas as pl
from jax.experimental.pallas import tpu as pltpu
from jax.sharding import PartitionSpec as P

MEMBERS = 128
REACH = 32
SCALE = (MEMBERS - 1) ** (-0.5)
F32 = jnp.float32
BF16 = jnp.bfloat16
ROWS_T = (((1,), (1,)), ((), ()))
ROWS_N = (((1,), (0,)), ((), ()))


def dot_t(x, a):
    return lax.dot_general(x, a, ROWS_T, preferred_element_type=F32)


def dot_n(x, a):
    return lax.dot_general(x, a, ROWS_N, preferred_element_type=F32)


def is_even():
    return lax.axis_index("space") % 2 == 0


def base_row(rows):
    return lax.axis_index("space") * rows


def block(ref, start, size):
    return ref[:, pl.ds(pl.multiple_of(start * size, size), size)]


def chunks(total, unroll, body):
    unroll = min(unroll, total)

    def step(i, carry):
        body([i * unroll + u for u in range(unroll)])
        return carry

    lax.fori_loop(0, total // unroll, step, 0)


def inner_pairs(rows):
    return ((2, 0, rows - REACH), (1, REACH, rows - REACH))


def split_pairs(pairs, ready):
    if ready is None:
        return pairs
    halves = []
    for k, low, count in pairs:
        halves += [(k, low, count // 2), (k, low + count // 2, count // 2)]
    return halves


def rim_pairs(rows):
    return ((1, 0, REACH), (2, rows - REACH, REACH))


def first_inner(cols, v_far, ops_far, acc, v, ops, v_sem, sems):
    rows = ops.shape[0]
    parts = sems.shape[0]
    step = rows // parts
    v_copy = pltpu.make_async_copy(v_far, v, v_sem)
    v_copy.start()
    copies = []
    for part in range(parts):
        where = pl.ds(part * step, step)
        copies.append(pltpu.make_async_copy(ops_far.at[where], ops.at[where], sems.at[part]))
        copies[-1].start()
    v_copy.wait()

    def ready(low, count):
        for part in range(low // step, (low + count) // step):
            copies[part].wait()

    forward_inner(cols, v, ops, acc, ready)


def forward_inner(cols, v, ops, acc, ready=None):
    rows, _, size, _ = ops.shape
    base = base_row(rows)
    for k, low, count in split_pairs(inner_pairs(rows), ready):
        if ready is not None:
            ready(low, count)

        def some(ids, k=k, low=low):
            outs = []
            for i in ids:
                r = low + i
                c = cols[k - 1, r] - base
                x = jnp.concatenate([block(v, r, size), block(v, c, size)], 1)
                outs.append((r, dot_t(x, jnp.concatenate([ops[r, 0], ops[r, k]], 1))))
            for r, o in outs:
                acc[r] = o

        chunks(count, 16, some)


def fill_wide(wide, v, mate, off, halo):
    length = v.shape[1]
    even = is_even()
    wide[:, halo : halo + length] = v[...]

    @pl.when(even)
    def _():
        wide[:, :halo] = off[...]
        wide[:, halo + length :] = mate[...]

    @pl.when(jnp.logical_not(even))
    def _():
        wide[:, :halo] = mate[...]
        wide[:, halo + length :] = off[...]


def pick(first, last):
    even = is_even()
    return jnp.where(even, last, first), jnp.where(even, first, last)


def forward_rim(cols, acc, v, mate, off, ops, out, wide):
    rows, _, size, _ = ops.shape
    base = base_row(rows)
    fill_wide(wide, v, mate, off, REACH * size)
    for k, low, count in rim_pairs(rows):

        def some(ids, k=k, low=low):
            outs = []
            for i in ids:
                r = low + i
                c = cols[k - 1, r] - base + REACH
                outs.append((r, acc[r] + dot_t(block(wide, c, size), ops[r, k])))
            for r, o in outs:
                out[:, pl.ds(pl.multiple_of(r * size, size), size)] = o.astype(BF16)

        chunks(count, 16, some)


def first_rim(cols, acc, v, mate, off, ops, out, to_mate, to_off, wide):
    forward_rim(cols, acc, v, mate, off, ops, out, wide)
    halo = REACH * ops.shape[2]
    length = out.shape[1]
    even = is_even()

    @pl.when(even)
    def _():
        to_mate[...] = out[:, length - halo :]
        to_off[...] = out[:, :halo]

    @pl.when(jnp.logical_not(even))
    def _():
        to_mate[...] = out[:, :halo]
        to_off[...] = out[:, length - halo :]


def member_sum(v, w, rows, size, store):
    for r in range(rows):
        x = v[:, r * size : (r + 1) * size].astype(F32)
        store(r, jnp.sum(x * w[:, r : r + 1], axis=0, keepdims=True))


def second_inner(cols, v, ops, w, innov, prec, acc, inc, innov_rows, prec_rows):
    forward_inner(cols, v, ops, acc)
    rows, _, size, _ = ops.shape
    for time in range(2):
        for r in range(rows):
            place = slice(time * rows + r, time * rows + r + 1)
            part = slice(r * size, (r + 1) * size)
            innov_rows[place, :] = innov[time : time + 1, part]
            prec_rows[place, :] = prec[time : time + 1, part]

    def store(r, s):
        inc[r : r + 1, :] = s

    member_sum(v, w, ops.shape[0], ops.shape[2], store)


def second_rim(cols, acc, v, mate, off, ops, w, inc_one, out, inc, inc_send, wide):
    rows = ops.shape[0]
    forward_rim(cols, acc, v, mate, off, ops, out, wide)
    inc[:rows, :] = inc_one[...]

    def store(r, s):
        inc[rows + r : rows + r + 1, :] = s

    member_sum(out, w, rows, ops.shape[2], store)
    inc_send[...] = inc[...].astype(BF16)


def cot_row(res, r):
    return jnp.broadcast_to(res[pl.ds(r, 1), :], (8, res.shape[1])).astype(BF16)


def weight_gradient(res, w, one, two):
    members, rows = w.shape
    size = res.shape[1]
    lanes = lax.broadcasted_iota(jnp.int32, (members, rows), 1)
    grown = jnp.zeros((members, rows), F32)
    for r in range(rows):
        part = slice(r * size, (r + 1) * size)
        prod = one[:, part].astype(F32) * res[r : r + 1, :] + two[:, part].astype(F32) * res[rows + r : rows + r + 1, :]
        grown = jnp.where(lanes == r, jnp.sum(prod, axis=1, keepdims=True), grown)
    grown = w[...] + SCALE * grown
    return grown, jnp.broadcast_to(jnp.sum(grown * grown, axis=1, keepdims=True), (members, size))


def residual_rim(inc, innov, prec, ops, cols, w, one, two, *rest):
    received = rest[:-5]
    res, to_mate, to_off, rim, gw = rest[-5:]
    rows, _, size, _ = ops.shape
    total = inc[...]
    for other in received:
        total = total + other[...].astype(F32)
    res[...] = prec[...] * (total * SCALE - innov[...])
    res_two = res.at[pl.ds(rows, rows), :]
    start = 0
    for k, low, count in rim_pairs(rows):

        def some(ids, k=k, low=low, start=start):
            outs = [(i, dot_n(cot_row(res_two, low + i), ops[low + i, k])) for i in ids]
            for i, o in outs:
                rim[pl.ds(start + i, 1), :] = o[:1]

        chunks(count, 16, some)
        start += count
    members = w.shape[0]
    gw[...], squares = weight_gradient(res, w, one, two)
    to_mate[REACH + members :, :] = squares
    first, last = rim[:REACH, :], rim[REACH:, :]
    mate, off = pick(first, last)
    to_mate[:REACH, :] = mate
    to_off[:REACH, :] = off
    mate, off = pick(w[:, :REACH], w[:, rows - REACH :])
    to_mate[REACH : REACH + members, :REACH] = mate
    to_off[REACH : REACH + members, :REACH] = off
    col = cols[...].astype(F32)
    mate, off = pick(col[:1, :REACH], col[1:, rows - REACH :])
    to_mate[REACH : REACH + 1, REACH : 2 * REACH] = mate
    to_off[REACH : REACH + 1, REACH : 2 * REACH] = off


def residual_inner(res, ops, y):
    rows, _, size, _ = ops.shape
    res_two = res.at[pl.ds(rows, rows), :]
    start = 0
    for k, low, count in inner_pairs(rows):

        def some(ids, k=k, low=low, start=start):
            outs = []
            for i in ids:
                r = low + i
                o = dot_n(cot_row(res_two, r), jnp.concatenate([ops[r, 0], ops[r, k]], 1))
                outs.append((r, i, o))
            for r, i, o in outs:
                y[pl.ds(r, 1), :] = o[:1, :size] + res[pl.ds(r, 1), :]
                y[pl.ds(rows + start + i, 1), :] = o[:1, size:]

        chunks(count, 16, some)
        start += count


def adjoint_rim(col_s, col_v, w, y, rim, mate, off, ops, mid, own, to_mate, to_off, vals, wp, tgt, wide):
    rows, _, size, _ = ops.shape
    members = w.shape[0]
    base = base_row(rows)
    even = is_even()
    inner = rows - REACH
    vals[:rows, :] = y[:rows, :].astype(BF16)
    vals[rows : rows + REACH, :] = rim[:REACH, :].astype(BF16)
    vals[rows + REACH : 2 * rows, :] = y[rows + inner : rows + 2 * inner, :].astype(BF16)
    vals[2 * rows : 2 * rows + inner, :] = y[rows : rows + inner, :].astype(BF16)
    vals[2 * rows + inner : 3 * rows, :] = rim[REACH:, :].astype(BF16)
    near, across = mate[: REACH + members, :], off[...]
    left = jnp.where(even, across, near)
    right = jnp.where(even, near, across)
    vals[3 * rows : 3 * rows + REACH, :] = left[:REACH, :].astype(BF16)
    vals[3 * rows + REACH :, :] = right[:REACH, :].astype(BF16)
    for k in range(3):
        wp[:, k * rows : (k + 1) * rows] = w[...] * SCALE
    wp[:, 3 * rows : 3 * rows + REACH] = left[REACH : REACH + members, :REACH] * SCALE
    wp[:, 3 * rows + REACH :] = right[REACH : REACH + members, :REACH] * SCALE
    shift = base.astype(F32)
    tgt[:, :rows] = lax.broadcasted_iota(jnp.int32, (8, rows), 1).astype(F32)
    for k in (1, 2):
        tgt[:, k * rows : (k + 1) * rows] = jnp.broadcast_to(col_v[k - 1 : k, :].astype(F32) - shift, (8, rows))
    for start, side in ((3 * rows, left), (3 * rows + REACH, right)):
        tgt[:, start : start + REACH] = jnp.broadcast_to(
            side[REACH : REACH + 1, REACH : 2 * REACH] - shift, (8, REACH)
        )
    weights = wp[...]
    target = tgt[:1, :]
    group = 8
    for g in range(rows // group):
        picked = [jnp.where(target == F32(g * group + c), weights, 0.0).astype(BF16) for c in range(group)]
        part = dot_n(jnp.concatenate(picked, 0), vals[...]).astype(BF16)
        mid[g * group * members : (g + 1) * group * members, :] = part
    wide[...] = jnp.zeros_like(wide)
    for k, low, count in rim_pairs(rows):

        def some(ids, k=k, low=low):
            outs = []
            for i in ids:
                r = low + i
                x = mid[pl.ds(pl.multiple_of(r * members, members), members), :]
                outs.append((col_s[k - 1, r] - base + REACH, dot_n(x, ops[r, k])))
            for c, o in outs:
                wide[c] = wide[c] + o

        chunks(count, 16, some)
    own[...] = wide[REACH : REACH + rows]

    @pl.when(even)
    def _():
        to_mate[...] = wide[REACH + rows :].astype(BF16)
        to_off[...] = wide[:REACH].astype(BF16)

    @pl.when(jnp.logical_not(even))
    def _():
        to_mate[...] = wide[:REACH].astype(BF16)
        to_off[...] = wide[REACH + rows :].astype(BF16)


def adjoint_inner(cols, mid, own, ops, out):
    rows, _, size, _ = ops.shape
    members = own.shape[1]
    base = base_row(rows)
    out[...] = own[...]
    for k, low, count in inner_pairs(rows):

        def some(ids, k=k, low=low):
            outs = []
            for i in ids:
                r = low + i
                x = mid[pl.ds(pl.multiple_of(r * members, members), members), :]
                o = dot_n(x, jnp.concatenate([ops[r, 0], ops[r, k]], 1))
                outs.append((r, o[:, :size]))
                outs.append((cols[k - 1, r] - base, o[:, size:]))
            for c, o in outs:
                out[c] = out[c] + o

        chunks(count, 16, some)


def finish(count, own, mate, off, gw, total, out, direction):
    rows, members, size = own.shape
    direction[...] = gw[...] / jnp.sqrt(total[:, :1] / count[0] + 1e-06)
    even = is_even()
    left = jnp.where(even, off[...], mate[...])
    right = jnp.where(even, mate[...], off[...])
    for c in range(rows):
        value = own[c]
        if c < REACH:
            value = value + left[c].astype(F32)
        if c >= rows - REACH:
            value = value + right[c - rows + REACH].astype(F32)
        out[:, c * size : (c + 1) * size] = value


SMEM = pl.BlockSpec(memory_space=pltpu.SMEM)
VMEM = pl.BlockSpec(memory_space=pltpu.VMEM)
FAR = pl.BlockSpec(memory_space=pltpu.HBM)


def run(body, outs, args, scalars=0, scratch=(), far=0, near=True):
    kind_of = pltpu.VMEM if near else jax.ShapeDtypeStruct
    return pl.pallas_call(
        body,
        out_shape=[kind_of(shape, kind) for shape, kind in outs],
        in_specs=[SMEM] * scalars + [VMEM] * (len(args) - scalars - far) + [FAR] * far,
        out_specs=[VMEM] * len(outs),
        scratch_shapes=list(scratch),
        compiler_params=pltpu.CompilerParams(vmem_limit_bytes=12 * 1024 * 1024),
        name=body.__name__,
    )(*args)


def on_device(ensemble, op_blocks, col_index, weights, innovations, obs_precision):
    members = ensemble.shape[0]
    rows, _, size, _ = op_blocks.shape
    halo = REACH * size
    length = rows * size
    tiles = lax.axis_size("space")
    groups = lax.axis_size("members")
    mates = [(i, i ^ 1) for i in range(tiles)]
    offs = []
    for i in range(1, tiles - 1, 2):
        offs += [(i, i + 1), (i + 1, i)]

    def swap(to_mate, to_off):
        from_off = lax.ppermute(to_off, "space", offs)
        from_mate = lax.ppermute(to_mate, "space", mates)
        return from_mate, from_off

    even = is_even()
    far = lambda value: pltpu.with_memory_space_constraint(value, pltpu.HBM)
    cols = col_index.T
    wide = pltpu.VMEM((members, length + 2 * halo), BF16)
    acc_kind = ((rows, members, size), F32)
    flat_kind = ((members, length), BF16)
    rim_kind = ((members, halo), BF16)

    to_mate = lax.dynamic_slice_in_dim(ensemble, jnp.where(even, length - halo, 0), halo, 1)
    to_off = lax.dynamic_slice_in_dim(ensemble, jnp.where(even, 0, length - halo), halo, 1)
    mate, off = swap(to_mate, to_off)
    acc, ens, ops = run(
        first_inner,
        [acc_kind, flat_kind, (op_blocks.shape, BF16)],
        (cols, far(ensemble), far(op_blocks)),
        1,
        [pltpu.SemaphoreType.DMA(()), pltpu.SemaphoreType.DMA((4,))],
        far=2,
    )
    one, to_mate, to_off = run(
        first_rim, [flat_kind, rim_kind, rim_kind], (cols, acc, ens, mate, off, ops), 1, [wide]
    )
    mate, off = swap(to_mate, to_off)
    row_kind = ((2 * rows, size), F32)
    acc, inc_one, innov, prec = run(
        second_inner,
        [acc_kind, ((rows, size), F32), row_kind, row_kind],
        (cols, one, ops, weights, innovations, obs_precision),
        1,
    )
    two, inc, inc_send = run(
        second_rim,
        [flat_kind, ((2 * rows, size), F32), ((2 * rows, size), BF16)],
        (cols, acc, one, mate, off, ops, weights, inc_one),
        1,
        [wide],
    )
    received = [
        lax.ppermute(inc_send, "members", [(i, i ^ step) for i in range(groups)])
        for step in range(1, groups)
    ]
    pay_kind = ((REACH + members, size), F32)
    mate_kind = ((REACH + 2 * members, size), F32)
    res, to_mate, to_off, rim, grad_weights = run(
        residual_rim,
        [((2 * rows, size), F32), mate_kind, pay_kind, ((2 * REACH, size), F32), ((members, rows), F32)],
        (
            inc,
            innov,
            prec,
            ops,
            cols,
            weights,
            one,
            two,
            *received,
        ),
    )
    own_squares = to_mate[REACH + members :]
    mate, off = swap(to_mate, to_off)
    (y,) = run(residual_inner, [((3 * rows - 2 * REACH, size), F32)], (res, ops))
    total = own_squares + mate[REACH + members :]
    strides = [2**power for power in range(1, tiles.bit_length() - 1)]

    def partner(value, stride):
        return lax.ppermute(value, "space", [(i, i ^ stride) for i in range(tiles)])

    total = total + partner(total, strides[0])
    pairs = 3 * rows + 2 * REACH
    swap_kind = ((REACH, members, size), BF16)
    mid, own, to_mate, to_off = run(
        adjoint_rim,
        [((rows * members, size), BF16), acc_kind, swap_kind, swap_kind],
        (cols, cols, weights, y, rim, mate, off, ops),
        1,
        [
            pltpu.VMEM((pairs, size), BF16),
            pltpu.VMEM((members, pairs), F32),
            pltpu.VMEM((8, pairs), F32),
            pltpu.VMEM((rows + 2 * REACH, members, size), F32),
        ],
    )
    to_mate, to_off, total = lax.optimization_barrier((to_mate, to_off, total))
    mate, off = swap(to_mate, to_off)
    for stride in strides[1:]:
        total = total + partner(total, stride)
    (own,) = run(adjoint_inner, [acc_kind], (cols, mid, own, ops), 1)
    grad_ens, direction = run(
        finish,
        [((members, length), F32), ((members, rows), F32)],
        (jnp.full((1,), rows * tiles, F32), own, mate, off, grad_weights, total),
        1,
        near=False,
    )
    return (grad_ens, direction)


def solution(mesh):
    placed = (
        P("members", "space"),
        P("space", None, None, None),
        P("space", None),
        P("members", "space"),
        P(None, "space"),
        P(None, "space"),
    )
    return jax.shard_map(
        on_device,
        mesh=mesh,
        in_specs=placed,
        out_specs=(P("members", "space"), P("members", "space")),
        check_vma=False,
    )
```

```python
import jax
import jax.numpy as jnp
from jax import lax
from jax.experimental import pallas as pl
from jax.experimental.pallas import tpu as pltpu
from jax.sharding import PartitionSpec as P

MEMBERS = 128
REACH = 32
SCALE = (MEMBERS - 1) ** (-0.5)
F32 = jnp.float32
BF16 = jnp.bfloat16
I32 = jnp.int32
UNROLL = 16


def dot_t(x, a):
    return lax.dot_general(x, a, (((1,), (1,)), ((), ())), preferred_element_type=F32)


def dot_n(x, a):
    return lax.dot_general(x, a, (((1,), (0,)), ((), ())), preferred_element_type=F32)


class Sides:
    def __init__(self, rows):
        place = lax.axis_index("space")
        self.even = place % 2 == 0
        self.base = place * rows
        self.flip = jnp.where(self.even, 0, 3 * REACH)
        self.off_row = jnp.where(self.even, 0, REACH)
        self.mate_row = REACH - self.off_row
        self.off_k = jnp.where(self.even, 1, 2)
        self.mate_k = 3 - self.off_k

    def place(self, col):
        return (col - self.base + REACH) ^ self.flip

    def pick(self, first, last):
        return jnp.where(self.even, first, last), jnp.where(self.even, last, first)


def lanes(ref, index, size):
    return ref.at[:, pl.ds(pl.multiple_of(index * size, size), size)]


def chunks(total, body):
    def step(i, carry):
        body([i * UNROLL + u for u in range(UNROLL)])
        return carry

    lax.fori_loop(0, total // UNROLL, step, 0)


def load(ens, off, mate, sems):
    size = ens.shape[1] // (2 * REACH)
    sides = Sides(2 * REACH)
    width = REACH * size
    copies = []
    for n, (row, out) in enumerate(((sides.off_row, off), (sides.mate_row, mate))):
        source = ens.at[:, pl.ds(pl.multiple_of(row * size, size), width)]
        copies.append(pltpu.make_async_copy(source, out, sems.at[n]))
        copies[-1].start()
    for copy in copies:
        copy.wait()


def inner(cols, wide, ops, acc, sides, ready=None):
    size = ops.shape[2]
    for row, k, q in ((sides.off_row, sides.mate_k, 0), (sides.mate_row, sides.off_k, REACH)):
        for half in range(2):
            low = half * REACH // 2
            if ready is not None:
                ready((q + low) // (REACH // 2))

            def some(ids, row=row, k=k, q=q, low=low):
                outs = []
                for i in ids:
                    r = row + low + i
                    e = sides.place(cols[k - 1, r])
                    x = [lanes(wide, REACH + q + low + i, size)[...], lanes(wide, e, size)[...]]
                    outs.append((q + low + i, dot_t(jnp.concatenate(x, 1), jnp.concatenate([ops[r, 0], ops[r, k]], 1))))
                for place, o in outs:
                    acc[place] = o

            chunks(REACH // 2, some)


def first_inner(cols, off, mate, ops_far, acc, wide, ops, sems):
    rows, _, size, _ = ops.shape
    sides = Sides(rows)
    step = REACH // 2
    copies = []
    for part in range(2 * REACH // step):
        start = (sides.off_row if part * step < REACH else sides.mate_row) + part * step % REACH
        where = pl.ds(start, step)
        copies.append(pltpu.make_async_copy(ops_far.at[where], ops.at[where], sems.at[part]))
        copies[-1].start()
    wide[:, REACH * size : 2 * REACH * size] = off[...]
    wide[:, 2 * REACH * size : 3 * REACH * size] = mate[...]
    inner(cols, wide, ops, acc, sides, lambda part: copies[part].wait())


def rim(cols, acc, wide, ops, sides, near, store):
    size = ops.shape[2]
    row, k, q = (sides.mate_row, sides.mate_k, REACH) if near else (sides.off_row, sides.off_k, 0)

    def some(ids):
        outs = []
        for i in ids:
            e = sides.place(cols[k - 1, row + i])
            outs.append((i, acc[q + i] + dot_t(lanes(wide, e, size)[...], ops[row + i, k])))
        for i, o in outs:
            store(i, o.astype(BF16))

    chunks(REACH, some)


def first_mate(cols, acc, wide_in, halo, ops, wide, out, send):
    size = ops.shape[2]
    wide[:, 3 * REACH * size :] = halo[...]

    def store(i, o):
        lanes(out, 2 * REACH + i, size)[...] = o
        lanes(send, i, size)[...] = o

    rim(cols, acc, wide, ops, Sides(ops.shape[0]), True, store)


def first_off(cols, acc, wide_in, out_in, halo, ops, wide, out, send):
    size = ops.shape[2]
    wide[:, : REACH * size] = halo[...]

    def store(i, o):
        lanes(out, REACH + i, size)[...] = o
        lanes(send, i, size)[...] = o

    rim(cols, acc, wide, ops, Sides(ops.shape[0]), False, store)


def turned(sides, w):
    swapped = jnp.concatenate([w[:, REACH:], w[:, :REACH]], 1)
    return jnp.where(sides.even, w, swapped)


def member_sums(value, start, w, first, count, size, store):
    for i in range(count):
        x = value[:, (start + i) * size : (start + i + 1) * size].astype(F32)
        store(i, jnp.sum(x * w[:, first + i : first + i + 1], axis=0, keepdims=True))


def second_inner(cols, wide, ops, w, innov, prec, acc, inc, innov_rows, prec_rows, w_turned):
    rows, _, size, _ = ops.shape
    sides = Sides(rows)
    inner(cols, wide, ops, acc, sides)
    weights = turned(sides, w[...])
    w_turned[...] = weights
    for q in range(rows):
        r = q + (sides.off_row if q < REACH else sides.mate_row - REACH)
        for time in range(2):
            place = slice(time * rows + q, time * rows + q + 1)
            innov_rows[place, :] = lanes(innov, r, size)[time : time + 1, :]
            prec_rows[place, :] = lanes(prec, r, size)[time : time + 1, :]

    def store(i, s):
        inc[i : i + 1, :] = s

    member_sums(wide, REACH, weights, 0, rows, size, store)


def second_mate(cols, acc, wide_in, halo, ops, w, wide, out, inc):
    size = ops.shape[2]
    wide[:, 3 * REACH * size :] = halo[...]

    def store(i, o):
        lanes(out, i, size)[...] = o

    rim(cols, acc, wide, ops, Sides(ops.shape[0]), True, store)

    def keep(i, s):
        inc[i : i + 1, :] = s

    member_sums(out, 0, w, REACH, REACH, size, keep)


def second_off(cols, acc, wide_in, halo, ops, w, inc_one, inc_mate, wide, out, inc, send):
    rows, _, size, _ = ops.shape
    wide[:, : REACH * size] = halo[...]

    def store(i, o):
        lanes(out, i, size)[...] = o

    rim(cols, acc, wide, ops, Sides(rows), False, store)

    def keep(i, s):
        inc[rows + i : rows + i + 1, :] = s

    member_sums(out, 0, w, 0, REACH, size, keep)
    inc[:rows, :] = inc_one[...]
    inc[rows + REACH :, :] = inc_mate[...]
    send[...] = inc[...].astype(BF16)


def cot_row(res, place):
    return jnp.broadcast_to(res[pl.ds(place, 1), :], (8, res.shape[1])).astype(BF16)


def rim_rows(res, ops, sides, near, out):
    rows = ops.shape[0]
    row, k, q = (sides.mate_row, sides.mate_k, REACH) if near else (sides.off_row, sides.off_k, 0)

    def some(ids):
        outs = [(i, dot_n(cot_row(res, rows + q + i), ops[row + i, k])) for i in ids]
        for i, o in outs:
            out[pl.ds(i, 1), :] = o[:1]

    chunks(REACH, some)


def side_facts(cols, w, sides, near, out):
    members = w.shape[0]
    first, last = (REACH, 2 * REACH) if near else (0, REACH)
    out[REACH : REACH + members, :REACH] = w[:, first:last]
    off, mate = sides.pick(cols[:1, :REACH], cols[1:, REACH:])
    out[REACH : REACH + 1, REACH : 2 * REACH] = (mate if near else off).astype(F32)


def residual_rim(cols, inc, innov, prec, ops, w, one, two_off, two_mate, *rest):
    received = rest[:-4]
    res, send_off, send_mate, gw = rest[-4:]
    rows, _, size, _ = ops.shape
    members = w.shape[0]
    sides = Sides(rows)
    total = inc[...]
    for other in received:
        total = total + other[...].astype(F32)
    res[...] = prec[...] * (total * SCALE - innov[...])
    for near, send in ((False, send_off), (True, send_mate)):
        rim_rows(res, ops, sides, near, send)
        side_facts(cols, w, sides, near, send)
    index = lax.broadcasted_iota(I32, (members, rows), 1)
    grown = jnp.zeros((members, rows), F32)
    for q in range(rows):
        two, place = (two_off, q) if q < REACH else (two_mate, q - REACH)
        prod = one[:, (REACH + q) * size : (REACH + q + 1) * size].astype(F32) * res[q : q + 1, :]
        prod = prod + two[:, place * size : (place + 1) * size].astype(F32) * res[rows + q : rows + q + 1, :]
        grown = jnp.where(index == q, jnp.sum(prod, axis=1, keepdims=True), grown)
    grown = w[...] + SCALE * grown
    gw[...] = grown
    send_mate[REACH + members :, :] = jnp.broadcast_to(jnp.sum(grown * grown, axis=1, keepdims=True), (members, size))


def residual_inner(res, ops, y):
    rows, _, size, _ = ops.shape
    sides = Sides(rows)
    for row, k, q in ((sides.off_row, sides.mate_k, 0), (sides.mate_row, sides.off_k, REACH)):

        def some(ids, row=row, k=k, q=q):
            outs = []
            for i in ids:
                r = row + i
                o = dot_n(cot_row(res, rows + q + i), jnp.concatenate([ops[r, 0], ops[r, k]], 1))
                outs.append((q + i, o))
            for place, o in outs:
                y[pl.ds(place, 1), :] = o[:1, :size] + res[pl.ds(place, 1), :]
                y[pl.ds(rows + place, 1), :] = o[:1, size:]

        chunks(REACH, some)


def middle(weights, target, vals, q, mid):
    members = weights.shape[0]
    group = 8
    for g in range(REACH // group):
        place = REACH + q + g * group
        picked = [jnp.where(target == place + c, weights, 0.0).astype(BF16) for c in range(group)]
        mid[g * group * members : (g + 1) * group * members, :] = dot_n(jnp.concatenate(picked, 0), vals).astype(BF16)


def adjoint_side(cols, mid, ops, sides, near, sums):
    members = mid.shape[0] // REACH
    row, k, low = (sides.mate_row, sides.mate_k, 2 * REACH) if near else (sides.off_row, sides.off_k, 0)
    sums[...] = jnp.zeros_like(sums)

    def some(ids):
        outs = []
        for i in ids:
            x = mid[pl.ds(pl.multiple_of(i * members, members), members), :]
            outs.append((sides.place(cols[k - 1, row + i]) - low, dot_n(x, ops[row + i, k])))
        for place, o in outs:
            sums[place] = sums[place] + o

    chunks(REACH, some)


def adjoint_off(cols, col_rows, w, y, own_off, own_mate, off, mate, ops, mid, sums, send, vals, wp, tgt):
    rows, _, size, _ = ops.shape
    members = w.shape[0]
    sides = Sides(rows)
    vals[:rows, :] = y[:rows, :].astype(BF16)
    vals[2 * rows : 3 * rows, :] = y[rows:, :].astype(BF16)
    for n, part in enumerate((own_off, own_mate)):
        vals[rows + n * REACH : rows + (n + 1) * REACH, :] = part[:REACH, :].astype(BF16)
    for k in range(3):
        wp[:, k * rows : (k + 1) * rows] = w[...] * SCALE
    col = col_rows[...]
    rim_off, rim_mate = sides.pick(col[:1, :REACH], col[1:, REACH:])
    inner_off, inner_mate = sides.pick(col[1:, :REACH], col[:1, REACH:])
    tgt[:, :rows] = lax.broadcasted_iota(I32, (1, rows), 1) + REACH
    for n, part in enumerate((rim_off, rim_mate, inner_off, inner_mate)):
        tgt[:, rows + n * REACH : rows + (n + 1) * REACH] = sides.place(part)
    for n, part in enumerate((off, mate)):
        where = slice(3 * rows + n * REACH, 3 * rows + (n + 1) * REACH)
        vals[where, :] = part[:REACH, :].astype(BF16)
        wp[:, where] = part[REACH : REACH + members, :REACH] * SCALE
        tgt[:, where] = sides.place(part[REACH : REACH + 1, REACH : 2 * REACH].astype(I32))
    middle(wp[...], tgt[...], vals[...], 0, mid)
    adjoint_side(cols, mid, ops, sides, False, sums)
    send[...] = sums[:REACH].astype(BF16)


def adjoint_mate(cols, wp, tgt, vals, ops, mid, sums, send):
    sides = Sides(ops.shape[0])
    middle(wp[...], tgt[...], vals[...], REACH, mid)
    adjoint_side(cols, mid, ops, sides, True, sums)
    send[...] = sums[REACH:].astype(BF16)


def adjoint_inner(cols, mid_off, mid_mate, sums_off, sums_mate, ops, out):
    rows, _, size, _ = ops.shape
    members = sums_off.shape[1]
    sides = Sides(rows)
    out[:REACH] = sums_off[REACH:]
    out[REACH:] = sums_mate[:REACH]
    for row, k, q, mid in ((sides.off_row, sides.mate_k, 0, mid_off), (sides.mate_row, sides.off_k, REACH, mid_mate)):

        def some(ids, row=row, k=k, q=q, mid=mid):
            outs = []
            for i in ids:
                r = row + i
                x = mid[pl.ds(pl.multiple_of(i * members, members), members), :]
                o = dot_n(x, jnp.concatenate([ops[r, 0], ops[r, k]], 1))
                outs.append((q + i, o[:, :size]))
                outs.append((sides.place(cols[k - 1, r]) - REACH, o[:, size:]))
            for place, o in outs:
                out[place] = out[place] + o

        chunks(REACH, some)


def finish(count, own, off, mate, gw, total, out, direction):
    rows, members, size = own.shape
    sides = Sides(rows)
    weights = gw[...] / jnp.sqrt(total[:, :1] / count[0] + 1e-06)
    direction[...] = turned(sides, weights)
    for row, q, halo in ((sides.off_row, 0, off), (sides.mate_row, REACH, mate)):
        for i in range(REACH):
            lanes(out, row + i, size)[...] = own[q + i] + halo[i].astype(F32)


SMEM = pl.BlockSpec(memory_space=pltpu.SMEM)
VMEM = pl.BlockSpec(memory_space=pltpu.VMEM)
FAR = pl.BlockSpec(memory_space=pltpu.HBM)


def run(body, outs, args, scalars=0, scratch=(), far=0, alias=None, near=True):
    kind_of = pltpu.VMEM if near else jax.ShapeDtypeStruct
    return pl.pallas_call(
        body,
        out_shape=[kind_of(shape, kind) for shape, kind in outs],
        in_specs=[SMEM] * scalars + [VMEM] * (len(args) - scalars - far) + [FAR] * far,
        out_specs=[VMEM] * len(outs),
        scratch_shapes=list(scratch),
        input_output_aliases=alias or {},
        compiler_params=pltpu.CompilerParams(vmem_limit_bytes=12 * 1024 * 1024),
        name=body.__name__,
    )(*args)


def on_device(ensemble, op_blocks, col_index, weights, innovations, obs_precision):
    members = ensemble.shape[0]
    rows, per_row, size, _ = op_blocks.shape
    assert rows == 2 * REACH and per_row == 3
    length = rows * size
    halo = REACH * size
    tiles = lax.axis_size("space")
    groups = lax.axis_size("members")
    mates = [(i, i ^ 1) for i in range(tiles)]
    offs = []
    for i in range(1, tiles - 1, 2):
        offs += [(i, i + 1), (i + 1, i)]
    sem = pltpu.SemaphoreType.DMA

    def far(value):
        return pltpu.with_memory_space_constraint(value, pltpu.HBM)

    def to_mate(value):
        return lax.ppermute(value, "space", mates)

    def to_off(value):
        return lax.ppermute(value, "space", offs)

    def partner(value, stride):
        return lax.ppermute(value, "space", [(i, i ^ stride) for i in range(tiles)])

    cols = col_index.T
    acc_kind = ((rows, members, size), F32)
    wide_kind = ((members, length + 2 * halo), BF16)
    side_kind = ((members, halo), BF16)
    part_kind = ((REACH, size), F32)
    row_kind = ((2 * rows, size), F32)

    off, mate = run(load, [side_kind, side_kind], (far(ensemble),), 0, [sem((2,))], far=1)
    from_off, from_mate = to_off(off), to_mate(mate)
    acc, wide, ops = run(
        first_inner,
        [acc_kind, wide_kind, (op_blocks.shape, BF16)],
        (cols, off, mate, far(op_blocks)),
        1,
        [sem((4,))],
        far=1,
    )
    wide, one, send = run(
        first_mate, [wide_kind, wide_kind, side_kind], (cols, acc, wide, from_mate, ops), 1, alias={2: 0}
    )
    from_mate = to_mate(send)
    wide, one, send = run(
        first_off,
        [wide_kind, wide_kind, side_kind],
        (cols, acc, wide, one, from_off, ops),
        1,
        alias={2: 0, 3: 1},
    )
    from_off = to_off(send)
    acc, inc_one, innov, prec, w = run(
        second_inner,
        [acc_kind, ((rows, size), F32), row_kind, row_kind, ((members, rows), F32)],
        (cols, one, ops, weights, innovations, obs_precision),
        1,
    )
    one, two_mate, inc_mate = run(
        second_mate, [wide_kind, side_kind, part_kind], (cols, acc, one, from_mate, ops, w), 1, alias={2: 0}
    )
    one, two_off, inc, send = run(
        second_off,
        [wide_kind, side_kind, row_kind, (row_kind[0], BF16)],
        (cols, acc, one, from_off, ops, w, inc_one, inc_mate),
        1,
        alias={2: 0},
    )
    received = [lax.ppermute(send, "members", [(i, i ^ step) for i in range(groups)]) for step in range(1, groups)]
    res, own_off, own_mate, grad_weights = run(
        residual_rim,
        [row_kind, ((REACH + members, size), F32), ((REACH + 2 * members, size), F32), ((members, rows), F32)],
        (cols, inc, innov, prec, ops, w, one, two_off, two_mate, *received),
    )
    from_off, from_mate = to_off(own_off), to_mate(own_mate)
    (y,) = run(residual_inner, [row_kind], (res, ops))
    total = own_mate[REACH + members :] + from_mate[REACH + members :]
    strides = [2**power for power in range(1, tiles.bit_length() - 1)]
    total = total + partner(total, strides[0])
    pairs = 3 * rows + 2 * REACH
    mid_kind = ((REACH * members, size), BF16)
    sums_kind = ((2 * REACH, members, size), F32)
    send_kind = ((REACH, members, size), BF16)
    mid_off, sums_off, send, vals, wp, tgt = run(
        adjoint_off,
        [mid_kind, sums_kind, send_kind, ((pairs, size), BF16), ((members, pairs), F32), ((1, pairs), I32)],
        (cols, cols, w, y, own_off, own_mate, from_off, from_mate, ops),
        1,
    )
    from_off = to_off(send)
    mid_mate, sums_mate, send = run(
        adjoint_mate, [mid_kind, sums_kind, send_kind], (cols, wp, tgt, vals, ops), 1
    )
    send, total = lax.optimization_barrier((send, total))
    for stride in strides[1:]:
        total = total + partner(total, stride)
    from_mate = to_mate(send)
    (own,) = run(adjoint_inner, [acc_kind], (cols, mid_off, mid_mate, sums_off, sums_mate, ops), 1)
    grad_ens, direction = run(
        finish,
        [((members, length), F32), ((members, rows), F32)],
        (jnp.full((1,), rows * tiles, F32), own, from_off, from_mate, grad_weights, total),
        1,
        near=False,
    )
    return (grad_ens, direction)


def solution(mesh):
    placed = (
        P("members", "space"),
        P("space", None, None, None),
        P("space", None),
        P("members", "space"),
        P(None, "space"),
        P(None, "space"),
    )
    return jax.shard_map(
        on_device,
        mesh=mesh,
        in_specs=placed,
        out_specs=(P("members", "space"), P("members", "space")),
        check_vma=False,
    )
```

```python
import functools

import jax
import jax.numpy as jnp
from jax import lax
from jax.experimental import pallas as pl
from jax.experimental.pallas import tpu as pltpu
from jax.sharding import PartitionSpec as P

MEMBERS = 128
REACH = 32
SCALE = (MEMBERS - 1) ** (-0.5)
F32 = jnp.float32
BF16 = jnp.bfloat16
I32 = jnp.int32
UNROLL = 32


def dot_t(x, a):
    return lax.dot_general(x, a, (((1,), (1,)), ((), ())), preferred_element_type=F32)


def dot_n(x, a):
    return lax.dot_general(x, a, (((1,), (0,)), ((), ())), preferred_element_type=F32)


class Sides:
    def __init__(self, rows):
        place = lax.axis_index("space")
        self.even = place % 2 == 0
        self.base = place * rows
        self.flip = jnp.where(self.even, 0, 3 * REACH)
        self.off_row = jnp.where(self.even, 0, REACH)
        self.mate_row = REACH - self.off_row
        self.off_k = jnp.where(self.even, 1, 2)
        self.mate_k = 3 - self.off_k

    def place(self, col):
        return (col - self.base + REACH) ^ self.flip

    def pick(self, first, last):
        return jnp.where(self.even, first, last), jnp.where(self.even, last, first)


def lanes(ref, index, size):
    return ref.at[:, pl.ds(index * size if isinstance(index, int) else pl.multiple_of(index * size, size), size)]


def chunks(total, body):
    unroll = min(total, UNROLL)

    def step(i, carry):
        body([i * unroll + u for u in range(unroll)])
        return carry

    if total == unroll:
        body(list(range(total)))
    else:
        lax.fori_loop(0, total // unroll, step, 0)


def load(ens, off, mate, sems):
    size = ens.shape[1] // (2 * REACH)
    sides = Sides(2 * REACH)
    width = REACH * size
    copies = []
    for n, (row, out) in enumerate(((sides.off_row, off), (sides.mate_row, mate))):
        source = ens.at[:, pl.ds(pl.multiple_of(row * size, size), width)]
        copies.append(pltpu.make_async_copy(source, out, sems.at[n]))
        copies[-1].start()
    for copy in copies:
        copy.wait()


def inner(cols, wide, ops, acc, sides, ready=None):
    size = ops.shape[2]
    for row, k, q in ((sides.off_row, sides.mate_k, 0), (sides.mate_row, sides.off_k, REACH)):
        step = REACH if ready is None else REACH // 2
        for low in range(0, REACH, step):
            if ready is not None:
                ready((q + low) // step)

            def some(ids, row=row, k=k, q=q, low=low):
                outs = []
                for i in ids:
                    r = row + low + i
                    e = sides.place(cols[k - 1, r])
                    x = [lanes(wide, REACH + q + low + i, size)[...], lanes(wide, e, size)[...]]
                    outs.append((q + low + i, dot_t(jnp.concatenate(x, 1), jnp.concatenate([ops[r, 0], ops[r, k]], 1))))
                for place, o in outs:
                    acc[place] = o

            chunks(step, some)


def first_inner(cols_in, off, mate, ops_far, acc, wide, ops, cols, sems):
    rows, _, size, _ = ops.shape
    sides = Sides(rows)
    step = REACH // 2
    copies = []
    for part in range(2 * REACH // step):
        start = (sides.off_row if part * step < REACH else sides.mate_row) + part * step % REACH
        where = pl.ds(start, step)
        copies.append(pltpu.make_async_copy(ops_far.at[where], ops.at[where], sems.at[part]))
        copies[-1].start()
    for k in range(cols.shape[0]):
        for r in range(rows):
            cols[k, r] = cols_in[k, r]
    wide[:, REACH * size : 2 * REACH * size] = off[...]
    wide[:, 2 * REACH * size : 3 * REACH * size] = mate[...]
    inner(cols, wide, ops, acc, sides, lambda part: copies[part].wait())


def rim(cols, acc, wide, ops, sides, near, store):
    size = ops.shape[2]
    row, k, q = (sides.mate_row, sides.mate_k, REACH) if near else (sides.off_row, sides.off_k, 0)

    def some(ids):
        outs = []
        for i in ids:
            e = sides.place(cols[k - 1, row + i])
            outs.append((i, acc[q + i] + dot_t(lanes(wide, e, size)[...], ops[row + i, k])))
        for i, o in outs:
            store(i, o.astype(BF16))

    chunks(REACH, some)


def first_mate(cols, acc, wide_in, halo, ops, wide, out, send):
    size = ops.shape[2]
    wide[:, 3 * REACH * size :] = halo[...]

    def store(i, o):
        lanes(out, 2 * REACH + i, size)[...] = o
        lanes(send, i, size)[...] = o

    rim(cols, acc, wide, ops, Sides(ops.shape[0]), True, store)


def first_off(cols, acc, wide_in, out_in, halo, ops, wide, out, send):
    size = ops.shape[2]
    wide[:, : REACH * size] = halo[...]

    def store(i, o):
        lanes(out, REACH + i, size)[...] = o
        lanes(send, i, size)[...] = o

    rim(cols, acc, wide, ops, Sides(ops.shape[0]), False, store)


def turned(sides, w):
    swapped = jnp.concatenate([w[:, REACH:], w[:, :REACH]], 1)
    return jnp.where(sides.even, w, swapped)


def member_sums(value, start, w, first, count, size, store):
    for i in range(count):
        x = value[:, (start + i) * size : (start + i + 1) * size].astype(F32)
        store(i, jnp.sum(x * w[:, first + i : first + i + 1], axis=0, keepdims=True))


def second_inner(cols, wide, ops, w, innov, prec, acc, inc, innov_rows, prec_rows, w_turned):
    rows, _, size, _ = ops.shape
    sides = Sides(rows)
    inner(cols, wide, ops, acc, sides)
    weights = turned(sides, w[...])
    w_turned[...] = weights
    for q in range(rows):
        r = q + (sides.off_row if q < REACH else sides.mate_row - REACH)
        for time in range(2):
            place = slice(time * rows + q, time * rows + q + 1)
            innov_rows[place, :] = lanes(innov, r, size)[time : time + 1, :]
            prec_rows[place, :] = lanes(prec, r, size)[time : time + 1, :]

    def store(i, s):
        inc[i : i + 1, :] = s

    member_sums(wide, REACH, weights, 0, rows, size, store)


def second_mate(cols, acc, wide_in, halo, ops, w, wide, out, inc):
    size = ops.shape[2]
    wide[:, 3 * REACH * size :] = halo[...]

    def store(i, o):
        lanes(out, i, size)[...] = o

    rim(cols, acc, wide, ops, Sides(ops.shape[0]), True, store)

    def keep(i, s):
        inc[i : i + 1, :] = s

    member_sums(out, 0, w, REACH, REACH, size, keep)


def second_off(cols, acc, wide_in, halo, ops, w, inc_one, inc_mate, wide, out, inc, send):
    rows, _, size, _ = ops.shape
    wide[:, : REACH * size] = halo[...]

    def store(i, o):
        lanes(out, i, size)[...] = o

    rim(cols, acc, wide, ops, Sides(rows), False, store)

    def keep(i, s):
        inc[rows + i : rows + i + 1, :] = s

    member_sums(out, 0, w, 0, REACH, size, keep)
    inc[:rows, :] = inc_one[...]
    inc[rows + REACH :, :] = inc_mate[...]
    send[...] = inc[...].astype(BF16)


def cot_row(res, place):
    return jnp.broadcast_to(res[pl.ds(place, 1), :], (8, res.shape[1])).astype(BF16)


def rim_rows(res, ops, sides, near, out):
    rows = ops.shape[0]
    row, k, q = (sides.mate_row, sides.mate_k, REACH) if near else (sides.off_row, sides.off_k, 0)

    def some(ids):
        outs = [(i, dot_n(cot_row(res, rows + q + i), ops[row + i, k])) for i in ids]
        for i, o in outs:
            out[pl.ds(i, 1), :] = o[:1]

    chunks(REACH, some)


def side_facts(cols, w, sides, near, out):
    members = w.shape[0]
    first, last = (REACH, 2 * REACH) if near else (0, REACH)
    out[REACH : REACH + members, :REACH] = w[:, first:last]
    off, mate = sides.pick(cols[:1, :REACH], cols[1:, REACH:])
    out[REACH : REACH + 1, REACH : 2 * REACH] = (mate if near else off).astype(F32)


def residual_rim(cols, inc, innov, prec, ops, w, one, two_off, two_mate, *rest):
    received = rest[:-4]
    res, send_off, send_mate, gw = rest[-4:]
    rows, _, size, _ = ops.shape
    members = w.shape[0]
    sides = Sides(rows)
    total = inc[...]
    for other in received:
        total = total + other[...].astype(F32)
    res[...] = prec[...] * (total * SCALE - innov[...])
    for near, send in ((False, send_off), (True, send_mate)):
        rim_rows(res, ops, sides, near, send)
        side_facts(cols, w, sides, near, send)
    index = lax.broadcasted_iota(I32, (members, rows), 1)
    grown = jnp.zeros((members, rows), F32)
    for q in range(rows):
        two, place = (two_off, q) if q < REACH else (two_mate, q - REACH)
        prod = one[:, (REACH + q) * size : (REACH + q + 1) * size].astype(F32) * res[q : q + 1, :]
        prod = prod + two[:, place * size : (place + 1) * size].astype(F32) * res[rows + q : rows + q + 1, :]
        grown = jnp.where(index == q, jnp.sum(prod, axis=1, keepdims=True), grown)
    grown = w[...] + SCALE * grown
    gw[...] = grown
    send_mate[REACH + members :, :] = jnp.broadcast_to(jnp.sum(grown * grown, axis=1, keepdims=True), (members, size))


def residual_inner(res, ops, y):
    rows, _, size, _ = ops.shape
    sides = Sides(rows)
    for row, k, q in ((sides.off_row, sides.mate_k, 0), (sides.mate_row, sides.off_k, REACH)):

        def some(ids, row=row, k=k, q=q):
            outs = []
            for i in ids:
                r = row + i
                o = dot_n(cot_row(res, rows + q + i), jnp.concatenate([ops[r, 0], ops[r, k]], 1))
                outs.append((q + i, o))
            for place, o in outs:
                y[pl.ds(place, 1), :] = o[:1, :size] + res[pl.ds(place, 1), :]
                y[pl.ds(rows + place, 1), :] = o[:1, size:]

        chunks(REACH, some)


def middle(weights, target, vals, q, mid):
    members = weights.shape[0]
    group = 8
    for g in range(REACH // group):
        place = REACH + q + g * group
        picked = [jnp.where(target == place + c, weights, 0.0).astype(BF16) for c in range(group)]
        mid[g * group * members : (g + 1) * group * members, :] = dot_n(jnp.concatenate(picked, 0), vals).astype(BF16)


def adjoint_side(cols, mid, ops, sides, near, sums):
    members = mid.shape[0] // REACH
    row, k, low = (sides.mate_row, sides.mate_k, 2 * REACH) if near else (sides.off_row, sides.off_k, 0)
    sums[...] = jnp.zeros_like(sums)

    def some(ids):
        outs = []
        for i in ids:
            x = mid[pl.ds(pl.multiple_of(i * members, members), members), :]
            outs.append((sides.place(cols[k - 1, row + i]) - low, dot_n(x, ops[row + i, k])))
        for place, o in outs:
            sums[place] = sums[place] + o

    chunks(REACH, some)


def adjoint_off(cols, col_rows, w, y, own_off, own_mate, off, mate, ops, mid, sums, send, vals, wp, tgt):
    rows, _, size, _ = ops.shape
    members = w.shape[0]
    sides = Sides(rows)
    vals[:rows, :] = y[:rows, :].astype(BF16)
    vals[2 * rows : 3 * rows, :] = y[rows:, :].astype(BF16)
    for n, part in enumerate((own_off, own_mate)):
        vals[rows + n * REACH : rows + (n + 1) * REACH, :] = part[:REACH, :].astype(BF16)
    for k in range(3):
        wp[:, k * rows : (k + 1) * rows] = w[...] * SCALE
    col = col_rows[...]
    rim_off, rim_mate = sides.pick(col[:1, :REACH], col[1:, REACH:])
    inner_off, inner_mate = sides.pick(col[1:, :REACH], col[:1, REACH:])
    tgt[:, :rows] = lax.broadcasted_iota(I32, (1, rows), 1) + REACH
    for n, part in enumerate((rim_off, rim_mate, inner_off, inner_mate)):
        tgt[:, rows + n * REACH : rows + (n + 1) * REACH] = sides.place(part)
    for n, part in enumerate((off, mate)):
        where = slice(3 * rows + n * REACH, 3 * rows + (n + 1) * REACH)
        vals[where, :] = part[:REACH, :].astype(BF16)
        wp[:, where] = part[REACH : REACH + members, :REACH] * SCALE
        tgt[:, where] = sides.place(part[REACH : REACH + 1, REACH : 2 * REACH].astype(I32))
    middle(wp[...], tgt[...], vals[...], 0, mid)
    adjoint_side(cols, mid, ops, sides, False, sums)
    send[...] = sums[:REACH].astype(BF16)


def adjoint_mate(cols, wp, tgt, vals, ops, mid, sums, send):
    sides = Sides(ops.shape[0])
    middle(wp[...], tgt[...], vals[...], REACH, mid)
    adjoint_side(cols, mid, ops, sides, True, sums)
    send[...] = sums[REACH:].astype(BF16)


def adjoint_inner(cols, mid_off, mid_mate, sums_off, sums_mate, ops, out):
    rows, _, size, _ = ops.shape
    members = sums_off.shape[1]
    sides = Sides(rows)
    out[:REACH] = sums_off[REACH:]
    out[REACH:] = sums_mate[:REACH]
    for row, k, q, mid in ((sides.off_row, sides.mate_k, 0, mid_off), (sides.mate_row, sides.off_k, REACH, mid_mate)):

        def some(ids, row=row, k=k, q=q, mid=mid):
            outs = []
            for i in ids:
                r = row + i
                x = mid[pl.ds(pl.multiple_of(i * members, members), members), :]
                o = dot_n(x, jnp.concatenate([ops[r, 0], ops[r, k]], 1))
                outs.append((q + i, o[:, :size]))
                outs.append((sides.place(cols[k - 1, r]) - REACH, o[:, size:]))
            for place, o in outs:
                out[place] = out[place] + o

        chunks(REACH, some)


def finish(own, off, mate, gw, total, out, direction, *, count):
    rows, members, size = own.shape
    sides = Sides(rows)
    weights = gw[...] / jnp.sqrt(total[:, :1] / count + 1e-06)
    direction[...] = turned(sides, weights)
    for row, q, halo in ((sides.off_row, 0, off), (sides.mate_row, REACH, mate)):
        for i in range(REACH):
            lanes(out, row + i, size)[...] = own[q + i] + halo[i].astype(F32)


SMEM = pl.BlockSpec(memory_space=pltpu.SMEM)
VMEM = pl.BlockSpec(memory_space=pltpu.VMEM)
FAR = pl.BlockSpec(memory_space=pltpu.HBM)


def run(body, outs, args, scalars=0, scratch=(), far=0, alias=None, near=True, table=None, **fixed):
    kind_of = pltpu.VMEM if near else jax.ShapeDtypeStruct
    shapes = [kind_of(shape, kind) for shape, kind in outs]
    places = [VMEM] * len(outs)
    if table is not None:
        shapes.append(pltpu.SMEM(table, I32))
        places.append(SMEM)
    return pl.pallas_call(
        functools.partial(body, **fixed) if fixed else body,
        out_shape=shapes,
        in_specs=[SMEM] * scalars + [VMEM] * (len(args) - scalars - far) + [FAR] * far,
        out_specs=places,
        scratch_shapes=list(scratch),
        input_output_aliases=alias or {},
        compiler_params=pltpu.CompilerParams(vmem_limit_bytes=12 * 1024 * 1024),
        name=body.__name__,
    )(*args)


def on_device(ensemble, op_blocks, col_index, weights, innovations, obs_precision):
    members = ensemble.shape[0]
    rows, per_row, size, _ = op_blocks.shape
    assert rows == 2 * REACH and per_row == 3
    length = rows * size
    halo = REACH * size
    tiles = lax.axis_size("space")
    groups = lax.axis_size("members")
    mates = [(i, i ^ 1) for i in range(tiles)]
    offs = []
    for i in range(1, tiles - 1, 2):
        offs += [(i, i + 1), (i + 1, i)]
    sem = pltpu.SemaphoreType.DMA

    def far(value):
        return pltpu.with_memory_space_constraint(value, pltpu.HBM)

    def to_mate(value):
        return lax.ppermute(value, "space", mates)

    def to_off(value):
        return lax.ppermute(value, "space", offs)

    def partner(value, stride):
        return lax.ppermute(value, "space", [(i, i ^ stride) for i in range(tiles)])

    cols = col_index.T
    acc_kind = ((rows, members, size), F32)
    wide_kind = ((members, length + 2 * halo), BF16)
    side_kind = ((members, halo), BF16)
    part_kind = ((REACH, size), F32)
    row_kind = ((2 * rows, size), F32)

    off, mate = run(load, [side_kind, side_kind], (far(ensemble),), 0, [sem((2,))], far=1)
    from_off, from_mate = to_off(off), to_mate(mate)
    acc, wide, ops, table = run(
        first_inner,
        [acc_kind, wide_kind, (op_blocks.shape, BF16)],
        (cols, off, mate, far(op_blocks)),
        1,
        [sem((4,))],
        far=1,
        table=cols.shape,
    )
    wide, one, send = run(
        first_mate, [wide_kind, wide_kind, side_kind], (table, acc, wide, from_mate, ops), 1, alias={2: 0}
    )
    from_mate = to_mate(send)
    wide, one, send = run(
        first_off,
        [wide_kind, wide_kind, side_kind],
        (table, acc, wide, one, from_off, ops),
        1,
        alias={2: 0, 3: 1},
    )
    from_off = to_off(send)
    acc, inc_one, innov, prec, w = run(
        second_inner,
        [acc_kind, ((rows, size), F32), row_kind, row_kind, ((members, rows), F32)],
        (table, one, ops, weights, innovations, obs_precision),
        1,
    )
    one, two_mate, inc_mate = run(
        second_mate, [wide_kind, side_kind, part_kind], (table, acc, one, from_mate, ops, w), 1, alias={2: 0}
    )
    one, two_off, inc, send = run(
        second_off,
        [wide_kind, side_kind, row_kind, (row_kind[0], BF16)],
        (table, acc, one, from_off, ops, w, inc_one, inc_mate),
        1,
        alias={2: 0},
    )
    received = [lax.ppermute(send, "members", [(i, i ^ step) for i in range(groups)]) for step in range(1, groups)]
    res, own_off, own_mate, grad_weights = run(
        residual_rim,
        [row_kind, ((REACH + members, size), F32), ((REACH + 2 * members, size), F32), ((members, rows), F32)],
        (cols, inc, innov, prec, ops, w, one, two_off, two_mate, *received),
    )
    from_off, from_mate = to_off(own_off), to_mate(own_mate)
    (y,) = run(residual_inner, [row_kind], (res, ops))
    total = own_mate[REACH + members :] + from_mate[REACH + members :]
    strides = [2**power for power in range(1, tiles.bit_length() - 1)]
    total = total + partner(total, strides[0])
    pairs = 3 * rows + 2 * REACH
    mid_kind = ((REACH * members, size), BF16)
    sums_kind = ((2 * REACH, members, size), F32)
    send_kind = ((REACH, members, size), BF16)
    mid_off, sums_off, send, vals, wp, tgt = run(
        adjoint_off,
        [mid_kind, sums_kind, send_kind, ((pairs, size), BF16), ((members, pairs), F32), ((1, pairs), I32)],
        (table, cols, w, y, own_off, own_mate, from_off, from_mate, ops),
        1,
    )
    from_off = to_off(send)
    mid_mate, sums_mate, send = run(
        adjoint_mate, [mid_kind, sums_kind, send_kind], (table, wp, tgt, vals, ops), 1
    )
    send, total = lax.optimization_barrier((send, total))
    for stride in strides[1:]:
        total = total + partner(total, stride)
    from_mate = to_mate(send)
    (own,) = run(adjoint_inner, [acc_kind], (table, mid_off, mid_mate, sums_off, sums_mate, ops), 1)
    grad_ens, direction = run(
        finish,
        [((members, length), F32), ((members, rows), F32)],
        (own, from_off, from_mate, grad_weights, total),
        near=False,
        count=rows * tiles,
    )
    return (grad_ens, direction)


def solution(mesh):
    placed = (
        P("members", "space"),
        P("space", None, None, None),
        P("space", None),
        P("members", "space"),
        P(None, "space"),
        P(None, "space"),
    )
    return jax.shard_map(
        on_device,
        mesh=mesh,
        in_specs=placed,
        out_specs=(P("members", "space"), P("members", "space")),
        check_vma=False,
    )
```

```python
import functools

import jax
import jax.numpy as jnp
from jax import lax
from jax.experimental import pallas as pl
from jax.experimental.pallas import tpu as pltpu
from jax.sharding import PartitionSpec as P

MEMBERS = 128
REACH = 32
SCALE = (MEMBERS - 1) ** (-0.5)
F32 = jnp.float32
BF16 = jnp.bfloat16
I32 = jnp.int32
UNROLL = 32


def dot_t(x, a):
    return lax.dot_general(x, a, (((1,), (1,)), ((), ())), preferred_element_type=F32)


def dot_n(x, a):
    return lax.dot_general(x, a, (((1,), (0,)), ((), ())), preferred_element_type=F32)


class Sides:
    def __init__(self, rows):
        place = lax.axis_index("space")
        self.even = place % 2 == 0
        self.base = place * rows
        self.flip = jnp.where(self.even, 0, 3 * REACH)
        self.off_row = jnp.where(self.even, 0, REACH)
        self.mate_row = REACH - self.off_row
        self.off_k = jnp.where(self.even, 1, 2)
        self.mate_k = 3 - self.off_k

    def place(self, col):
        return (col - self.base + REACH) ^ self.flip

    def pick(self, first, last):
        return jnp.where(self.even, first, last), jnp.where(self.even, last, first)


def lanes(ref, index, size):
    return ref.at[:, pl.ds(index * size if isinstance(index, int) else pl.multiple_of(index * size, size), size)]


def chunks(total, body):
    unroll = min(total, UNROLL)

    def step(i, carry):
        body([i * unroll + u for u in range(unroll)])
        return carry

    if total == unroll:
        body(list(range(total)))
    else:
        lax.fori_loop(0, total // unroll, step, 0)


def split_terms(value):
    high = value.astype(BF16)
    return high, (value - high.astype(F32)).astype(BF16)


def as_column(row):
    count = row.shape[1]
    shape = (count, count)
    on = lax.broadcasted_iota(I32, shape, 0) == lax.broadcasted_iota(I32, shape, 1)
    return jnp.sum(jnp.where(on, jnp.broadcast_to(row.astype(F32), shape), 0.0), axis=1, keepdims=True)


def load(ens, w_far, cols_far, off, mate, w, cols, sems):
    size = ens.shape[1] // (2 * REACH)
    sides = Sides(2 * REACH)
    width = REACH * size
    copies = []
    for n, (row, out) in enumerate(((sides.off_row, off.at[:, :width]), (sides.mate_row, mate))):
        source = ens.at[:, pl.ds(pl.multiple_of(row * size, size), width)]
        copies.append(pltpu.make_async_copy(source, out, sems.at[n]))
    copies.append(pltpu.make_async_copy(w_far, w, sems.at[2]))
    copies.append(pltpu.make_async_copy(cols_far, cols, sems.at[3]))
    for copy in copies:
        copy.start()
    for copy in reversed(copies):
        copy.wait()
    high, low = split_terms(sides.pick(w[:, :REACH], w[:, REACH:])[0])
    col = sides.pick(cols[:1, :REACH], cols[1:, REACH:])[0]
    spread = [jnp.broadcast_to(part.astype(F32), high.shape).astype(BF16) for part in (col >> 8, col & 255)]
    off[:, width:] = jnp.concatenate([high, low] + spread, 1)


def inner(cols, wide, ops, acc, sides, ready=None):
    size = ops.shape[2]
    for row, k, q in ((sides.off_row, sides.mate_k, 0), (sides.mate_row, sides.off_k, REACH)):
        step = REACH if ready is None else REACH // 2
        for low in range(0, REACH, step):
            if ready is not None:
                ready((q + low) // step)

            def some(ids, row=row, k=k, q=q, low=low):
                outs = []
                for i in ids:
                    r = row + low + i
                    e = sides.place(cols[k - 1, r])
                    x = [lanes(wide, REACH + q + low + i, size)[...], lanes(wide, e, size)[...]]
                    outs.append((q + low + i, dot_t(jnp.concatenate(x, 1), jnp.concatenate([ops[r, 0], ops[r, k]], 1))))
                for place, o in outs:
                    acc[place] = o

            chunks(step, some)


def first_inner(cols_in, off, mate, ops_far, acc, wide, ops, cols, sems):
    rows, _, size, _ = ops.shape
    sides = Sides(rows)
    step = REACH // 2
    copies = []
    for part in range(2 * REACH // step):
        start = (sides.off_row if part * step < REACH else sides.mate_row) + part * step % REACH
        where = pl.ds(start, step)
        copies.append(pltpu.make_async_copy(ops_far.at[where], ops.at[where], sems.at[part]))
        copies[-1].start()
    for k in range(cols.shape[0]):
        for r in range(rows):
            cols[k, r] = cols_in[k, r]
    wide[:, REACH * size : 2 * REACH * size] = off[:, : REACH * size]
    wide[:, 2 * REACH * size : 3 * REACH * size] = mate[...]
    inner(cols, wide, ops, acc, sides, lambda part: copies[part].wait())


def rim(cols, acc, wide, ops, sides, near, store):
    size = ops.shape[2]
    row, k, q = (sides.mate_row, sides.mate_k, REACH) if near else (sides.off_row, sides.off_k, 0)

    def some(ids):
        outs = []
        for i in ids:
            e = sides.place(cols[k - 1, row + i])
            outs.append((i, acc[q + i] + dot_t(lanes(wide, e, size)[...], ops[row + i, k])))
        for i, o in outs:
            store(i, o.astype(BF16))

    chunks(REACH, some)


def first_mate(cols, acc, wide_in, halo, ops, wide, out, send):
    size = ops.shape[2]
    out[:, : REACH * size] = jnp.zeros_like(halo)
    wide[:, 3 * REACH * size :] = halo[...]

    def store(i, o):
        lanes(out, 2 * REACH + i, size)[...] = o
        lanes(send, i, size)[...] = o

    rim(cols, acc, wide, ops, Sides(ops.shape[0]), True, store)


def first_off(cols, acc, wide_in, out_in, halo, ops, wide, out, send, slot):
    size = ops.shape[2]
    width = REACH * size
    sides = Sides(ops.shape[0])
    wide[:, :width] = halo[:, :width]
    facts = halo[:, width:].astype(F32)
    weights = facts[:, :REACH] + facts[:, REACH : 2 * REACH]
    col = as_column(facts[:1, 2 * REACH : 3 * REACH] * 256.0 + facts[:1, 3 * REACH : 4 * REACH]).astype(I32)
    place = sides.place(col) - REACH
    place = jnp.where((place >= 0) & (place < REACH), place, -1)
    slot[...] = jnp.broadcast_to(place, slot.shape)

    def store(i, o):
        lanes(out, REACH + i, size)[...] = o

    rim(cols, acc, wide, ops, sides, False, store)
    for p in range(REACH):
        at = slot[p, 0]
        x = lanes(out, REACH + jnp.maximum(at, 0), size)[...].astype(F32)
        part = jnp.sum(x * weights[:, p : p + 1], axis=0, keepdims=True)
        send[p : p + 1, :] = jnp.where(at >= 0, part, 0.0)


def turned(sides, w):
    swapped = jnp.concatenate([w[:, REACH:], w[:, :REACH]], 1)
    return jnp.where(sides.even, w, swapped)


def member_sums(value, start, w, first, count, size, store):
    for i in range(count):
        x = value[:, (start + i) * size : (start + i + 1) * size].astype(F32)
        store(i, jnp.sum(x * w[:, first + i : first + i + 1], axis=0, keepdims=True))


def second_inner(cols, wide, ops, w, innov, prec, acc, inc, innov_rows, prec_rows, w_turned, two_off, inc_off):
    rows, _, size, _ = ops.shape
    sides = Sides(rows)
    inner(cols, wide, ops, acc, sides)
    weights = turned(sides, w[...])
    w_turned[...] = weights
    for q in range(rows):
        r = q + (sides.off_row if q < REACH else sides.mate_row - REACH)
        for time in range(2):
            place = slice(time * rows + q, time * rows + q + 1)
            innov_rows[place, :] = lanes(innov, r, size)[time : time + 1, :]
            prec_rows[place, :] = lanes(prec, r, size)[time : time + 1, :]

    def store(i, s):
        inc[i : i + 1, :] = s

    member_sums(wide, REACH, weights, 0, rows, size, store)

    def keep_row(i, o):
        lanes(two_off, i, size)[...] = o

    rim(cols, acc, wide, ops, sides, False, keep_row)

    def keep(i, s):
        inc_off[i : i + 1, :] = s

    member_sums(two_off, 0, weights, 0, REACH, size, keep)


def second_mate(cols, acc, wide_in, halo, ops, w, wide, out, inc):
    size = ops.shape[2]
    wide[:, 3 * REACH * size :] = halo[...]

    def store(i, o):
        lanes(out, i, size)[...] = o

    rim(cols, acc, wide, ops, Sides(ops.shape[0]), True, store)

    def keep(i, s):
        inc[i : i + 1, :] = s

    member_sums(out, 0, w, REACH, REACH, size, keep)


def second_off(halo, ops, inc_one, inc_off, inc_mate, inc, send):
    rows, _, size, _ = ops.shape
    sides = Sides(rows)
    inc[:rows, :] = inc_one[...]
    inc[rows + REACH :, :] = inc_mate[...]
    parts = []
    for i in range(REACH):
        row = jnp.broadcast_to(halo[i : i + 1, :], (8, size)).astype(BF16)
        parts.append(dot_t(row, ops[sides.off_row + i, sides.off_k]))
    for i, part in enumerate(parts):
        inc[rows + i : rows + i + 1, :] = inc_off[i : i + 1, :] + part[:1]
    send[...] = inc[...].astype(BF16)


def cot_row(res, place):
    return jnp.broadcast_to(res[pl.ds(place, 1), :], (8, res.shape[1])).astype(BF16)


def rim_rows(res, ops, sides, near, out):
    rows = ops.shape[0]
    row, k, q = (sides.mate_row, sides.mate_k, REACH) if near else (sides.off_row, sides.off_k, 0)

    def some(ids):
        outs = [(i, dot_n(cot_row(res, rows + q + i), ops[row + i, k])) for i in ids]
        for i, o in outs:
            out[pl.ds(i, 1), :] = o[:1]

    chunks(REACH, some)


def side_facts(cols, w, sides, near, out):
    members = w.shape[0]
    first, last = (REACH, 2 * REACH) if near else (0, REACH)
    out[REACH : REACH + members, :REACH] = w[:, first:last]
    off, mate = sides.pick(cols[:1, :REACH], cols[1:, REACH:])
    out[REACH : REACH + 1, REACH : 2 * REACH] = (mate if near else off).astype(F32)


def residual_rim(cols, inc, innov, prec, ops, w, one, two_off, two_mate, *rest):
    received = rest[:-4]
    res, send_off, send_mate, gw = rest[-4:]
    rows, _, size, _ = ops.shape
    members = w.shape[0]
    sides = Sides(rows)
    total = inc[...]
    for other in received:
        total = total + other[...].astype(F32)
    res[...] = prec[...] * (total * SCALE - innov[...])
    for near, send in ((False, send_off), (True, send_mate)):
        rim_rows(res, ops, sides, near, send)
        side_facts(cols, w, sides, near, send)
    index = lax.broadcasted_iota(I32, (members, rows), 1)
    grown = jnp.zeros((members, rows), F32)
    for q in range(rows):
        two, place = (two_off, q) if q < REACH else (two_mate, q - REACH)
        prod = one[:, (REACH + q) * size : (REACH + q + 1) * size].astype(F32) * res[q : q + 1, :]
        prod = prod + two[:, place * size : (place + 1) * size].astype(F32) * res[rows + q : rows + q + 1, :]
        grown = jnp.where(index == q, jnp.sum(prod, axis=1, keepdims=True), grown)
    grown = w[...] + SCALE * grown
    gw[...] = grown
    send_off[REACH : REACH + members, 2 * REACH : 3 * REACH] = grown[:, :REACH]


def residual_inner(res, ops, y):
    rows, _, size, _ = ops.shape
    sides = Sides(rows)
    for row, k, q in ((sides.off_row, sides.mate_k, 0), (sides.mate_row, sides.off_k, REACH)):

        def some(ids, row=row, k=k, q=q):
            outs = []
            for i in ids:
                r = row + i
                o = dot_n(cot_row(res, rows + q + i), jnp.concatenate([ops[r, 0], ops[r, k]], 1))
                outs.append((q + i, o))
            for place, o in outs:
                y[pl.ds(place, 1), :] = o[:1, :size] + res[pl.ds(place, 1), :]
                y[pl.ds(rows + place, 1), :] = o[:1, size:]

        chunks(REACH, some)


def middle(weights, target, vals, q, mid):
    members = weights.shape[0]
    group = 8
    for g in range(REACH // group):
        place = REACH + q + g * group
        picked = [jnp.where(target == place + c, weights, 0.0).astype(BF16) for c in range(group)]
        mid[g * group * members : (g + 1) * group * members, :] = dot_n(jnp.concatenate(picked, 0), vals).astype(BF16)


def adjoint_side(cols, mid, ops, sides, near, sums):
    members = mid.shape[0] // REACH
    row, k, low = (sides.mate_row, sides.mate_k, 2 * REACH) if near else (sides.off_row, sides.off_k, 0)
    sums[...] = jnp.zeros_like(sums)

    def some(ids):
        outs = []
        for i in ids:
            x = mid[pl.ds(pl.multiple_of(i * members, members), members), :]
            outs.append((sides.place(cols[k - 1, row + i]) - low, dot_n(x, ops[row + i, k])))
        for place, o in outs:
            sums[place] = sums[place] + o

    chunks(REACH, some)


def adjoint_off(cols, col_rows, w, y, own_off, own_mate, off, mate, ops, one, gw, slot, mid, sums, send, vals, wp, tgt, squares):
    rows, _, size, _ = ops.shape
    members = w.shape[0]
    sides = Sides(rows)
    vals[:rows, :] = y[:rows, :].astype(BF16)
    vals[2 * rows : 3 * rows, :] = y[rows:, :].astype(BF16)
    for n, part in enumerate((own_off, own_mate)):
        vals[rows + n * REACH : rows + (n + 1) * REACH, :] = part[:REACH, :].astype(BF16)
    for k in range(3):
        wp[:, k * rows : (k + 1) * rows] = w[...] * SCALE
    col = col_rows[...]
    rim_off, rim_mate = sides.pick(col[:1, :REACH], col[1:, REACH:])
    inner_off, inner_mate = sides.pick(col[1:, :REACH], col[:1, REACH:])
    tgt[:, :rows] = lax.broadcasted_iota(I32, (1, rows), 1) + REACH
    for n, part in enumerate((rim_off, rim_mate, inner_off, inner_mate)):
        tgt[:, rows + n * REACH : rows + (n + 1) * REACH] = sides.place(part)
    for n, part in enumerate((off, mate)):
        where = slice(3 * rows + n * REACH, 3 * rows + (n + 1) * REACH)
        vals[where, :] = part[:REACH, :].astype(BF16)
        wp[:, where] = part[REACH : REACH + members, :REACH] * SCALE
        tgt[:, where] = sides.place(part[REACH : REACH + 1, REACH : 2 * REACH].astype(I32))
    middle(wp[...], tgt[...], vals[...], 0, mid)
    adjoint_side(cols, mid, ops, sides, False, sums)
    send[:REACH] = sums[:REACH].astype(BF16)
    index = lax.broadcasted_iota(I32, (members, REACH), 1)
    drawn = jnp.zeros((members, REACH), F32)
    for p in range(REACH):
        at = slot[p, 0]
        x = lanes(one, REACH + jnp.maximum(at, 0), size)[...].astype(F32) * off[p : p + 1, :]
        part = jnp.where(at >= 0, jnp.sum(x, axis=1, keepdims=True), 0.0)
        drawn = jnp.where(index == p, part, drawn)
    drawn = drawn * SCALE
    high, low = split_terms(drawn)
    send[REACH] = jnp.concatenate([high, low, jnp.zeros((members, size - 2 * REACH), BF16)], 1)
    theirs = off[REACH : REACH + members, 2 * REACH : 3 * REACH]
    grown = gw[...]
    total = jnp.sum(grown * grown, axis=1, keepdims=True)
    total = total + jnp.sum((2.0 * theirs + drawn) * drawn, axis=1, keepdims=True)
    squares[...] = jnp.broadcast_to(total, squares.shape)


def adjoint_mate(cols, wp, tgt, vals, ops, mid, sums, send):
    sides = Sides(ops.shape[0])
    middle(wp[...], tgt[...], vals[...], REACH, mid)
    adjoint_side(cols, mid, ops, sides, True, sums)
    send[...] = sums[REACH:].astype(BF16)


def adjoint_inner(cols, mid_off, mid_mate, sums_off, sums_mate, ops, out):
    rows, _, size, _ = ops.shape
    members = sums_off.shape[1]
    sides = Sides(rows)
    out[:REACH] = sums_off[REACH:]
    out[REACH:] = sums_mate[:REACH]
    for row, k, q, mid in ((sides.off_row, sides.mate_k, 0, mid_off), (sides.mate_row, sides.off_k, REACH, mid_mate)):

        def some(ids, row=row, k=k, q=q, mid=mid):
            outs = []
            for i in ids:
                r = row + i
                x = mid[pl.ds(pl.multiple_of(i * members, members), members), :]
                o = dot_n(x, jnp.concatenate([ops[r, 0], ops[r, k]], 1))
                outs.append((q + i, o[:, :size]))
                outs.append((sides.place(cols[k - 1, r]) - REACH, o[:, size:]))
            for place, o in outs:
                out[place] = out[place] + o

        chunks(REACH, some)


def finish(own, off, mate, gw, total, out, direction, *, count):
    rows, members, size = own.shape
    sides = Sides(rows)
    drawn = off[REACH].astype(F32)
    grown = gw[...]
    drawn = drawn[:, :REACH] + drawn[:, REACH : 2 * REACH]
    grown = jnp.concatenate([grown[:, :REACH] + drawn, grown[:, REACH:]], 1)
    direction[...] = turned(sides, grown / jnp.sqrt(total[:, :1] / count + 1e-06))
    for row, q, halo in ((sides.off_row, 0, off), (sides.mate_row, REACH, mate)):
        for i in range(REACH):
            lanes(out, row + i, size)[...] = own[q + i] + halo[i].astype(F32)


SMEM = pl.BlockSpec(memory_space=pltpu.SMEM)
VMEM = pl.BlockSpec(memory_space=pltpu.VMEM)
FAR = pl.BlockSpec(memory_space=pltpu.HBM)


def run(body, outs, args, scalars=0, scratch=(), far=0, alias=None, near=True, table=None, **fixed):
    kind_of = pltpu.VMEM if near else jax.ShapeDtypeStruct
    shapes = [kind_of(shape, kind) for shape, kind in outs]
    places = [VMEM] * len(outs)
    if table is not None:
        shapes.append(pltpu.SMEM(table, I32))
        places.append(SMEM)
    return pl.pallas_call(
        functools.partial(body, **fixed) if fixed else body,
        out_shape=shapes,
        in_specs=[SMEM] * scalars + [VMEM] * (len(args) - scalars - far) + [FAR] * far,
        out_specs=places,
        scratch_shapes=list(scratch),
        input_output_aliases=alias or {},
        compiler_params=pltpu.CompilerParams(vmem_limit_bytes=12 * 1024 * 1024),
        name=body.__name__,
    )(*args)


def on_device(ensemble, op_blocks, col_index, weights, innovations, obs_precision):
    members = ensemble.shape[0]
    rows, per_row, size, _ = op_blocks.shape
    assert rows == 2 * REACH and per_row == 3
    length = rows * size
    halo = REACH * size
    tiles = lax.axis_size("space")
    groups = lax.axis_size("members")
    mates = [(i, i ^ 1) for i in range(tiles)]
    offs = []
    for i in range(1, tiles - 1, 2):
        offs += [(i, i + 1), (i + 1, i)]
    sem = pltpu.SemaphoreType.DMA

    def far(value):
        return pltpu.with_memory_space_constraint(value, pltpu.HBM)

    def to_mate(value):
        return lax.ppermute(value, "space", mates)

    def to_off(value):
        return lax.ppermute(value, "space", offs)

    def partner(value, stride):
        return lax.ppermute(value, "space", [(i, i ^ stride) for i in range(tiles)])

    cols = col_index.T
    acc_kind = ((rows, members, size), F32)
    wide_kind = ((members, length + 2 * halo), BF16)
    side_kind = ((members, halo), BF16)
    part_kind = ((REACH, size), F32)
    row_kind = ((2 * rows, size), F32)

    off, mate = run(
        load,
        [((members, halo + 4 * REACH), BF16), side_kind],
        (far(ensemble), far(weights), far(cols)),
        0,
        [pltpu.VMEM((members, rows), F32), pltpu.VMEM(cols.shape, I32), sem((4,))],
        far=3,
    )
    from_off, from_mate = to_off(off), to_mate(mate)
    acc, wide, ops, table = run(
        first_inner,
        [acc_kind, wide_kind, (op_blocks.shape, BF16)],
        (cols, off, mate, far(op_blocks)),
        1,
        [sem((4,))],
        far=1,
        table=cols.shape,
    )
    wide, one, send = run(
        first_mate, [wide_kind, wide_kind, side_kind], (table, acc, wide, from_mate, ops), 1, alias={2: 0}
    )
    from_mate = to_mate(send)
    wide, one, send, slot = run(
        first_off,
        [wide_kind, wide_kind, part_kind, ((REACH, size), I32)],
        (table, acc, wide, one, from_off, ops),
        1,
        alias={2: 0, 3: 1},
    )
    from_off = to_off(send)
    acc, inc_one, innov, prec, w, two_off, inc_off = run(
        second_inner,
        [acc_kind, ((rows, size), F32), row_kind, row_kind, ((members, rows), F32), side_kind, part_kind],
        (table, one, ops, weights, innovations, obs_precision),
        1,
    )
    one, two_mate, inc_mate = run(
        second_mate, [wide_kind, side_kind, part_kind], (table, acc, one, from_mate, ops, w), 1, alias={2: 0}
    )
    inc, send = run(second_off, [row_kind, (row_kind[0], BF16)], (from_off, ops, inc_one, inc_off, inc_mate))
    received = [lax.ppermute(send, "members", [(i, i ^ step) for i in range(groups)]) for step in range(1, groups)]
    pay_kind = ((REACH + members, size), F32)
    res, own_off, own_mate, grad_weights = run(
        residual_rim,
        [row_kind, pay_kind, pay_kind, ((members, rows), F32)],
        (cols, inc, innov, prec, ops, w, one, two_off, two_mate, *received),
    )
    from_off, from_mate = to_off(own_off), to_mate(own_mate)
    (y,) = run(residual_inner, [row_kind], (res, ops))
    pairs = 3 * rows + 2 * REACH
    mid_kind = ((REACH * members, size), BF16)
    sums_kind = ((2 * REACH, members, size), F32)
    send_kind = ((REACH, members, size), BF16)
    mid_off, sums_off, send, vals, wp, tgt, total = run(
        adjoint_off,
        [
            mid_kind,
            sums_kind,
            ((REACH + 1, members, size), BF16),
            ((pairs, size), BF16),
            ((members, pairs), F32),
            ((1, pairs), I32),
            ((members, size), F32),
        ],
        (table, cols, w, y, own_off, own_mate, from_off, from_mate, ops, one, grad_weights, slot),
        1,
    )
    from_off = to_off(send)
    total = total + partner(total, 1)
    mid_mate, sums_mate, send = run(
        adjoint_mate, [mid_kind, sums_kind, send_kind], (table, wp, tgt, vals, ops), 1
    )
    send, total = lax.optimization_barrier((send, total))
    from_mate = to_mate(send)
    stride = 2
    while stride < tiles:
        total = total + partner(total, stride)
        stride *= 2
    (own,) = run(adjoint_inner, [acc_kind], (table, mid_off, mid_mate, sums_off, sums_mate, ops), 1)
    grad_ens, direction = run(
        finish,
        [((members, length), F32), ((members, rows), F32)],
        (own, from_off, from_mate, grad_weights, total),
        near=False,
        count=rows * tiles,
    )
    return (grad_ens, direction)


def solution(mesh):
    placed = (
        P("members", "space"),
        P("space", None, None, None),
        P("space", None),
        P("members", "space"),
        P(None, "space"),
        P(None, "space"),
    )
    return jax.shard_map(
        on_device,
        mesh=mesh,
        in_specs=placed,
        out_specs=(P("members", "space"), P("members", "space")),
        check_vma=False,
    )
```

```python
import functools

import jax
import jax.numpy as jnp
from jax import lax
from jax.experimental import pallas as pl
from jax.experimental.pallas import tpu as pltpu
from jax.sharding import PartitionSpec as P

MEMBERS = 128
REACH = 32
SCALE = (MEMBERS - 1) ** (-0.5)
F32 = jnp.float32
BF16 = jnp.bfloat16
I32 = jnp.int32
UNROLL = 32


def dot_t(x, a):
    return lax.dot_general(x, a, (((1,), (1,)), ((), ())), preferred_element_type=F32)


def dot_n(x, a):
    return lax.dot_general(x, a, (((1,), (0,)), ((), ())), preferred_element_type=F32)


class Sides:
    def __init__(self, rows):
        place = lax.axis_index("space")
        self.even = place % 2 == 0
        self.base = place * rows
        self.flip = jnp.where(self.even, 0, 3 * REACH)
        self.off_row = jnp.where(self.even, 0, REACH)
        self.mate_row = REACH - self.off_row
        self.off_k = jnp.where(self.even, 1, 2)
        self.mate_k = 3 - self.off_k

    def place(self, col):
        return (col - self.base + REACH) ^ self.flip

    def pick(self, first, last):
        return jnp.where(self.even, first, last), jnp.where(self.even, last, first)


def lanes(ref, index, size):
    return ref.at[:, pl.ds(index * size if isinstance(index, int) else pl.multiple_of(index * size, size), size)]


def chunks(total, body):
    unroll = min(total, UNROLL)

    def step(i, carry):
        body([i * unroll + u for u in range(unroll)])
        return carry

    if total == unroll:
        body(list(range(total)))
    else:
        lax.fori_loop(0, total // unroll, step, 0)


def split_terms(value):
    high = value.astype(BF16)
    return high, (value - high.astype(F32)).astype(BF16)


def as_column(row):
    count = row.shape[1]
    shape = (count, count)
    on = lax.broadcasted_iota(I32, shape, 0) == lax.broadcasted_iota(I32, shape, 1)
    return jnp.sum(jnp.where(on, jnp.broadcast_to(row.astype(F32), shape), 0.0), axis=1, keepdims=True)


def load(ens, w_far, cols_far, off, mate, w, cols, sems):
    size = ens.shape[1] // (2 * REACH)
    sides = Sides(2 * REACH)
    width = REACH * size
    copies = []
    for n, (row, out) in enumerate(((sides.off_row, off.at[:, :width]), (sides.mate_row, mate))):
        source = ens.at[:, pl.ds(pl.multiple_of(row * size, size), width)]
        copies.append(pltpu.make_async_copy(source, out, sems.at[n]))
    copies.append(pltpu.make_async_copy(w_far, w, sems.at[2]))
    copies.append(pltpu.make_async_copy(cols_far, cols, sems.at[3]))
    for copy in copies:
        copy.start()
    for copy in reversed(copies):
        copy.wait()
    high, low = split_terms(sides.pick(w[:, :REACH], w[:, REACH:])[0])
    col = sides.pick(cols[:1, :REACH], cols[1:, REACH:])[0]
    spread = [jnp.broadcast_to(part.astype(F32), high.shape).astype(BF16) for part in (col >> 8, col & 255)]
    off[:, width:] = jnp.concatenate([high, low] + spread, 1)


def inner(cols, wide, ops, acc, sides, ready=None):
    size = ops.shape[2]
    for row, k, q in ((sides.off_row, sides.mate_k, 0), (sides.mate_row, sides.off_k, REACH)):
        step = REACH if ready is None else REACH // 2
        for low in range(0, REACH, step):
            if ready is not None:
                ready((q + low) // step)

            def some(ids, row=row, k=k, q=q, low=low):
                outs = []
                for i in ids:
                    r = row + low + i
                    e = sides.place(cols[k - 1, r])
                    x = [lanes(wide, REACH + q + low + i, size)[...], lanes(wide, e, size)[...]]
                    outs.append((q + low + i, dot_t(jnp.concatenate(x, 1), jnp.concatenate([ops[r, 0], ops[r, k]], 1))))
                for place, o in outs:
                    acc[place] = o

            chunks(step, some)


def first_inner(cols_in, off, mate, ops_far, acc, wide, ops, cols, sems):
    rows, _, size, _ = ops.shape
    sides = Sides(rows)
    step = REACH // 2
    copies = []
    for part in range(2 * REACH // step):
        start = (sides.off_row if part * step < REACH else sides.mate_row) + part * step % REACH
        where = pl.ds(start, step)
        copies.append(pltpu.make_async_copy(ops_far.at[where], ops.at[where], sems.at[part]))
        copies[-1].start()
    for k in range(cols.shape[0]):
        for r in range(rows):
            cols[k, r] = cols_in[k, r]
    wide[:, REACH * size : 2 * REACH * size] = off[:, : REACH * size]
    wide[:, 2 * REACH * size : 3 * REACH * size] = mate[...]
    inner(cols, wide, ops, acc, sides, lambda part: copies[part].wait())


def rim(cols, acc, wide, ops, sides, near, store):
    size = ops.shape[2]
    row, k, q = (sides.mate_row, sides.mate_k, REACH) if near else (sides.off_row, sides.off_k, 0)

    def some(ids):
        outs = []
        for i in ids:
            e = sides.place(cols[k - 1, row + i])
            outs.append((i, acc[q + i] + dot_t(lanes(wide, e, size)[...], ops[row + i, k])))
        for i, o in outs:
            store(i, o.astype(BF16))

    chunks(REACH, some)


def first_mate(cols, acc, wide_in, halo, ops, wide, out, send):
    size = ops.shape[2]
    out[:, : REACH * size] = jnp.zeros_like(halo)
    wide[:, 3 * REACH * size :] = halo[...]

    def store(i, o):
        lanes(out, 2 * REACH + i, size)[...] = o
        lanes(send, i, size)[...] = o

    rim(cols, acc, wide, ops, Sides(ops.shape[0]), True, store)


def first_off(cols, acc, wide_in, out_in, halo, ops, wide, out, send, slot):
    size = ops.shape[2]
    width = REACH * size
    sides = Sides(ops.shape[0])
    wide[:, :width] = halo[:, :width]
    facts = halo[:, width:].astype(F32)
    weights = facts[:, :REACH] + facts[:, REACH : 2 * REACH]
    col = as_column(facts[:1, 2 * REACH : 3 * REACH] * 256.0 + facts[:1, 3 * REACH : 4 * REACH]).astype(I32)
    place = sides.place(col) - REACH
    place = jnp.where((place >= 0) & (place < REACH), place, -1)
    slot[...] = jnp.broadcast_to(place, slot.shape)

    def store(i, o):
        lanes(out, REACH + i, size)[...] = o

    rim(cols, acc, wide, ops, sides, False, store)
    for p in range(REACH):
        at = slot[p, 0]
        x = lanes(out, REACH + jnp.maximum(at, 0), size)[...].astype(F32)
        part = jnp.sum(x * weights[:, p : p + 1], axis=0, keepdims=True)
        send[p : p + 1, :] = jnp.where(at >= 0, part, 0.0)


def turned(sides, w):
    swapped = jnp.concatenate([w[:, REACH:], w[:, :REACH]], 1)
    return jnp.where(sides.even, w, swapped)


def member_sums(value, start, w, first, count, size, store):
    for i in range(count):
        x = value[:, (start + i) * size : (start + i + 1) * size].astype(F32)
        store(i, jnp.sum(x * w[:, first + i : first + i + 1], axis=0, keepdims=True))


def second_inner(cols, wide, ops, w, innov, prec, acc, inc, innov_rows, prec_rows, w_turned, two_off, inc_off):
    rows, _, size, _ = ops.shape
    sides = Sides(rows)
    inner(cols, wide, ops, acc, sides)
    weights = turned(sides, w[...])
    w_turned[...] = weights
    for q in range(rows):
        r = q + (sides.off_row if q < REACH else sides.mate_row - REACH)
        for time in range(2):
            place = slice(time * rows + q, time * rows + q + 1)
            innov_rows[place, :] = lanes(innov, r, size)[time : time + 1, :]
            prec_rows[place, :] = lanes(prec, r, size)[time : time + 1, :]

    def store(i, s):
        inc[i : i + 1, :] = s

    member_sums(wide, REACH, weights, 0, rows, size, store)

    def keep_row(i, o):
        lanes(two_off, i, size)[...] = o

    rim(cols, acc, wide, ops, sides, False, keep_row)

    def keep(i, s):
        inc_off[i : i + 1, :] = s

    member_sums(two_off, 0, weights, 0, REACH, size, keep)


def second_mate(cols, acc, wide_in, halo, ops, w, wide, out, inc):
    size = ops.shape[2]
    wide[:, 3 * REACH * size :] = halo[...]

    def store(i, o):
        lanes(out, i, size)[...] = o

    rim(cols, acc, wide, ops, Sides(ops.shape[0]), True, store)

    def keep(i, s):
        inc[i : i + 1, :] = s

    member_sums(out, 0, w, REACH, REACH, size, keep)


def second_off(halo, ops, inc_one, inc_off, inc_mate, inc, send):
    rows, _, size, _ = ops.shape
    sides = Sides(rows)
    inc[:rows, :] = inc_one[...]
    inc[rows + REACH :, :] = inc_mate[...]
    parts = []
    for i in range(REACH):
        row = jnp.broadcast_to(halo[i : i + 1, :], (8, size)).astype(BF16)
        parts.append(dot_t(row, ops[sides.off_row + i, sides.off_k]))
    for i, part in enumerate(parts):
        inc[rows + i : rows + i + 1, :] = inc_off[i : i + 1, :] + part[:1]
    send[...] = inc[...].astype(BF16)


def cot_row(res, place):
    return jnp.broadcast_to(res[pl.ds(place, 1), :], (8, res.shape[1])).astype(BF16)


def rim_rows(res, ops, sides, near, out):
    rows = ops.shape[0]
    row, k, q = (sides.mate_row, sides.mate_k, REACH) if near else (sides.off_row, sides.off_k, 0)

    def some(ids):
        outs = [(i, dot_n(cot_row(res, rows + q + i), ops[row + i, k])) for i in ids]
        for i, o in outs:
            out[pl.ds(i, 1), :] = o[:1]

    chunks(REACH, some)


def side_facts(cols, w, sides, near, out):
    members = w.shape[0]
    first, last = (REACH, 2 * REACH) if near else (0, REACH)
    out[REACH : REACH + members, :REACH] = w[:, first:last]
    off, mate = sides.pick(cols[:1, :REACH], cols[1:, REACH:])
    out[REACH : REACH + 1, REACH : 2 * REACH] = (mate if near else off).astype(F32)


def residual_rim(cols, inc, innov, prec, ops, w, one, two_off, two_mate, *rest):
    received = rest[:-4]
    res, send_off, send_mate, gw = rest[-4:]
    rows, _, size, _ = ops.shape
    members = w.shape[0]
    sides = Sides(rows)
    total = inc[...]
    for other in received:
        total = total + other[...].astype(F32)
    res[...] = prec[...] * (total * SCALE - innov[...])
    for near, send in ((False, send_off), (True, send_mate)):
        rim_rows(res, ops, sides, near, send)
        side_facts(cols, w, sides, near, send)
    index = lax.broadcasted_iota(I32, (members, rows), 1)
    grown = jnp.zeros((members, rows), F32)
    for q in range(rows):
        two, place = (two_off, q) if q < REACH else (two_mate, q - REACH)
        prod = one[:, (REACH + q) * size : (REACH + q + 1) * size].astype(F32) * res[q : q + 1, :]
        prod = prod + two[:, place * size : (place + 1) * size].astype(F32) * res[rows + q : rows + q + 1, :]
        grown = jnp.where(index == q, jnp.sum(prod, axis=1, keepdims=True), grown)
    grown = w[...] + SCALE * grown
    gw[...] = grown
    send_off[REACH : REACH + members, 2 * REACH : 3 * REACH] = grown[:, :REACH]


def residual_inner(res, ops, y):
    rows, _, size, _ = ops.shape
    sides = Sides(rows)
    for row, k, q in ((sides.off_row, sides.mate_k, 0), (sides.mate_row, sides.off_k, REACH)):

        def some(ids, row=row, k=k, q=q):
            outs = []
            for i in ids:
                r = row + i
                o = dot_n(cot_row(res, rows + q + i), jnp.concatenate([ops[r, 0], ops[r, k]], 1))
                outs.append((q + i, o))
            for place, o in outs:
                y[pl.ds(place, 1), :] = o[:1, :size] + res[pl.ds(place, 1), :]
                y[pl.ds(rows + place, 1), :] = o[:1, size:]

        chunks(REACH, some)


def middle(weights, target, vals, q, mid):
    members = weights.shape[0]
    group = 8
    for g in range(REACH // group):
        place = REACH + q + g * group
        picked = [jnp.where(target == place + c, weights, 0.0).astype(BF16) for c in range(group)]
        mid[g * group * members : (g + 1) * group * members, :] = dot_n(jnp.concatenate(picked, 0), vals).astype(BF16)


def adjoint_side(cols, mid, ops, sides, near, sums):
    members = mid.shape[0] // REACH
    row, k, low = (sides.mate_row, sides.mate_k, 2 * REACH) if near else (sides.off_row, sides.off_k, 0)
    sums[...] = jnp.zeros_like(sums)

    def some(ids):
        outs = []
        for i in ids:
            x = mid[pl.ds(pl.multiple_of(i * members, members), members), :]
            outs.append((sides.place(cols[k - 1, row + i]) - low, dot_n(x, ops[row + i, k])))
        for place, o in outs:
            sums[place] = sums[place] + o

    chunks(REACH, some)


def adjoint_off(cols, col_rows, w, y, own_off, own_mate, off, mate, ops, one, gw, slot, mid, sums, send, vals, wp, tgt, squares):
    rows, _, size, _ = ops.shape
    members = w.shape[0]
    sides = Sides(rows)
    vals[:rows, :] = y[:rows, :].astype(BF16)
    vals[2 * rows : 3 * rows, :] = y[rows:, :].astype(BF16)
    for n, part in enumerate((own_off, own_mate)):
        vals[rows + n * REACH : rows + (n + 1) * REACH, :] = part[:REACH, :].astype(BF16)
    for k in range(3):
        wp[:, k * rows : (k + 1) * rows] = w[...] * SCALE
    col = col_rows[...]
    rim_off, rim_mate = sides.pick(col[:1, :REACH], col[1:, REACH:])
    inner_off, inner_mate = sides.pick(col[1:, :REACH], col[:1, REACH:])
    tgt[:, :rows] = lax.broadcasted_iota(I32, (1, rows), 1) + REACH
    for n, part in enumerate((rim_off, rim_mate, inner_off, inner_mate)):
        tgt[:, rows + n * REACH : rows + (n + 1) * REACH] = sides.place(part)
    for n, part in enumerate((off, mate)):
        where = slice(3 * rows + n * REACH, 3 * rows + (n + 1) * REACH)
        vals[where, :] = part[:REACH, :].astype(BF16)
        wp[:, where] = part[REACH : REACH + members, :REACH] * SCALE
        tgt[:, where] = sides.place(part[REACH : REACH + 1, REACH : 2 * REACH].astype(I32))
    middle(wp[...], tgt[...], vals[...], 0, mid)
    adjoint_side(cols, mid, ops, sides, False, sums)
    send[:REACH] = sums[:REACH].astype(BF16)
    index = lax.broadcasted_iota(I32, (members, REACH), 1)
    drawn = jnp.zeros((members, REACH), F32)
    for p in range(REACH):
        at = slot[p, 0]
        x = lanes(one, REACH + jnp.maximum(at, 0), size)[...].astype(F32) * off[p : p + 1, :]
        part = jnp.where(at >= 0, jnp.sum(x, axis=1, keepdims=True), 0.0)
        drawn = jnp.where(index == p, part, drawn)
    drawn = drawn * SCALE
    high, low = split_terms(drawn)
    send[REACH] = jnp.concatenate([high, low, jnp.zeros((members, size - 2 * REACH), BF16)], 1)
    theirs = off[REACH : REACH + members, 2 * REACH : 3 * REACH]
    grown = gw[...]
    total = jnp.sum(grown * grown, axis=1, keepdims=True)
    total = total + jnp.sum((2.0 * theirs + drawn) * drawn, axis=1, keepdims=True)
    squares[...] = jnp.broadcast_to(total, squares.shape)


def adjoint_mate(cols, wp, tgt, vals, ops, mid, sums, send):
    sides = Sides(ops.shape[0])
    middle(wp[...], tgt[...], vals[...], REACH, mid)
    adjoint_side(cols, mid, ops, sides, True, sums)
    send[...] = sums[REACH:].astype(BF16)


def adjoint_inner(cols, mid_off, mid_mate, sums_off, sums_mate, ops, out):
    rows, _, size, _ = ops.shape
    members = sums_off.shape[1]
    sides = Sides(rows)
    out[:REACH] = sums_off[REACH:]
    out[REACH:] = sums_mate[:REACH]
    for row, k, q, mid in ((sides.off_row, sides.mate_k, 0, mid_off), (sides.mate_row, sides.off_k, REACH, mid_mate)):

        def some(ids, row=row, k=k, q=q, mid=mid):
            outs = []
            for i in ids:
                r = row + i
                x = mid[pl.ds(pl.multiple_of(i * members, members), members), :]
                o = dot_n(x, jnp.concatenate([ops[r, 0], ops[r, k]], 1))
                outs.append((q + i, o[:, :size]))
                outs.append((sides.place(cols[k - 1, r]) - REACH, o[:, size:]))
            for place, o in outs:
                out[place] = out[place] + o

        chunks(REACH, some)


def finish(own, off, mate, out):
    size = own.shape[2]
    sides = Sides(own.shape[0])
    for row, q, halo in ((sides.off_row, 0, off), (sides.mate_row, REACH, mate)):
        for i in range(REACH):
            lanes(out, row + i, size)[...] = own[q + i] + halo[i].astype(F32)


def normalize(off, gw, total, mate_total, direction, *, count):
    drawn = off[REACH].astype(F32)
    drawn = drawn[:, :REACH] + drawn[:, REACH : 2 * REACH]
    grown = gw[...]
    grown = jnp.concatenate([grown[:, :REACH] + drawn, grown[:, REACH:]], 1)
    mean = (total[:, :1] + mate_total[:, :1]) / count
    direction[...] = turned(Sides(2 * REACH), grown / jnp.sqrt(mean + 1e-06))


SMEM = pl.BlockSpec(memory_space=pltpu.SMEM)
VMEM = pl.BlockSpec(memory_space=pltpu.VMEM)
FAR = pl.BlockSpec(memory_space=pltpu.HBM)


def run(body, outs, args, scalars=0, scratch=(), far=0, alias=None, near=True, table=None, **fixed):
    kind_of = pltpu.VMEM if near else jax.ShapeDtypeStruct
    shapes = [kind_of(shape, kind) for shape, kind in outs]
    places = [VMEM] * len(outs)
    if table is not None:
        shapes.append(pltpu.SMEM(table, I32))
        places.append(SMEM)
    return pl.pallas_call(
        functools.partial(body, **fixed) if fixed else body,
        out_shape=shapes,
        in_specs=[SMEM] * scalars + [VMEM] * (len(args) - scalars - far) + [FAR] * far,
        out_specs=places,
        scratch_shapes=list(scratch),
        input_output_aliases=alias or {},
        compiler_params=pltpu.CompilerParams(vmem_limit_bytes=12 * 1024 * 1024),
        name=body.__name__,
    )(*args)


def on_device(ensemble, op_blocks, col_index, weights, innovations, obs_precision):
    members = ensemble.shape[0]
    rows, per_row, size, _ = op_blocks.shape
    assert rows == 2 * REACH and per_row == 3
    length = rows * size
    halo = REACH * size
    tiles = lax.axis_size("space")
    groups = lax.axis_size("members")
    mates = [(i, i ^ 1) for i in range(tiles)]
    offs = []
    for i in range(1, tiles - 1, 2):
        offs += [(i, i + 1), (i + 1, i)]
    sem = pltpu.SemaphoreType.DMA

    def far(value):
        return pltpu.with_memory_space_constraint(value, pltpu.HBM)

    def to_mate(value):
        return lax.ppermute(value, "space", mates)

    def to_off(value):
        return lax.ppermute(value, "space", offs)

    def partner(value, stride):
        return lax.ppermute(value, "space", [(i, i ^ stride) for i in range(tiles)])

    cols = col_index.T
    acc_kind = ((rows, members, size), F32)
    wide_kind = ((members, length + 2 * halo), BF16)
    side_kind = ((members, halo), BF16)
    part_kind = ((REACH, size), F32)
    row_kind = ((2 * rows, size), F32)

    off, mate = run(
        load,
        [((members, halo + 4 * REACH), BF16), side_kind],
        (far(ensemble), far(weights), far(cols)),
        0,
        [pltpu.VMEM((members, rows), F32), pltpu.VMEM(cols.shape, I32), sem((4,))],
        far=3,
    )
    from_off, from_mate = to_off(off), to_mate(mate)
    acc, wide, ops, table = run(
        first_inner,
        [acc_kind, wide_kind, (op_blocks.shape, BF16)],
        (cols, off, mate, far(op_blocks)),
        1,
        [sem((4,))],
        far=1,
        table=cols.shape,
    )
    wide, one, send = run(
        first_mate, [wide_kind, wide_kind, side_kind], (table, acc, wide, from_mate, ops), 1, alias={2: 0}
    )
    from_mate = to_mate(send)
    wide, one, send, slot = run(
        first_off,
        [wide_kind, wide_kind, part_kind, ((REACH, size), I32)],
        (table, acc, wide, one, from_off, ops),
        1,
        alias={2: 0, 3: 1},
    )
    from_off = to_off(send)
    acc, inc_one, innov, prec, w, two_off, inc_off = run(
        second_inner,
        [acc_kind, ((rows, size), F32), row_kind, row_kind, ((members, rows), F32), side_kind, part_kind],
        (table, one, ops, weights, innovations, obs_precision),
        1,
    )
    one, two_mate, inc_mate = run(
        second_mate, [wide_kind, side_kind, part_kind], (table, acc, one, from_mate, ops, w), 1, alias={2: 0}
    )
    inc, send = run(second_off, [row_kind, (row_kind[0], BF16)], (from_off, ops, inc_one, inc_off, inc_mate))
    received = [lax.ppermute(send, "members", [(i, i ^ step) for i in range(groups)]) for step in range(1, groups)]
    pay_kind = ((REACH + members, size), F32)
    res, own_off, own_mate, grad_weights = run(
        residual_rim,
        [row_kind, pay_kind, pay_kind, ((members, rows), F32)],
        (cols, inc, innov, prec, ops, w, one, two_off, two_mate, *received),
    )
    from_off, from_mate = to_off(own_off), to_mate(own_mate)
    (y,) = run(residual_inner, [row_kind], (res, ops))
    pairs = 3 * rows + 2 * REACH
    mid_kind = ((REACH * members, size), BF16)
    sums_kind = ((2 * REACH, members, size), F32)
    send_kind = ((REACH, members, size), BF16)
    mid_off, sums_off, send, vals, wp, tgt, total = run(
        adjoint_off,
        [
            mid_kind,
            sums_kind,
            ((REACH + 1, members, size), BF16),
            ((pairs, size), BF16),
            ((members, pairs), F32),
            ((1, pairs), I32),
            ((members, size), F32),
        ],
        (table, cols, w, y, own_off, own_mate, from_off, from_mate, ops, one, grad_weights, slot),
        1,
    )
    from_off = to_off(send)
    total = total + partner(total, 2)
    mid_mate, sums_mate, send = run(
        adjoint_mate, [mid_kind, sums_kind, send_kind], (table, wp, tgt, vals, ops), 1
    )
    send, total = lax.optimization_barrier((send, total))
    from_mate = to_mate(send)
    stride = 4
    while stride < tiles:
        total = total + partner(total, stride)
        stride *= 2
    (own,) = run(adjoint_inner, [acc_kind], (table, mid_off, mid_mate, sums_off, sums_mate, ops), 1)
    total, own = lax.optimization_barrier((total, own))
    mate_total = to_mate(total)
    (grad_ens,) = run(finish, [((members, length), F32)], (own, from_off, from_mate), near=False)
    grad_ens, grad_weights = lax.optimization_barrier((grad_ens, grad_weights))
    (direction,) = run(
        normalize,
        [((members, rows), F32)],
        (from_off, grad_weights, total, mate_total),
        near=False,
        count=rows * tiles,
    )
    return (grad_ens, direction)


def solution(mesh):
    placed = (
        P("members", "space"),
        P("space", None, None, None),
        P("space", None),
        P("members", "space"),
        P(None, "space"),
        P(None, "space"),
    )
    return jax.shard_map(
        on_device,
        mesh=mesh,
        in_specs=placed,
        out_specs=(P("members", "space"), P("members", "space")),
        check_vma=False,
    )
```

```python
import functools

import jax
import jax.numpy as jnp
from jax import lax
from jax.experimental import pallas as pl
from jax.experimental.pallas import tpu as pltpu
from jax.sharding import PartitionSpec as P

MEMBERS = 128
REACH = 32
SCALE = (MEMBERS - 1) ** (-0.5)
F32 = jnp.float32
BF16 = jnp.bfloat16
I32 = jnp.int32
UNROLL = 32


def dot_t(x, a):
    return lax.dot_general(x, a, (((1,), (1,)), ((), ())), preferred_element_type=F32)


def dot_n(x, a):
    return lax.dot_general(x, a, (((1,), (0,)), ((), ())), preferred_element_type=F32)


class Sides:
    def __init__(self, rows):
        place = lax.axis_index("space")
        self.even = place % 2 == 0
        self.base = place * rows
        self.flip = jnp.where(self.even, 0, 3 * REACH)
        self.off_row = jnp.where(self.even, 0, REACH)
        self.mate_row = REACH - self.off_row
        self.off_k = jnp.where(self.even, 1, 2)
        self.mate_k = 3 - self.off_k

    def place(self, col):
        return (col - self.base + REACH) ^ self.flip

    def pick(self, first, last):
        return jnp.where(self.even, first, last), jnp.where(self.even, last, first)


def lanes(ref, index, size):
    return ref.at[:, pl.ds(index * size if isinstance(index, int) else pl.multiple_of(index * size, size), size)]


def chunks(total, body):
    unroll = min(total, UNROLL)

    def step(i, carry):
        body([i * unroll + u for u in range(unroll)])
        return carry

    if total == unroll:
        body(list(range(total)))
    else:
        lax.fori_loop(0, total // unroll, step, 0)


def split_terms(value):
    high = value.astype(BF16)
    return high, (value - high.astype(F32)).astype(BF16)


def as_column(row):
    count = row.shape[1]
    shape = (count, count)
    on = lax.broadcasted_iota(I32, shape, 0) == lax.broadcasted_iota(I32, shape, 1)
    return jnp.sum(jnp.where(on, jnp.broadcast_to(row.astype(F32), shape), 0.0), axis=1, keepdims=True)


def load(ens, w_far, cols_far, off, mate, w, cols, sems):
    size = ens.shape[1] // (2 * REACH)
    sides = Sides(2 * REACH)
    width = REACH * size
    copies = []
    for n, (row, out) in enumerate(((sides.off_row, off.at[:, :width]), (sides.mate_row, mate))):
        source = ens.at[:, pl.ds(pl.multiple_of(row * size, size), width)]
        copies.append(pltpu.make_async_copy(source, out, sems.at[n]))
    copies.append(pltpu.make_async_copy(w_far, w, sems.at[2]))
    copies.append(pltpu.make_async_copy(cols_far, cols, sems.at[3]))
    for copy in copies:
        copy.start()
    copies[3].wait()
    copies[2].wait()
    high, low = split_terms(sides.pick(w[:, :REACH], w[:, REACH:])[0])
    col = sides.pick(cols[:1, :REACH], cols[1:, REACH:])[0]
    spread = [jnp.broadcast_to(part.astype(F32), high.shape).astype(BF16) for part in (col >> 8, col & 255)]
    off[:, width:] = jnp.concatenate([high, low] + spread, 1)
    copies[1].wait()
    copies[0].wait()


def inner(cols, wide, ops, acc, sides, ready=None):
    size = ops.shape[2]
    for row, k, q in ((sides.off_row, sides.mate_k, 0), (sides.mate_row, sides.off_k, REACH)):
        step = REACH if ready is None else REACH // 2
        for low in range(0, REACH, step):
            if ready is not None:
                ready((q + low) // step)

            def some(ids, row=row, k=k, q=q, low=low):
                outs = []
                for i in ids:
                    r = row + low + i
                    e = sides.place(cols[k - 1, r])
                    x = [lanes(wide, REACH + q + low + i, size)[...], lanes(wide, e, size)[...]]
                    outs.append((q + low + i, dot_t(jnp.concatenate(x, 1), jnp.concatenate([ops[r, 0], ops[r, k]], 1))))
                for place, o in outs:
                    acc[place] = o

            chunks(step, some)


def first_inner(cols_in, off, mate, ops_far, acc, wide, ops, cols, sems):
    rows, _, size, _ = ops.shape
    sides = Sides(rows)
    step = REACH // 2
    copies = []
    for part in range(2 * REACH // step):
        start = (sides.off_row if part * step < REACH else sides.mate_row) + part * step % REACH
        where = pl.ds(start, step)
        copies.append(pltpu.make_async_copy(ops_far.at[where], ops.at[where], sems.at[part]))
        copies[-1].start()
    for k in range(cols.shape[0]):
        for r in range(rows):
            cols[k, r] = cols_in[k, r]
    wide[:, REACH * size : 2 * REACH * size] = off[:, : REACH * size]
    wide[:, 2 * REACH * size : 3 * REACH * size] = mate[...]
    inner(cols, wide, ops, acc, sides, lambda part: copies[part].wait())


def rim(cols, acc, wide, ops, sides, near, store):
    size = ops.shape[2]
    row, k, q = (sides.mate_row, sides.mate_k, REACH) if near else (sides.off_row, sides.off_k, 0)

    def some(ids):
        outs = []
        for i in ids:
            e = sides.place(cols[k - 1, row + i])
            outs.append((i, acc[q + i] + dot_t(lanes(wide, e, size)[...], ops[row + i, k])))
        for i, o in outs:
            store(i, o.astype(BF16))

    chunks(REACH, some)


def first_mate(cols, acc, wide_in, halo, ops, wide, out, send):
    size = ops.shape[2]
    out[:, : REACH * size] = jnp.zeros_like(halo)
    wide[:, 3 * REACH * size :] = halo[...]

    def store(i, o):
        lanes(out, 2 * REACH + i, size)[...] = o
        lanes(send, i, size)[...] = o

    rim(cols, acc, wide, ops, Sides(ops.shape[0]), True, store)


def first_off(cols, acc, wide_in, out_in, halo, ops, wide, out, send, slot, near_w, near_at, sums):
    size = ops.shape[2]
    width = REACH * size
    sides = Sides(ops.shape[0])
    wide[:, :width] = halo[:, :width]
    facts = halo[:, width:].astype(F32)
    weights = facts[:, :REACH] + facts[:, REACH : 2 * REACH]
    col = facts[:1, 2 * REACH : 3 * REACH] * 256.0 + facts[:1, 3 * REACH : 4 * REACH]
    near_w[...] = weights
    near_at[...] = sides.place(col.astype(I32))
    place = sides.place(as_column(col).astype(I32)) - REACH
    place = jnp.where((place >= 0) & (place < REACH), place, -1)
    slot[...] = jnp.broadcast_to(place, slot.shape)

    def store(i, o):
        lanes(out, REACH + i, size)[...] = o

    rim(cols, acc, wide, ops, sides, False, store)
    for p in range(REACH):
        at = slot[p, 0]
        x = lanes(out, REACH + jnp.maximum(at, 0), size)[...].astype(F32)
        part = jnp.sum(x * weights[:, p : p + 1], axis=0, keepdims=True)
        sums[p : p + 1, :] = jnp.where(at >= 0, part, 0.0)
    send[...] = sums[...].astype(BF16)


def turned(sides, w):
    swapped = jnp.concatenate([w[:, REACH:], w[:, :REACH]], 1)
    return jnp.where(sides.even, w, swapped)


def member_sums(value, start, w, first, count, size, store):
    for i in range(count):
        x = value[:, (start + i) * size : (start + i + 1) * size].astype(F32)
        store(i, jnp.sum(x * w[:, first + i : first + i + 1], axis=0, keepdims=True))


def second_inner(cols, wide, ops, w, innov, prec, acc, inc, innov_rows, prec_rows, w_turned, two_off, inc_off):
    rows, _, size, _ = ops.shape
    sides = Sides(rows)
    inner(cols, wide, ops, acc, sides)
    weights = turned(sides, w[...])
    w_turned[...] = weights
    for q in range(rows):
        r = q + (sides.off_row if q < REACH else sides.mate_row - REACH)
        for time in range(2):
            place = slice(time * rows + q, time * rows + q + 1)
            innov_rows[place, :] = lanes(innov, r, size)[time : time + 1, :]
            prec_rows[place, :] = lanes(prec, r, size)[time : time + 1, :]

    def store(i, s):
        inc[i : i + 1, :] = s

    member_sums(wide, REACH, weights, 0, rows, size, store)

    def keep_row(i, o):
        lanes(two_off, i, size)[...] = o

    rim(cols, acc, wide, ops, sides, False, keep_row)

    def keep(i, s):
        inc_off[i : i + 1, :] = s

    member_sums(two_off, 0, weights, 0, REACH, size, keep)


def second_mate(cols, acc, wide_in, halo, ops, w, wide, out, inc):
    size = ops.shape[2]
    wide[:, 3 * REACH * size :] = halo[...]

    def store(i, o):
        lanes(out, i, size)[...] = o

    rim(cols, acc, wide, ops, Sides(ops.shape[0]), True, store)

    def keep(i, s):
        inc[i : i + 1, :] = s

    member_sums(out, 0, w, REACH, REACH, size, keep)


def second_off(halo, ops, inc_one, inc_off, inc_mate, inc, send):
    rows, _, size, _ = ops.shape
    sides = Sides(rows)
    inc[:rows, :] = inc_one[...]
    inc[rows + REACH :, :] = inc_mate[...]
    parts = []
    for i in range(REACH):
        row = jnp.broadcast_to(halo[i : i + 1, :].astype(F32), (8, size)).astype(BF16)
        parts.append(dot_t(row, ops[sides.off_row + i, sides.off_k]))
    for i, part in enumerate(parts):
        inc[rows + i : rows + i + 1, :] = inc_off[i : i + 1, :] + part[:1]
    send[...] = inc[...].astype(BF16)


def cot_row(res, place):
    return jnp.broadcast_to(res[pl.ds(place, 1), :], (8, res.shape[1])).astype(BF16)


def rim_rows(res, ops, sides, near, out):
    rows = ops.shape[0]
    row, k, q = (sides.mate_row, sides.mate_k, REACH) if near else (sides.off_row, sides.off_k, 0)

    def some(ids):
        outs = [(i, dot_n(cot_row(res, rows + q + i), ops[row + i, k])) for i in ids]
        for i, o in outs:
            out[pl.ds(i, 1), :] = o[:1]

    chunks(REACH, some)


def residual_rim(cols, inc, innov, prec, ops, w, one, two_off, two_mate, *rest):
    received = rest[:-5]
    res, rim_off, send_off, send_mate, gw = rest[-5:]
    rows, _, size, _ = ops.shape
    members = w.shape[0]
    sides = Sides(rows)
    total = inc[...]
    for other in received:
        total = total + other[...].astype(F32)
    res[...] = prec[...] * (total * SCALE - innov[...])
    rim_rows(res, ops, sides, False, rim_off)
    rim_rows(res, ops, sides, True, send_mate)
    send_off[:REACH, :] = rim_off[...].astype(BF16)
    send_mate[REACH:, :REACH] = w[:, REACH:]
    send_mate[REACH : REACH + 1, REACH : 2 * REACH] = sides.pick(cols[:1, :REACH], cols[1:, REACH:])[1].astype(F32)
    index = lax.broadcasted_iota(I32, (members, rows), 1)
    grown = jnp.zeros((members, rows), F32)
    for q in range(rows):
        two, place = (two_off, q) if q < REACH else (two_mate, q - REACH)
        prod = one[:, (REACH + q) * size : (REACH + q + 1) * size].astype(F32) * res[q : q + 1, :]
        prod = prod + two[:, place * size : (place + 1) * size].astype(F32) * res[rows + q : rows + q + 1, :]
        grown = jnp.where(index == q, jnp.sum(prod, axis=1, keepdims=True), grown)
    grown = w[...] + SCALE * grown
    gw[...] = grown
    high, low = split_terms(grown[:, :REACH])
    send_off[REACH:, :] = jnp.concatenate([high, low, jnp.zeros((members, size - 2 * REACH), BF16)], 1)


def residual_inner(res, ops, y):
    rows, _, size, _ = ops.shape
    sides = Sides(rows)
    for row, k, q in ((sides.off_row, sides.mate_k, 0), (sides.mate_row, sides.off_k, REACH)):

        def some(ids, row=row, k=k, q=q):
            outs = []
            for i in ids:
                r = row + i
                o = dot_n(cot_row(res, rows + q + i), jnp.concatenate([ops[r, 0], ops[r, k]], 1))
                outs.append((q + i, o))
            for place, o in outs:
                y[pl.ds(place, 1), :] = o[:1, :size] + res[pl.ds(place, 1), :]
                y[pl.ds(rows + place, 1), :] = o[:1, size:]

        chunks(REACH, some)


def middle(weights, target, vals, q, mid):
    members = weights.shape[0]
    group = 8
    for g in range(REACH // group):
        place = REACH + q + g * group
        picked = [jnp.where(target == place + c, weights, 0.0).astype(BF16) for c in range(group)]
        mid[g * group * members : (g + 1) * group * members, :] = dot_n(jnp.concatenate(picked, 0), vals).astype(BF16)


def adjoint_side(cols, mid, ops, sides, near, sums):
    members = mid.shape[0] // REACH
    row, k, low = (sides.mate_row, sides.mate_k, 2 * REACH) if near else (sides.off_row, sides.off_k, 0)
    sums[...] = jnp.zeros_like(sums)

    def some(ids):
        outs = []
        for i in ids:
            x = mid[pl.ds(pl.multiple_of(i * members, members), members), :]
            outs.append((sides.place(cols[k - 1, row + i]) - low, dot_n(x, ops[row + i, k])))
        for place, o in outs:
            sums[place] = sums[place] + o

    chunks(REACH, some)


def adjoint_off(cols, col_rows, w, y, own_off, own_mate, off, mate, near_w, near_at, ops, one, gw, slot, mid, sums, send, vals, wp, tgt, squares):
    rows, _, size, _ = ops.shape
    members = w.shape[0]
    sides = Sides(rows)
    vals[:rows, :] = y[:rows, :].astype(BF16)
    vals[2 * rows : 3 * rows, :] = y[rows:, :].astype(BF16)
    for n, part in enumerate((own_off, own_mate)):
        vals[rows + n * REACH : rows + (n + 1) * REACH, :] = part[:REACH, :].astype(BF16)
    for k in range(3):
        wp[:, k * rows : (k + 1) * rows] = w[...] * SCALE
    col = col_rows[...]
    rim_off, rim_mate = sides.pick(col[:1, :REACH], col[1:, REACH:])
    inner_off, inner_mate = sides.pick(col[1:, :REACH], col[:1, REACH:])
    tgt[:, :rows] = lax.broadcasted_iota(I32, (1, rows), 1) + REACH
    for n, part in enumerate((rim_off, rim_mate, inner_off, inner_mate)):
        tgt[:, rows + n * REACH : rows + (n + 1) * REACH] = sides.place(part)
    where = slice(3 * rows, 3 * rows + REACH)
    vals[where, :] = off[:REACH, :]
    wp[:, where] = near_w[...] * SCALE
    tgt[:, where] = near_at[...]
    where = slice(3 * rows + REACH, 3 * rows + 2 * REACH)
    vals[where, :] = mate[:REACH, :].astype(BF16)
    wp[:, where] = mate[REACH:, :REACH] * SCALE
    tgt[:, where] = sides.place(mate[REACH : REACH + 1, REACH : 2 * REACH].astype(I32))
    middle(wp[...], tgt[...], vals[...], 0, mid)
    adjoint_side(cols, mid, ops, sides, False, sums)
    send[:REACH] = sums[:REACH].astype(BF16)
    index = lax.broadcasted_iota(I32, (members, REACH), 1)
    drawn = jnp.zeros((members, REACH), F32)
    for p in range(REACH):
        at = slot[p, 0]
        x = lanes(one, REACH + jnp.maximum(at, 0), size)[...].astype(F32) * off[p : p + 1, :].astype(F32)
        part = jnp.where(at >= 0, jnp.sum(x, axis=1, keepdims=True), 0.0)
        drawn = jnp.where(index == p, part, drawn)
    drawn = drawn * SCALE
    high, low = split_terms(drawn)
    send[REACH] = jnp.concatenate([high, low, jnp.zeros((members, size - 2 * REACH), BF16)], 1)
    theirs = off[REACH:, :REACH].astype(F32) + off[REACH:, REACH : 2 * REACH].astype(F32)
    grown = gw[...]
    total = jnp.sum(grown * grown, axis=1, keepdims=True)
    total = total + jnp.sum((2.0 * theirs + drawn) * drawn, axis=1, keepdims=True)
    squares[...] = jnp.broadcast_to(total, squares.shape)


def adjoint_mate(cols, wp, tgt, vals, ops, mid, sums, send):
    sides = Sides(ops.shape[0])
    middle(wp[...], tgt[...], vals[...], REACH, mid)
    adjoint_side(cols, mid, ops, sides, True, sums)
    send[...] = sums[REACH:].astype(BF16)


def adjoint_inner(cols, mid_off, mid_mate, sums_off, sums_mate, ops, out):
    rows, _, size, _ = ops.shape
    members = sums_off.shape[1]
    sides = Sides(rows)
    out[:REACH] = sums_off[REACH:]
    out[REACH:] = sums_mate[:REACH]
    for row, k, q, mid in ((sides.off_row, sides.mate_k, 0, mid_off), (sides.mate_row, sides.off_k, REACH, mid_mate)):

        def some(ids, row=row, k=k, q=q, mid=mid):
            outs = []
            for i in ids:
                r = row + i
                x = mid[pl.ds(pl.multiple_of(i * members, members), members), :]
                o = dot_n(x, jnp.concatenate([ops[r, 0], ops[r, k]], 1))
                outs.append((q + i, o[:, :size]))
                outs.append((sides.place(cols[k - 1, r]) - REACH, o[:, size:]))
            for place, o in outs:
                out[place] = out[place] + o

        chunks(REACH, some)


def finish(own, off, mate, gw, total, mate_total, out, direction, *, count):
    size = own.shape[2]
    sides = Sides(own.shape[0])
    drawn = off[REACH].astype(F32)
    drawn = drawn[:, :REACH] + drawn[:, REACH : 2 * REACH]
    grown = gw[...]
    grown = jnp.concatenate([grown[:, :REACH] + drawn, grown[:, REACH:]], 1)
    mean = (total[:, :1] + mate_total[:, :1]) / count
    direction[...] = turned(sides, grown / jnp.sqrt(mean + 1e-06))
    for row, q, halo in ((sides.off_row, 0, off), (sides.mate_row, REACH, mate)):
        for i in range(REACH):
            lanes(out, row + i, size)[...] = own[q + i] + halo[i].astype(F32)


SMEM = pl.BlockSpec(memory_space=pltpu.SMEM)
VMEM = pl.BlockSpec(memory_space=pltpu.VMEM)
FAR = pl.BlockSpec(memory_space=pltpu.HBM)


def run(body, outs, args, scalars=0, scratch=(), far=0, alias=None, near=True, table=None, **fixed):
    kind_of = pltpu.VMEM if near else jax.ShapeDtypeStruct
    shapes = [kind_of(shape, kind) for shape, kind in outs]
    places = [VMEM] * len(outs)
    if table is not None:
        shapes.append(pltpu.SMEM(table, I32))
        places.append(SMEM)
    return pl.pallas_call(
        functools.partial(body, **fixed) if fixed else body,
        out_shape=shapes,
        in_specs=[SMEM] * scalars + [VMEM] * (len(args) - scalars - far) + [FAR] * far,
        out_specs=places,
        scratch_shapes=list(scratch),
        input_output_aliases=alias or {},
        compiler_params=pltpu.CompilerParams(vmem_limit_bytes=12 * 1024 * 1024),
        name=body.__name__,
    )(*args)


def on_device(ensemble, op_blocks, col_index, weights, innovations, obs_precision):
    members = ensemble.shape[0]
    rows, per_row, size, _ = op_blocks.shape
    assert rows == 2 * REACH and per_row == 3
    length = rows * size
    halo = REACH * size
    tiles = lax.axis_size("space")
    groups = lax.axis_size("members")
    mates = [(i, i ^ 1) for i in range(tiles)]
    offs = []
    for i in range(1, tiles - 1, 2):
        offs += [(i, i + 1), (i + 1, i)]
    sem = pltpu.SemaphoreType.DMA

    def far(value):
        return pltpu.with_memory_space_constraint(value, pltpu.HBM)

    def to_mate(value):
        return lax.ppermute(value, "space", mates)

    def to_off(value):
        return lax.ppermute(value, "space", offs)

    def partner(value, stride):
        return lax.ppermute(value, "space", [(i, i ^ stride) for i in range(tiles)])

    cols = col_index.T
    acc_kind = ((rows, members, size), F32)
    wide_kind = ((members, length + 2 * halo), BF16)
    side_kind = ((members, halo), BF16)
    part_kind = ((REACH, size), F32)
    row_kind = ((2 * rows, size), F32)

    off, mate = run(
        load,
        [((members, halo + 4 * REACH), BF16), side_kind],
        (far(ensemble), far(weights), far(cols)),
        0,
        [pltpu.VMEM((members, rows), F32), pltpu.VMEM(cols.shape, I32), sem((4,))],
        far=3,
    )
    from_off, from_mate = to_off(off), to_mate(mate)
    acc, wide, ops, table = run(
        first_inner,
        [acc_kind, wide_kind, (op_blocks.shape, BF16)],
        (cols, off, mate, far(op_blocks)),
        1,
        [sem((4,))],
        far=1,
        table=cols.shape,
    )
    wide, one, send = run(
        first_mate, [wide_kind, wide_kind, side_kind], (table, acc, wide, from_mate, ops), 1, alias={2: 0}
    )
    from_mate = to_mate(send)
    wide, one, send, slot, near_w, near_at = run(
        first_off,
        [
            wide_kind,
            wide_kind,
            ((REACH, size), BF16),
            ((REACH, size), I32),
            ((members, REACH), F32),
            ((1, REACH), I32),
        ],
        (table, acc, wide, one, from_off, ops),
        1,
        [pltpu.VMEM((REACH, size), F32)],
        alias={2: 0, 3: 1},
    )
    from_off = to_off(send)
    acc, inc_one, innov, prec, w, two_off, inc_off = run(
        second_inner,
        [acc_kind, ((rows, size), F32), row_kind, row_kind, ((members, rows), F32), side_kind, part_kind],
        (table, one, ops, weights, innovations, obs_precision),
        1,
    )
    one, two_mate, inc_mate = run(
        second_mate, [wide_kind, side_kind, part_kind], (table, acc, one, from_mate, ops, w), 1, alias={2: 0}
    )
    inc, send = run(second_off, [row_kind, (row_kind[0], BF16)], (from_off, ops, inc_one, inc_off, inc_mate))
    received = [lax.ppermute(send, "members", [(i, i ^ step) for i in range(groups)]) for step in range(1, groups)]
    pay_kind = ((REACH + members, size), F32)
    res, rim_off, own_off, own_mate, grad_weights = run(
        residual_rim,
        [row_kind, part_kind, (pay_kind[0], BF16), pay_kind, ((members, rows), F32)],
        (cols, inc, innov, prec, ops, w, one, two_off, two_mate, *received),
    )
    from_off, from_mate = to_off(own_off), to_mate(own_mate)
    (y,) = run(residual_inner, [row_kind], (res, ops))
    pairs = 3 * rows + 2 * REACH
    mid_kind = ((REACH * members, size), BF16)
    sums_kind = ((2 * REACH, members, size), F32)
    send_kind = ((REACH, members, size), BF16)
    mid_off, sums_off, send, vals, wp, tgt, total = run(
        adjoint_off,
        [
            mid_kind,
            sums_kind,
            ((REACH + 1, members, size), BF16),
            ((pairs, size), BF16),
            ((members, pairs), F32),
            ((1, pairs), I32),
            ((members, size), F32),
        ],
        (table, cols, w, y, rim_off, own_mate, from_off, from_mate, near_w, near_at, ops, one, grad_weights, slot),
        1,
    )
    from_off = to_off(send)
    total = total + partner(total, 2)
    mid_mate, sums_mate, send = run(
        adjoint_mate, [mid_kind, sums_kind, send_kind], (table, wp, tgt, vals, ops), 1
    )
    send, total = lax.optimization_barrier((send, total))
    from_mate = to_mate(send)
    stride = 4
    while stride < tiles:
        total = total + partner(total, stride)
        stride *= 2
    (own,) = run(adjoint_inner, [acc_kind], (table, mid_off, mid_mate, sums_off, sums_mate, ops), 1)
    total, own = lax.optimization_barrier((total, own))
    mate_total = to_mate(total)
    grad_ens, direction = run(
        finish,
        [((members, length), F32), ((members, rows), F32)],
        (own, from_off, from_mate, grad_weights, total, mate_total),
        near=False,
        count=rows * tiles,
    )
    return (grad_ens, direction)


def solution(mesh):
    placed = (
        P("members", "space"),
        P("space", None, None, None),
        P("space", None),
        P("members", "space"),
        P(None, "space"),
        P(None, "space"),
    )
    return jax.shard_map(
        on_device,
        mesh=mesh,
        in_specs=placed,
        out_specs=(P("members", "space"), P("members", "space")),
        check_vma=False,
    )
```

```python
import functools

import jax
import jax.numpy as jnp
from jax import lax
from jax.experimental import pallas as pl
from jax.experimental.pallas import tpu as pltpu
from jax.sharding import PartitionSpec as P

MEMBERS = 128
REACH = 32
SCALE = (MEMBERS - 1) ** (-0.5)
F32 = jnp.float32
BF16 = jnp.bfloat16
I32 = jnp.int32
UNROLL = 32
HOPS = 5


def dot_t(x, a):
    return lax.dot_general(x, a, (((1,), (1,)), ((), ())), preferred_element_type=F32)


def dot_n(x, a):
    return lax.dot_general(x, a, (((1,), (0,)), ((), ())), preferred_element_type=F32)


class Sides:
    def __init__(self, rows):
        place = lax.axis_index("space")
        self.even = place % 2 == 0
        self.base = place * rows
        self.flip = jnp.where(self.even, 0, 3 * REACH)
        self.off_row = jnp.where(self.even, 0, REACH)
        self.mate_row = REACH - self.off_row
        self.off_k = jnp.where(self.even, 1, 2)
        self.mate_k = 3 - self.off_k

    def place(self, col):
        return (col - self.base + REACH) ^ self.flip

    def pick(self, first, last):
        return jnp.where(self.even, first, last), jnp.where(self.even, last, first)


def lanes(ref, index, size):
    return ref.at[:, pl.ds(index * size if isinstance(index, int) else pl.multiple_of(index * size, size), size)]


def chunks(total, body):
    unroll = min(total, UNROLL)

    def step(i, carry):
        body([i * unroll + u for u in range(unroll)])
        return carry

    if total == unroll:
        body(list(range(total)))
    else:
        lax.fori_loop(0, total // unroll, step, 0)


def split_terms(value):
    high = value.astype(BF16)
    return high, (value - high.astype(F32)).astype(BF16)


def as_column(row):
    count = row.shape[1]
    shape = (count, count)
    on = lax.broadcasted_iota(I32, shape, 0) == lax.broadcasted_iota(I32, shape, 1)
    return jnp.sum(jnp.where(on, jnp.broadcast_to(row.astype(F32), shape), 0.0), axis=1, keepdims=True)


def load(ens, w_far, cols_far, off, mate, w, cols, sems):
    size = ens.shape[1] // (2 * REACH)
    sides = Sides(2 * REACH)
    width = REACH * size
    copies = []
    for n, (row, out) in enumerate(((sides.off_row, off.at[:, :width]), (sides.mate_row, mate))):
        source = ens.at[:, pl.ds(pl.multiple_of(row * size, size), width)]
        copies.append(pltpu.make_async_copy(source, out, sems.at[n]))
    copies.append(pltpu.make_async_copy(w_far, w, sems.at[2]))
    copies.append(pltpu.make_async_copy(cols_far, cols, sems.at[3]))
    for copy in copies:
        copy.start()
    copies[3].wait()
    copies[2].wait()
    high, low = split_terms(sides.pick(w[:, :REACH], w[:, REACH:])[0])
    col = sides.pick(cols[:1, :REACH], cols[1:, REACH:])[0]
    spread = [jnp.broadcast_to(part.astype(F32), high.shape).astype(BF16) for part in (col >> 8, col & 255)]
    off[:, width:] = jnp.concatenate([high, low] + spread, 1)
    copies[1].wait()
    copies[0].wait()


def inner(cols, wide, ops, acc, sides, ready=None):
    size = ops.shape[2]
    for row, k, q in ((sides.off_row, sides.mate_k, 0), (sides.mate_row, sides.off_k, REACH)):
        step = REACH if ready is None else REACH // 2
        for low in range(0, REACH, step):
            if ready is not None:
                ready((q + low) // step)

            def some(ids, row=row, k=k, q=q, low=low):
                outs = []
                for i in ids:
                    r = row + low + i
                    e = sides.place(cols[k - 1, r])
                    x = [lanes(wide, REACH + q + low + i, size)[...], lanes(wide, e, size)[...]]
                    outs.append((q + low + i, dot_t(jnp.concatenate(x, 1), jnp.concatenate([ops[r, 0], ops[r, k]], 1))))
                for place, o in outs:
                    acc[place] = o

            chunks(step, some)


def first_inner(cols_in, off, mate, ops_far, acc, wide, ops, cols, sems):
    rows, _, size, _ = ops.shape
    sides = Sides(rows)
    step = REACH // 2
    copies = []
    for part in range(2 * REACH // step):
        start = (sides.off_row if part * step < REACH else sides.mate_row) + part * step % REACH
        where = pl.ds(start, step)
        copies.append(pltpu.make_async_copy(ops_far.at[where], ops.at[where], sems.at[part]))
        copies[-1].start()
    for k in range(cols.shape[0]):
        for r in range(rows):
            cols[k, r] = cols_in[k, r]
    wide[:, REACH * size : 2 * REACH * size] = off[:, : REACH * size]
    wide[:, 2 * REACH * size : 3 * REACH * size] = mate[...]
    inner(cols, wide, ops, acc, sides, lambda part: copies[part].wait())


def rim(cols, acc, wide, ops, sides, near, store):
    size = ops.shape[2]
    row, k, q = (sides.mate_row, sides.mate_k, REACH) if near else (sides.off_row, sides.off_k, 0)

    def some(ids):
        outs = []
        for i in ids:
            e = sides.place(cols[k - 1, row + i])
            outs.append((i, acc[q + i] + dot_t(lanes(wide, e, size)[...], ops[row + i, k])))
        for i, o in outs:
            store(i, o.astype(BF16))

    chunks(REACH, some)


def first_mate(cols, acc, wide_in, halo, ops, wide, out, send):
    size = ops.shape[2]
    out[:, : REACH * size] = jnp.zeros_like(halo)
    wide[:, 3 * REACH * size :] = halo[...]

    def store(i, o):
        lanes(out, 2 * REACH + i, size)[...] = o
        lanes(send, i, size)[...] = o

    rim(cols, acc, wide, ops, Sides(ops.shape[0]), True, store)


def first_off(cols, acc, wide_in, out_in, halo, ops, wide, out, send, slot, near_w, near_at, sums):
    size = ops.shape[2]
    width = REACH * size
    sides = Sides(ops.shape[0])
    wide[:, :width] = halo[:, :width]
    facts = halo[:, width:].astype(F32)
    weights = facts[:, :REACH] + facts[:, REACH : 2 * REACH]
    col = facts[:1, 2 * REACH : 3 * REACH] * 256.0 + facts[:1, 3 * REACH : 4 * REACH]
    near_w[...] = weights
    near_at[...] = sides.place(col.astype(I32))
    place = sides.place(as_column(col).astype(I32)) - REACH
    place = jnp.where((place >= 0) & (place < REACH), place, -1)
    slot[...] = jnp.broadcast_to(place, slot.shape)

    def store(i, o):
        lanes(out, REACH + i, size)[...] = o

    rim(cols, acc, wide, ops, sides, False, store)
    for p in range(REACH):
        at = slot[p, 0]
        x = lanes(out, REACH + jnp.maximum(at, 0), size)[...].astype(F32)
        part = jnp.sum(x * weights[:, p : p + 1], axis=0, keepdims=True)
        sums[p : p + 1, :] = jnp.where(at >= 0, part, 0.0)
    send[...] = sums[...].astype(BF16)


def turned(sides, w):
    swapped = jnp.concatenate([w[:, REACH:], w[:, :REACH]], 1)
    return jnp.where(sides.even, w, swapped)


def member_sums(value, start, w, first, count, size, store):
    for i in range(count):
        x = value[:, (start + i) * size : (start + i + 1) * size].astype(F32)
        store(i, jnp.sum(x * w[:, first + i : first + i + 1], axis=0, keepdims=True))


def rim_and_inner(col, sides):
    rim_off, rim_mate = sides.pick(col[:1, :REACH], col[1:, REACH:])
    inner_off, inner_mate = sides.pick(col[1:, :REACH], col[:1, REACH:])
    return [sides.place(part) for part in (rim_off, rim_mate, inner_off, inner_mate)]


def hop_rows(cols, col_rows, near_at, sides, shape):
    rim_off, _, inner_off, inner_mate = rim_and_inner(col_rows, sides)
    own = lax.broadcasted_iota(I32, (1, REACH), 1) + REACH
    blank = jnp.full((1, 3 * REACH), -1, I32)
    targets = (jnp.concatenate([own, rim_off, inner_off, inner_mate], 1), jnp.concatenate([near_at, blank], 1))
    found = [jnp.full(target.shape, -1, I32) for target in targets]
    for i in range(REACH):
        hop = sides.place(cols[sides.off_k - 1, sides.off_row + i])
        hop = jnp.where(hop < REACH, hop, -1)
        found = [jnp.where(target == REACH + i, hop, old) for target, old in zip(targets, found)]
    row = lax.broadcasted_iota(I32, shape, 0)
    first, second = [jnp.broadcast_to(part, shape) for part in found]
    return jnp.where(row == 0, first, jnp.where(row == 1, second, -1)).astype(F32).astype(BF16)


def second_inner(
    cols, wide, ops, w, innov, prec, col_rows, near_at, acc, inc, innov_rows, prec_rows, w_turned, two_off, inc_off, hops
):
    rows, _, size, _ = ops.shape
    sides = Sides(rows)
    inner(cols, wide, ops, acc, sides)
    weights = turned(sides, w[...])
    w_turned[...] = weights
    for q in range(rows):
        r = q + (sides.off_row if q < REACH else sides.mate_row - REACH)
        for time in range(2):
            place = slice(time * rows + q, time * rows + q + 1)
            innov_rows[place, :] = lanes(innov, r, size)[time : time + 1, :]
            prec_rows[place, :] = lanes(prec, r, size)[time : time + 1, :]

    def store(i, s):
        inc[i : i + 1, :] = s

    member_sums(wide, REACH, weights, 0, rows, size, store)

    def keep_row(i, o):
        lanes(two_off, i, size)[...] = o

    rim(cols, acc, wide, ops, sides, False, keep_row)

    def keep(i, s):
        inc_off[i : i + 1, :] = s

    member_sums(two_off, 0, weights, 0, REACH, size, keep)
    hops[...] = hop_rows(cols, col_rows[...], near_at[...], sides, hops.shape)


def second_mate(cols, acc, wide_in, halo, ops, w, wide, out, inc):
    size = ops.shape[2]
    wide[:, 3 * REACH * size :] = halo[...]

    def store(i, o):
        lanes(out, i, size)[...] = o

    rim(cols, acc, wide, ops, Sides(ops.shape[0]), True, store)

    def keep(i, s):
        inc[i : i + 1, :] = s

    member_sums(out, 0, w, REACH, REACH, size, keep)


def second_off(halo, ops, inc_one, inc_off, inc_mate, inc, send):
    rows, _, size, _ = ops.shape
    sides = Sides(rows)
    inc[:rows, :] = inc_one[...]
    inc[rows + REACH :, :] = inc_mate[...]
    parts = []
    for i in range(REACH):
        row = jnp.broadcast_to(halo[i : i + 1, :].astype(F32), (8, size)).astype(BF16)
        parts.append(dot_t(row, ops[sides.off_row + i, sides.off_k]))
    for i, part in enumerate(parts):
        inc[rows + i : rows + i + 1, :] = inc_off[i : i + 1, :] + part[:1]
    send[...] = inc[...].astype(BF16)


def cot_row(res, place):
    return jnp.broadcast_to(res[pl.ds(place, 1), :], (8, res.shape[1])).astype(BF16)


def rim_rows(res, ops, sides, near, out):
    rows = ops.shape[0]
    row, k, q = (sides.mate_row, sides.mate_k, REACH) if near else (sides.off_row, sides.off_k, 0)

    def some(ids):
        outs = [(i, dot_n(cot_row(res, rows + q + i), ops[row + i, k])) for i in ids]
        for i, o in outs:
            out[pl.ds(i, 1), :] = o[:1]

    chunks(REACH, some)


def residual_rim(cols, inc, innov, prec, ops, w, one, two_off, two_mate, hops, *rest):
    received = rest[:-5]
    res, rim_off, send_off, send_mate, gw = rest[-5:]
    rows, _, size, _ = ops.shape
    members = w.shape[0]
    sides = Sides(rows)
    total = inc[...]
    for other in received:
        total = total + other[...].astype(F32)
    res[...] = prec[...] * (total * SCALE - innov[...])
    rim_rows(res, ops, sides, False, rim_off)
    rim_rows(res, ops, sides, True, send_mate)
    send_off[:REACH, :] = rim_off[...].astype(BF16)
    send_mate[REACH:, :REACH] = w[:, REACH:]
    send_mate[REACH : REACH + 1, REACH : 2 * REACH] = sides.pick(cols[:1, :REACH], cols[1:, REACH:])[1].astype(F32)
    index = lax.broadcasted_iota(I32, (members, rows), 1)
    grown = jnp.zeros((members, rows), F32)
    for q in range(rows):
        two, place = (two_off, q) if q < REACH else (two_mate, q - REACH)
        prod = one[:, (REACH + q) * size : (REACH + q + 1) * size].astype(F32) * res[q : q + 1, :]
        prod = prod + two[:, place * size : (place + 1) * size].astype(F32) * res[rows + q : rows + q + 1, :]
        grown = jnp.where(index == q, jnp.sum(prod, axis=1, keepdims=True), grown)
    grown = w[...] + SCALE * grown
    gw[...] = grown
    terms = split_terms(grown[:, :REACH]) + split_terms(w[:, REACH:])
    send_off[REACH : REACH + members, :] = jnp.concatenate(terms, 1)
    send_off[REACH + members :, :] = hops[...]


def residual_inner(res, ops, y):
    rows, _, size, _ = ops.shape
    sides = Sides(rows)
    for row, k, q in ((sides.off_row, sides.mate_k, 0), (sides.mate_row, sides.off_k, REACH)):

        def some(ids, row=row, k=k, q=q):
            outs = []
            for i in ids:
                r = row + i
                o = dot_n(cot_row(res, rows + q + i), jnp.concatenate([ops[r, 0], ops[r, k]], 1))
                outs.append((q + i, o))
            for place, o in outs:
                y[pl.ds(place, 1), :] = o[:1, :size] + res[pl.ds(place, 1), :]
                y[pl.ds(rows + place, 1), :] = o[:1, size:]

        chunks(REACH, some)


def middle(weights, target, vals, q, mid):
    members = weights.shape[0]
    group = 8
    for g in range(REACH // group):
        place = REACH + q + g * group
        picked = [jnp.where(target == place + c, weights, 0.0).astype(BF16) for c in range(group)]
        mid[g * group * members : (g + 1) * group * members, :] = dot_n(jnp.concatenate(picked, 0), vals).astype(BF16)


def adjoint_side(cols, mid, ops, sides, near, sums):
    members = mid.shape[0] // REACH
    row, k, low = (sides.mate_row, sides.mate_k, 2 * REACH) if near else (sides.off_row, sides.off_k, 0)
    sums[...] = jnp.zeros_like(sums)

    def some(ids):
        outs = []
        for i in ids:
            x = mid[pl.ds(pl.multiple_of(i * members, members), members), :]
            outs.append((sides.place(cols[k - 1, row + i]) - low, dot_n(x, ops[row + i, k])))
        for place, o in outs:
            sums[place] = sums[place] + o

    chunks(REACH, some)


def adjoint_off(
    cols, col_rows, w, y, own_off, own_mate, off, mate, near_w, near_at, ops, one, gw, slot, send, vals, wp, tgt, squares, hop
):
    rows, _, size, _ = ops.shape
    members = w.shape[0]
    sides = Sides(rows)

    def point(k, row, i):
        return sides.place(cols[k - 1, row + i]) - REACH

    groups = (
        (y, 0, lambda i: i),
        (own_off, 0, lambda i: point(sides.off_k, sides.off_row, i)),
        (y, rows, lambda i: point(sides.mate_k, sides.off_row, i)),
        (y, rows + REACH, lambda i: point(sides.off_k, sides.mate_row, i)),
        (off, 0, lambda i: slot[i, 0]),
    )
    for n, (source, start, at) in enumerate(groups):
        outs = []
        for i in range(REACH):
            row = jnp.broadcast_to(source[start + i : start + i + 1, :].astype(F32), (8, size)).astype(BF16)
            place = jnp.clip(at(i), 0, REACH - 1)
            outs.append(dot_n(row, ops[sides.off_row + place, sides.off_k]))
        for i, o in enumerate(outs):
            hop[n * REACH + i : n * REACH + i + 1, :] = o[:1]
    send[: HOPS * REACH, :] = hop[...].astype(BF16)
    index = lax.broadcasted_iota(I32, (members, REACH), 1)
    drawn = jnp.zeros((members, REACH), F32)
    for p in range(REACH):
        at = slot[p, 0]
        x = lanes(one, REACH + jnp.maximum(at, 0), size)[...].astype(F32) * off[p : p + 1, :].astype(F32)
        part = jnp.where(at >= 0, jnp.sum(x, axis=1, keepdims=True), 0.0)
        drawn = jnp.where(index == p, part, drawn)
    drawn = drawn * SCALE
    high, low = split_terms(drawn)
    send[HOPS * REACH :, :] = jnp.concatenate([high, low, jnp.zeros((members, size - 2 * REACH), BF16)], 1)
    theirs = off[REACH : REACH + members, : 2 * REACH].astype(F32)
    theirs = theirs[:, :REACH] + theirs[:, REACH:]
    grown = gw[...]
    total = jnp.sum(grown * grown, axis=1, keepdims=True)
    total = total + jnp.sum((2.0 * theirs + drawn) * drawn, axis=1, keepdims=True)
    squares[...] = jnp.broadcast_to(total, squares.shape)
    vals[:rows, :] = y[:rows, :].astype(BF16)
    vals[2 * rows : 3 * rows, :] = y[rows:, :].astype(BF16)
    for n, part in enumerate((own_off, own_mate)):
        vals[rows + n * REACH : rows + (n + 1) * REACH, :] = part[:REACH, :].astype(BF16)
    for k in range(3):
        wp[:, k * rows : (k + 1) * rows] = w[...] * SCALE
    tgt[:, :rows] = lax.broadcasted_iota(I32, (1, rows), 1) + REACH
    for n, part in enumerate(rim_and_inner(col_rows[...], sides)):
        tgt[:, rows + n * REACH : rows + (n + 1) * REACH] = part
    where = slice(3 * rows, 3 * rows + REACH)
    vals[where, :] = off[:REACH, :]
    wp[:, where] = near_w[...] * SCALE
    tgt[:, where] = near_at[...]
    where = slice(3 * rows + REACH, 3 * rows + 2 * REACH)
    vals[where, :] = mate[:REACH, :].astype(BF16)
    wp[:, where] = mate[REACH:, :REACH] * SCALE
    tgt[:, where] = sides.place(mate[REACH : REACH + 1, REACH : 2 * REACH].astype(I32))


def adjoint_mate(cols, mid, ops, sums, send):
    adjoint_side(cols, mid, ops, Sides(ops.shape[0]), True, sums)
    send[...] = sums[REACH:].astype(BF16)


def adjoint_inner(cols, wp, tgt, vals, ops, w, near, near_w, out, spread, mid_mate, mid_off, sums_off):
    rows, _, size, _ = ops.shape
    members = w.shape[0]
    sides = Sides(rows)
    middle(wp[...], tgt[...], vals[...], 0, mid_off)
    middle(wp[...], tgt[...], vals[...], REACH, mid_mate)
    adjoint_side(cols, mid_off, ops, sides, False, sums_off)
    out[:REACH] = sums_off[REACH:]
    out[REACH:] = jnp.zeros((REACH, members, size), F32)
    for row, k, q, mid in ((sides.off_row, sides.mate_k, 0, mid_off), (sides.mate_row, sides.off_k, REACH, mid_mate)):

        def some(ids, row=row, k=k, q=q, mid=mid):
            outs = []
            for i in ids:
                r = row + i
                x = mid[pl.ds(i * members if isinstance(i, int) else pl.multiple_of(i * members, members), members), :]
                o = dot_n(x, jnp.concatenate([ops[r, 0], ops[r, k]], 1))
                outs.append((q + i, o[:, :size]))
                outs.append((sides.place(cols[k - 1, r]) - REACH, o[:, size:]))
            for place, o in outs:
                out[place] = out[place] + o

        chunks(REACH, some)
    terms = near[REACH : REACH + members, 2 * REACH :].astype(F32)
    far_w = terms[:, :REACH] + terms[:, REACH:]
    near_rows = near_w[...]
    blank = jnp.zeros((members, (8 - HOPS) * REACH), F32)
    weights = jnp.concatenate([near_rows, near_rows, near_rows, far_w, w[:, :REACH], blank], 1) * SCALE
    hops = near[REACH + members :, :].astype(F32)
    target = jnp.concatenate([hops[:1, :], hops[1:2, :]], 1)
    for c in range(REACH):
        spread[c * members : (c + 1) * members, :] = jnp.where(target == float(c), weights, 0.0).astype(BF16)


def finish(own, sums_mate, off, mate, spread, gw, total, mate_total, out, direction, vectors, *, count):
    rows, members, size = own.shape
    sides = Sides(rows)
    vectors[: HOPS * REACH, :] = off[: HOPS * REACH, :]
    vectors[HOPS * REACH :, :] = jnp.zeros(((8 - HOPS) * REACH, size), BF16)
    for i in range(REACH):
        lanes(out, sides.mate_row + i, size)[...] = own[REACH + i] + (sums_mate[i] + mate[i].astype(F32))
    group = 8
    for g in range(REACH // group):
        halo = dot_n(spread[g * group * members : (g + 1) * group * members, :], vectors[...])
        for c in range(group):
            i = g * group + c
            lanes(out, sides.off_row + i, size)[...] = own[i] + halo[c * members : (c + 1) * members, :]
    drawn = off[HOPS * REACH :, :].astype(F32)
    drawn = drawn[:, :REACH] + drawn[:, REACH : 2 * REACH]
    grown = gw[...]
    grown = jnp.concatenate([grown[:, :REACH] + drawn, grown[:, REACH:]], 1)
    mean = (total[:, :1] + mate_total[:, :1]) / count
    direction[...] = turned(sides, grown / jnp.sqrt(mean + 1e-06))


SMEM = pl.BlockSpec(memory_space=pltpu.SMEM)
VMEM = pl.BlockSpec(memory_space=pltpu.VMEM)
FAR = pl.BlockSpec(memory_space=pltpu.HBM)


def run(body, outs, args, scalars=0, scratch=(), far=0, alias=None, near=True, table=None, **fixed):
    kind_of = pltpu.VMEM if near else jax.ShapeDtypeStruct
    shapes = [kind_of(shape, kind) for shape, kind in outs]
    places = [VMEM] * len(outs)
    if table is not None:
        shapes.append(pltpu.SMEM(table, I32))
        places.append(SMEM)
    return pl.pallas_call(
        functools.partial(body, **fixed) if fixed else body,
        out_shape=shapes,
        in_specs=[SMEM] * scalars + [VMEM] * (len(args) - scalars - far) + [FAR] * far,
        out_specs=places,
        scratch_shapes=list(scratch),
        input_output_aliases=alias or {},
        compiler_params=pltpu.CompilerParams(vmem_limit_bytes=12 * 1024 * 1024),
        name=body.__name__,
    )(*args)


def on_device(ensemble, op_blocks, col_index, weights, innovations, obs_precision):
    members = ensemble.shape[0]
    rows, per_row, size, _ = op_blocks.shape
    assert rows == 2 * REACH and per_row == 3
    length = rows * size
    halo = REACH * size
    tiles = lax.axis_size("space")
    groups = lax.axis_size("members")
    mates = [(i, i ^ 1) for i in range(tiles)]
    offs = []
    for i in range(1, tiles - 1, 2):
        offs += [(i, i + 1), (i + 1, i)]
    sem = pltpu.SemaphoreType.DMA

    def far(value):
        return pltpu.with_memory_space_constraint(value, pltpu.HBM)

    def to_mate(value):
        return lax.ppermute(value, "space", mates)

    def to_off(value):
        return lax.ppermute(value, "space", offs)

    def partner(value, stride):
        return lax.ppermute(value, "space", [(i, i ^ stride) for i in range(tiles)])

    cols = col_index.T
    acc_kind = ((rows, members, size), F32)
    wide_kind = ((members, length + 2 * halo), BF16)
    side_kind = ((members, halo), BF16)
    part_kind = ((REACH, size), F32)
    row_kind = ((2 * rows, size), F32)

    off, mate = run(
        load,
        [((members, halo + 4 * REACH), BF16), side_kind],
        (far(ensemble), far(weights), far(cols)),
        0,
        [pltpu.VMEM((members, rows), F32), pltpu.VMEM(cols.shape, I32), sem((4,))],
        far=3,
    )
    from_off, from_mate = to_off(off), to_mate(mate)
    acc, wide, ops, table = run(
        first_inner,
        [acc_kind, wide_kind, (op_blocks.shape, BF16)],
        (cols, off, mate, far(op_blocks)),
        1,
        [sem((4,))],
        far=1,
        table=cols.shape,
    )
    wide, one, send = run(
        first_mate, [wide_kind, wide_kind, side_kind], (table, acc, wide, from_mate, ops), 1, alias={2: 0}
    )
    from_mate = to_mate(send)
    wide, one, send, slot, near_w, near_at = run(
        first_off,
        [
            wide_kind,
            wide_kind,
            ((REACH, size), BF16),
            ((REACH, size), I32),
            ((members, REACH), F32),
            ((1, REACH), I32),
        ],
        (table, acc, wide, one, from_off, ops),
        1,
        [pltpu.VMEM((REACH, size), F32)],
        alias={2: 0, 3: 1},
    )
    from_off = to_off(send)
    acc, inc_one, innov, prec, w, two_off, inc_off, hops = run(
        second_inner,
        [
            acc_kind,
            ((rows, size), F32),
            row_kind,
            row_kind,
            ((members, rows), F32),
            side_kind,
            part_kind,
            ((16, size), BF16),
        ],
        (table, one, ops, weights, innovations, obs_precision, cols, near_at),
        1,
    )
    one, two_mate, inc_mate = run(
        second_mate, [wide_kind, side_kind, part_kind], (table, acc, one, from_mate, ops, w), 1, alias={2: 0}
    )
    inc, send = run(second_off, [row_kind, (row_kind[0], BF16)], (from_off, ops, inc_one, inc_off, inc_mate))
    received = [lax.ppermute(send, "members", [(i, i ^ step) for i in range(groups)]) for step in range(1, groups)]
    pay_kind = ((REACH + members, size), F32)
    res, rim_off, own_off, own_mate, grad_weights = run(
        residual_rim,
        [row_kind, part_kind, ((REACH + members + 16, size), BF16), pay_kind, ((members, rows), F32)],
        (cols, inc, innov, prec, ops, w, one, two_off, two_mate, hops, *received),
    )
    from_off, from_mate = to_off(own_off), to_mate(own_mate)
    (y,) = run(residual_inner, [row_kind], (res, ops))
    pairs = 3 * rows + 2 * REACH
    mid_kind = ((REACH * members, size), BF16)
    sums_kind = ((2 * REACH, members, size), F32)
    send_kind = ((REACH, members, size), BF16)
    send, vals, wp, tgt, total = run(
        adjoint_off,
        [
            ((HOPS * REACH + members, size), BF16),
            ((pairs, size), BF16),
            ((members, pairs), F32),
            ((1, pairs), I32),
            ((members, size), F32),
        ],
        (table, cols, w, y, rim_off, own_mate, from_off, from_mate, near_w, near_at, ops, one, grad_weights, slot),
        1,
        [pltpu.VMEM((HOPS * REACH, size), F32)],
    )
    near = from_off
    from_off = to_off(send)
    total = total + partner(total, 2)
    own, spread, mid_mate = run(
        adjoint_inner,
        [acc_kind, ((REACH * members, 8 * REACH), BF16), mid_kind],
        (table, wp, tgt, vals, ops, w, near, near_w),
        1,
        [pltpu.VMEM(*mid_kind), pltpu.VMEM(*sums_kind)],
    )
    mid_mate, from_off, total = lax.optimization_barrier((mid_mate, from_off, total))
    stride = 4
    while stride < tiles:
        total = total + partner(total, stride)
        stride *= 2
    sums_mate, send = run(adjoint_mate, [sums_kind, send_kind], (table, mid_mate, ops), 1)
    from_mate = to_mate(send)
    mate_total = to_mate(total)
    grad_ens, direction = run(
        finish,
        [((members, length), F32), ((members, rows), F32)],
        (own, sums_mate, from_off, from_mate, spread, grad_weights, total, mate_total),
        0,
        [pltpu.VMEM((8 * REACH, size), BF16)],
        near=False,
        count=rows * tiles,
    )
    return (grad_ens, direction)


def solution(mesh):
    placed = (
        P("members", "space"),
        P("space", None, None, None),
        P("space", None),
        P("members", "space"),
        P(None, "space"),
        P(None, "space"),
    )
    return jax.shard_map(
        on_device,
        mesh=mesh,
        in_specs=placed,
        out_specs=(P("members", "space"), P("members", "space")),
        check_vma=False,
    )
```

```python
import functools

import jax
import jax.numpy as jnp
from jax import lax
from jax.experimental import pallas as pl
from jax.experimental.pallas import tpu as pltpu
from jax.sharding import PartitionSpec as P

MEMBERS = 128
REACH = 32
SCALE = (MEMBERS - 1) ** (-0.5)
F32 = jnp.float32
BF16 = jnp.bfloat16
I32 = jnp.int32
UNROLL = 32


def dot_t(x, a):
    return lax.dot_general(x, a, (((1,), (1,)), ((), ())), preferred_element_type=F32)


def dot_n(x, a):
    return lax.dot_general(x, a, (((1,), (0,)), ((), ())), preferred_element_type=F32)


class Sides:
    def __init__(self, rows):
        place = lax.axis_index("space")
        self.even = place % 2 == 0
        self.base = place * rows
        self.flip = jnp.where(self.even, 0, 3 * REACH)
        self.off_row = jnp.where(self.even, 0, REACH)
        self.mate_row = REACH - self.off_row
        self.off_k = jnp.where(self.even, 1, 2)
        self.mate_k = 3 - self.off_k

    def place(self, col):
        return (col - self.base + REACH) ^ self.flip

    def pick(self, first, last):
        return jnp.where(self.even, first, last), jnp.where(self.even, last, first)


def lanes(ref, index, size):
    return ref.at[:, pl.ds(index * size if isinstance(index, int) else pl.multiple_of(index * size, size), size)]


def chunks(total, body):
    unroll = min(total, UNROLL)

    def step(i, carry):
        body([i * unroll + u for u in range(unroll)])
        return carry

    if total == unroll:
        body(list(range(total)))
    else:
        lax.fori_loop(0, total // unroll, step, 0)


def split_terms(value):
    high = value.astype(BF16)
    return high, (value - high.astype(F32)).astype(BF16)


def as_column(row):
    count = row.shape[1]
    shape = (count, count)
    on = lax.broadcasted_iota(I32, shape, 0) == lax.broadcasted_iota(I32, shape, 1)
    return jnp.sum(jnp.where(on, jnp.broadcast_to(row.astype(F32), shape), 0.0), axis=1, keepdims=True)


def load(ens, w_far, cols_far, off, mate, w, cols, sems):
    size = ens.shape[1] // (2 * REACH)
    sides = Sides(2 * REACH)
    width = REACH * size
    copies = []
    for n, (row, out) in enumerate(((sides.off_row, off.at[:, :width]), (sides.mate_row, mate))):
        source = ens.at[:, pl.ds(pl.multiple_of(row * size, size), width)]
        copies.append(pltpu.make_async_copy(source, out, sems.at[n]))
    copies.append(pltpu.make_async_copy(w_far, w, sems.at[2]))
    copies.append(pltpu.make_async_copy(cols_far, cols, sems.at[3]))
    for copy in copies:
        copy.start()
    copies[3].wait()
    copies[2].wait()
    high, low = split_terms(sides.pick(w[:, :REACH], w[:, REACH:])[0])
    col = sides.pick(cols[:1, :REACH], cols[1:, REACH:])[0]
    spread = [jnp.broadcast_to(part.astype(F32), high.shape).astype(BF16) for part in (col >> 8, col & 255)]
    off[:, width:] = jnp.concatenate([high, low] + spread, 1)
    copies[1].wait()
    copies[0].wait()


def inner(cols, wide, ops, acc, sides, ready=None):
    size = ops.shape[2]
    for row, k, q in ((sides.off_row, sides.mate_k, 0), (sides.mate_row, sides.off_k, REACH)):
        step = REACH if ready is None else REACH // 2
        for low in range(0, REACH, step):
            if ready is not None:
                ready((q + low) // step)

            def some(ids, row=row, k=k, q=q, low=low):
                outs = []
                for i in ids:
                    r = row + low + i
                    e = sides.place(cols[k - 1, r])
                    x = [lanes(wide, REACH + q + low + i, size)[...], lanes(wide, e, size)[...]]
                    outs.append((q + low + i, dot_t(jnp.concatenate(x, 1), jnp.concatenate([ops[r, 0], ops[r, k]], 1))))
                for place, o in outs:
                    acc[place] = o

            chunks(step, some)


def first_inner(cols_in, off, mate, ops_far, acc, wide, ops, cols, sems):
    rows, _, size, _ = ops.shape
    sides = Sides(rows)
    step = REACH // 2
    copies = []
    for part in range(2 * REACH // step):
        start = (sides.off_row if part * step < REACH else sides.mate_row) + part * step % REACH
        where = pl.ds(start, step)
        copies.append(pltpu.make_async_copy(ops_far.at[where], ops.at[where], sems.at[part]))
        copies[-1].start()
    for k in range(cols.shape[0]):
        for r in range(rows):
            cols[k, r] = cols_in[k, r]
    wide[:, REACH * size : 2 * REACH * size] = off[:, : REACH * size]
    wide[:, 2 * REACH * size : 3 * REACH * size] = mate[...]
    inner(cols, wide, ops, acc, sides, lambda part: copies[part].wait())


def rim(cols, acc, wide, ops, sides, near, store):
    size = ops.shape[2]
    row, k, q = (sides.mate_row, sides.mate_k, REACH) if near else (sides.off_row, sides.off_k, 0)

    def some(ids):
        outs = []
        for i in ids:
            e = sides.place(cols[k - 1, row + i])
            outs.append((i, acc[q + i] + dot_t(lanes(wide, e, size)[...], ops[row + i, k])))
        for i, o in outs:
            store(i, o.astype(BF16))

    chunks(REACH, some)


def first_mate(cols, acc, wide_in, halo, ops, wide, out, send):
    size = ops.shape[2]
    out[:, : REACH * size] = jnp.zeros_like(halo)
    wide[:, 3 * REACH * size :] = halo[...]

    def store(i, o):
        lanes(out, 2 * REACH + i, size)[...] = o
        lanes(send, i, size)[...] = o

    rim(cols, acc, wide, ops, Sides(ops.shape[0]), True, store)


def first_off(cols, acc, wide_in, out_in, halo, ops, wide, out, send, slot, near_w, near_at, sums):
    size = ops.shape[2]
    width = REACH * size
    sides = Sides(ops.shape[0])
    wide[:, :width] = halo[:, :width]
    facts = halo[:, width:].astype(F32)
    weights = facts[:, :REACH] + facts[:, REACH : 2 * REACH]
    col = facts[:1, 2 * REACH : 3 * REACH] * 256.0 + facts[:1, 3 * REACH : 4 * REACH]
    near_w[...] = weights
    near_at[...] = sides.place(col.astype(I32))
    place = sides.place(as_column(col).astype(I32)) - REACH
    place = jnp.where((place >= 0) & (place < REACH), place, -1)
    slot[...] = jnp.broadcast_to(place, slot.shape)

    def store(i, o):
        lanes(out, REACH + i, size)[...] = o

    rim(cols, acc, wide, ops, sides, False, store)
    for p in range(REACH):
        at = slot[p, 0]
        x = lanes(out, REACH + jnp.maximum(at, 0), size)[...].astype(F32)
        part = jnp.sum(x * weights[:, p : p + 1], axis=0, keepdims=True)
        sums[p : p + 1, :] = jnp.where(at >= 0, part, 0.0)
    send[...] = sums[...].astype(BF16)


def turned(sides, w):
    swapped = jnp.concatenate([w[:, REACH:], w[:, :REACH]], 1)
    return jnp.where(sides.even, w, swapped)


def member_sums(value, start, w, first, count, size, store):
    for i in range(count):
        x = value[:, (start + i) * size : (start + i + 1) * size].astype(F32)
        store(i, jnp.sum(x * w[:, first + i : first + i + 1], axis=0, keepdims=True))


def second_inner(cols, wide, ops, w, innov, prec, acc, inc, innov_rows, prec_rows, w_turned, two_off, inc_off):
    rows, _, size, _ = ops.shape
    sides = Sides(rows)
    inner(cols, wide, ops, acc, sides)
    weights = turned(sides, w[...])
    w_turned[...] = weights
    for q in range(rows):
        r = q + (sides.off_row if q < REACH else sides.mate_row - REACH)
        for time in range(2):
            place = slice(time * rows + q, time * rows + q + 1)
            innov_rows[place, :] = lanes(innov, r, size)[time : time + 1, :]
            prec_rows[place, :] = lanes(prec, r, size)[time : time + 1, :]

    def store(i, s):
        inc[i : i + 1, :] = s

    member_sums(wide, REACH, weights, 0, rows, size, store)

    def keep_row(i, o):
        lanes(two_off, i, size)[...] = o

    rim(cols, acc, wide, ops, sides, False, keep_row)

    def keep(i, s):
        inc_off[i : i + 1, :] = s

    member_sums(two_off, 0, weights, 0, REACH, size, keep)


def second_mate(cols, acc, wide_in, halo, ops, w, wide, out, inc):
    size = ops.shape[2]
    wide[:, 3 * REACH * size :] = halo[...]

    def store(i, o):
        lanes(out, i, size)[...] = o

    rim(cols, acc, wide, ops, Sides(ops.shape[0]), True, store)

    def keep(i, s):
        inc[i : i + 1, :] = s

    member_sums(out, 0, w, REACH, REACH, size, keep)


def second_off(halo, ops, inc_one, inc_off, inc_mate, inc, send):
    rows, _, size, _ = ops.shape
    sides = Sides(rows)
    inc[:rows, :] = inc_one[...]
    inc[rows + REACH :, :] = inc_mate[...]
    parts = []
    for i in range(REACH):
        row = jnp.broadcast_to(halo[i : i + 1, :].astype(F32), (8, size)).astype(BF16)
        parts.append(dot_t(row, ops[sides.off_row + i, sides.off_k]))
    for i, part in enumerate(parts):
        inc[rows + i : rows + i + 1, :] = inc_off[i : i + 1, :] + part[:1]
    send[...] = inc[...].astype(BF16)


def cot_row(res, place):
    return jnp.broadcast_to(res[pl.ds(place, 1), :], (8, res.shape[1])).astype(BF16)


def rim_rows(res, ops, sides, near, out):
    rows = ops.shape[0]
    row, k, q = (sides.mate_row, sides.mate_k, REACH) if near else (sides.off_row, sides.off_k, 0)

    def some(ids):
        outs = [(i, dot_n(cot_row(res, rows + q + i), ops[row + i, k])) for i in ids]
        for i, o in outs:
            out[pl.ds(i, 1), :] = o[:1]

    chunks(REACH, some)


def residual_rim(cols, inc, innov, prec, ops, w, one, two_off, two_mate, *rest):
    received = rest[:-5]
    res, rim_off, send_off, send_mate, gw = rest[-5:]
    rows, _, size, _ = ops.shape
    members = w.shape[0]
    sides = Sides(rows)
    total = inc[...]
    for other in received:
        total = total + other[...].astype(F32)
    res[...] = prec[...] * (total * SCALE - innov[...])
    rim_rows(res, ops, sides, False, rim_off)
    rim_rows(res, ops, sides, True, send_mate)
    send_off[:REACH, :] = rim_off[...].astype(BF16)
    send_mate[REACH:, :REACH] = w[:, REACH:]
    send_mate[REACH : REACH + 1, REACH : 2 * REACH] = sides.pick(cols[:1, :REACH], cols[1:, REACH:])[1].astype(F32)
    index = lax.broadcasted_iota(I32, (members, rows), 1)
    grown = jnp.zeros((members, rows), F32)
    for q in range(rows):
        two, place = (two_off, q) if q < REACH else (two_mate, q - REACH)
        prod = one[:, (REACH + q) * size : (REACH + q + 1) * size].astype(F32) * res[q : q + 1, :]
        prod = prod + two[:, place * size : (place + 1) * size].astype(F32) * res[rows + q : rows + q + 1, :]
        grown = jnp.where(index == q, jnp.sum(prod, axis=1, keepdims=True), grown)
    grown = w[...] + SCALE * grown
    gw[...] = grown
    high, low = split_terms(grown[:, :REACH])
    send_off[REACH:, :] = jnp.concatenate([high, low, jnp.zeros((members, size - 2 * REACH), BF16)], 1)


def residual_inner(res, ops, y):
    rows, _, size, _ = ops.shape
    sides = Sides(rows)
    for row, k, q in ((sides.off_row, sides.mate_k, 0), (sides.mate_row, sides.off_k, REACH)):

        def some(ids, row=row, k=k, q=q):
            outs = []
            for i in ids:
                r = row + i
                o = dot_n(cot_row(res, rows + q + i), jnp.concatenate([ops[r, 0], ops[r, k]], 1))
                outs.append((q + i, o))
            for place, o in outs:
                y[pl.ds(place, 1), :] = o[:1, :size] + res[pl.ds(place, 1), :]
                y[pl.ds(rows + place, 1), :] = o[:1, size:]

        chunks(REACH, some)


def middle(weights, target, vals, q, mid):
    members = weights.shape[0]
    group = 8
    for g in range(REACH // group):
        place = REACH + q + g * group
        picked = [jnp.where(target == place + c, weights, 0.0).astype(BF16) for c in range(group)]
        mid[g * group * members : (g + 1) * group * members, :] = dot_n(jnp.concatenate(picked, 0), vals).astype(BF16)


def adjoint_side(cols, mid, ops, sides, near, sums):
    members = mid.shape[0] // REACH
    row, k, low = (sides.mate_row, sides.mate_k, 2 * REACH) if near else (sides.off_row, sides.off_k, 0)
    sums[...] = jnp.zeros_like(sums)

    def some(ids):
        outs = []
        for i in ids:
            x = mid[pl.ds(pl.multiple_of(i * members, members), members), :]
            outs.append((sides.place(cols[k - 1, row + i]) - low, dot_n(x, ops[row + i, k])))
        for place, o in outs:
            sums[place] = sums[place] + o

    chunks(REACH, some)


def adjoint_off(cols, col_rows, w, y, own_off, own_mate, off, mate, near_w, near_at, ops, one, gw, slot, mid, sums, send, vals, wp, tgt, squares):
    rows, _, size, _ = ops.shape
    members = w.shape[0]
    sides = Sides(rows)
    vals[:rows, :] = y[:rows, :].astype(BF16)
    vals[2 * rows : 3 * rows, :] = y[rows:, :].astype(BF16)
    for n, part in enumerate((own_off, own_mate)):
        vals[rows + n * REACH : rows + (n + 1) * REACH, :] = part[:REACH, :].astype(BF16)
    for k in range(3):
        wp[:, k * rows : (k + 1) * rows] = w[...] * SCALE
    col = col_rows[...]
    rim_off, rim_mate = sides.pick(col[:1, :REACH], col[1:, REACH:])
    inner_off, inner_mate = sides.pick(col[1:, :REACH], col[:1, REACH:])
    tgt[:, :rows] = lax.broadcasted_iota(I32, (1, rows), 1) + REACH
    for n, part in enumerate((rim_off, rim_mate, inner_off, inner_mate)):
        tgt[:, rows + n * REACH : rows + (n + 1) * REACH] = sides.place(part)
    where = slice(3 * rows, 3 * rows + REACH)
    vals[where, :] = off[:REACH, :]
    wp[:, where] = near_w[...] * SCALE
    tgt[:, where] = near_at[...]
    where = slice(3 * rows + REACH, 3 * rows + 2 * REACH)
    vals[where, :] = mate[:REACH, :].astype(BF16)
    wp[:, where] = mate[REACH:, :REACH] * SCALE
    tgt[:, where] = sides.place(mate[REACH : REACH + 1, REACH : 2 * REACH].astype(I32))
    middle(wp[...], tgt[...], vals[...], 0, mid)
    adjoint_side(cols, mid, ops, sides, False, sums)
    send[:REACH] = sums[:REACH].astype(BF16)
    index = lax.broadcasted_iota(I32, (members, REACH), 1)
    drawn = jnp.zeros((members, REACH), F32)
    for p in range(REACH):
        at = slot[p, 0]
        x = lanes(one, REACH + jnp.maximum(at, 0), size)[...].astype(F32) * off[p : p + 1, :].astype(F32)
        part = jnp.where(at >= 0, jnp.sum(x, axis=1, keepdims=True), 0.0)
        drawn = jnp.where(index == p, part, drawn)
    drawn = drawn * SCALE
    high, low = split_terms(drawn)
    send[REACH] = jnp.concatenate([high, low, jnp.zeros((members, size - 2 * REACH), BF16)], 1)
    theirs = off[REACH:, :REACH].astype(F32) + off[REACH:, REACH : 2 * REACH].astype(F32)
    grown = gw[...]
    total = jnp.sum(grown * grown, axis=1, keepdims=True)
    total = total + jnp.sum((2.0 * theirs + drawn) * drawn, axis=1, keepdims=True)
    squares[...] = jnp.broadcast_to(total, squares.shape)


def adjoint_mate(cols, wp, tgt, vals, ops, mid, sums, send):
    sides = Sides(ops.shape[0])
    middle(wp[...], tgt[...], vals[...], REACH, mid)
    adjoint_side(cols, mid, ops, sides, True, sums)
    send[...] = sums[REACH:].astype(BF16)


def adjoint_inner(cols, mid_off, mid_mate, sums_off, sums_mate, ops, out):
    rows, _, size, _ = ops.shape
    members = sums_off.shape[1]
    sides = Sides(rows)
    out[:REACH] = sums_off[REACH:]
    out[REACH:] = sums_mate[:REACH]
    for row, k, q, mid in ((sides.off_row, sides.mate_k, 0, mid_off), (sides.mate_row, sides.off_k, REACH, mid_mate)):

        def some(ids, row=row, k=k, q=q, mid=mid):
            outs = []
            for i in ids:
                r = row + i
                x = mid[pl.ds(pl.multiple_of(i * members, members), members), :]
                o = dot_n(x, jnp.concatenate([ops[r, 0], ops[r, k]], 1))
                outs.append((q + i, o[:, :size]))
                outs.append((sides.place(cols[k - 1, r]) - REACH, o[:, size:]))
            for place, o in outs:
                out[place] = out[place] + o

        chunks(REACH, some)


def write_side(own, q, halo, row, out, half, sems):
    size = own.shape[2]
    groups = sems.shape[0]
    step = REACH // groups
    copies = []
    for g in range(groups):
        for i in range(g * step, (g + 1) * step):
            half[:, i * size : (i + 1) * size] = own[q + i] + halo[i].astype(F32)
        part = half.at[:, g * step * size : (g + 1) * step * size]
        place = out.at[:, pl.ds(pl.multiple_of((row + g * step) * size, size), step * size)]
        copies.append(pltpu.make_async_copy(part, place, sems.at[g]))
        copies[-1].start()
    return copies


def finish_mate(own, mate, out, half, sems):
    sides = Sides(own.shape[0])
    for copy in write_side(own, REACH, mate, sides.mate_row, out, half, sems):
        copy.wait()


def finish_off(own, off, gw, total, mate_total, out_in, out, direction, half, sems, *, count):
    sides = Sides(own.shape[0])
    copies = write_side(own, 0, off, sides.off_row, out, half, sems)
    drawn = off[REACH].astype(F32)
    drawn = drawn[:, :REACH] + drawn[:, REACH : 2 * REACH]
    grown = gw[...]
    grown = jnp.concatenate([grown[:, :REACH] + drawn, grown[:, REACH:]], 1)
    mean = (total[:, :1] + mate_total[:, :1]) / count
    direction[...] = turned(sides, grown / jnp.sqrt(mean + 1e-06))
    for copy in copies:
        copy.wait()


SMEM = pl.BlockSpec(memory_space=pltpu.SMEM)
VMEM = pl.BlockSpec(memory_space=pltpu.VMEM)
FAR = pl.BlockSpec(memory_space=pltpu.HBM)


def run(body, outs, args, scalars=0, scratch=(), far=0, alias=None, near=True, far_outs=0, table=None, **fixed):
    kind_of = pltpu.VMEM if near else jax.ShapeDtypeStruct
    shapes = [kind_of(shape, kind) for shape, kind in outs]
    places = [FAR] * far_outs + [VMEM] * (len(outs) - far_outs)
    if table is not None:
        shapes.append(pltpu.SMEM(table, I32))
        places.append(SMEM)
    return pl.pallas_call(
        functools.partial(body, **fixed) if fixed else body,
        out_shape=shapes,
        in_specs=[SMEM] * scalars + [VMEM] * (len(args) - scalars - far) + [FAR] * far,
        out_specs=places,
        scratch_shapes=list(scratch),
        input_output_aliases=alias or {},
        compiler_params=pltpu.CompilerParams(vmem_limit_bytes=12 * 1024 * 1024),
        name=body.__name__,
    )(*args)


def on_device(ensemble, op_blocks, col_index, weights, innovations, obs_precision):
    members = ensemble.shape[0]
    rows, per_row, size, _ = op_blocks.shape
    assert rows == 2 * REACH and per_row == 3
    length = rows * size
    halo = REACH * size
    tiles = lax.axis_size("space")
    groups = lax.axis_size("members")
    mates = [(i, i ^ 1) for i in range(tiles)]
    offs = []
    for i in range(1, tiles - 1, 2):
        offs += [(i, i + 1), (i + 1, i)]
    sem = pltpu.SemaphoreType.DMA

    def far(value):
        return pltpu.with_memory_space_constraint(value, pltpu.HBM)

    def to_mate(value):
        return lax.ppermute(value, "space", mates)

    def to_off(value):
        return lax.ppermute(value, "space", offs)

    def partner(value, stride):
        return lax.ppermute(value, "space", [(i, i ^ stride) for i in range(tiles)])

    cols = col_index.T
    acc_kind = ((rows, members, size), F32)
    wide_kind = ((members, length + 2 * halo), BF16)
    side_kind = ((members, halo), BF16)
    part_kind = ((REACH, size), F32)
    row_kind = ((2 * rows, size), F32)

    off, mate = run(
        load,
        [((members, halo + 4 * REACH), BF16), side_kind],
        (far(ensemble), far(weights), far(cols)),
        0,
        [pltpu.VMEM((members, rows), F32), pltpu.VMEM(cols.shape, I32), sem((4,))],
        far=3,
    )
    from_off, from_mate = to_off(off), to_mate(mate)
    acc, wide, ops, table = run(
        first_inner,
        [acc_kind, wide_kind, (op_blocks.shape, BF16)],
        (cols, off, mate, far(op_blocks)),
        1,
        [sem((4,))],
        far=1,
        table=cols.shape,
    )
    wide, one, send = run(
        first_mate, [wide_kind, wide_kind, side_kind], (table, acc, wide, from_mate, ops), 1, alias={2: 0}
    )
    from_mate = to_mate(send)
    wide, one, send, slot, near_w, near_at = run(
        first_off,
        [
            wide_kind,
            wide_kind,
            ((REACH, size), BF16),
            ((REACH, size), I32),
            ((members, REACH), F32),
            ((1, REACH), I32),
        ],
        (table, acc, wide, one, from_off, ops),
        1,
        [pltpu.VMEM((REACH, size), F32)],
        alias={2: 0, 3: 1},
    )
    from_off = to_off(send)
    acc, inc_one, innov, prec, w, two_off, inc_off = run(
        second_inner,
        [acc_kind, ((rows, size), F32), row_kind, row_kind, ((members, rows), F32), side_kind, part_kind],
        (table, one, ops, weights, innovations, obs_precision),
        1,
    )
    one, two_mate, inc_mate = run(
        second_mate, [wide_kind, side_kind, part_kind], (table, acc, one, from_mate, ops, w), 1, alias={2: 0}
    )
    inc, send = run(second_off, [row_kind, (row_kind[0], BF16)], (from_off, ops, inc_one, inc_off, inc_mate))
    received = [lax.ppermute(send, "members", [(i, i ^ step) for i in range(groups)]) for step in range(1, groups)]
    pay_kind = ((REACH + members, size), F32)
    res, rim_off, own_off, own_mate, grad_weights = run(
        residual_rim,
        [row_kind, part_kind, (pay_kind[0], BF16), pay_kind, ((members, rows), F32)],
        (cols, inc, innov, prec, ops, w, one, two_off, two_mate, *received),
    )
    from_off, from_mate = to_off(own_off), to_mate(own_mate)
    (y,) = run(residual_inner, [row_kind], (res, ops))
    pairs = 3 * rows + 2 * REACH
    mid_kind = ((REACH * members, size), BF16)
    sums_kind = ((2 * REACH, members, size), F32)
    send_kind = ((REACH, members, size), BF16)
    mid_off, sums_off, send, vals, wp, tgt, total = run(
        adjoint_off,
        [
            mid_kind,
            sums_kind,
            ((REACH + 1, members, size), BF16),
            ((pairs, size), BF16),
            ((members, pairs), F32),
            ((1, pairs), I32),
            ((members, size), F32),
        ],
        (table, cols, w, y, rim_off, own_mate, from_off, from_mate, near_w, near_at, ops, one, grad_weights, slot),
        1,
    )
    from_off = to_off(send)
    total = total + partner(total, 2)
    mid_mate, sums_mate, send = run(
        adjoint_mate, [mid_kind, sums_kind, send_kind], (table, wp, tgt, vals, ops), 1
    )
    send, total = lax.optimization_barrier((send, total))
    from_mate = to_mate(send)
    stride = 4
    while stride < tiles:
        total = total + partner(total, stride)
        stride *= 2
    (own,) = run(adjoint_inner, [acc_kind], (table, mid_off, mid_mate, sums_off, sums_mate, ops), 1)
    total, own = lax.optimization_barrier((total, own))
    mate_total = to_mate(total)
    half = pltpu.VMEM((members, halo), F32)
    grad_kind = ((members, length), F32)
    (grad_ens,) = run(finish_mate, [grad_kind], (own, from_mate), 0, [half, sem((4,))], near=False, far_outs=1)
    grad_ens, direction = run(
        finish_off,
        [grad_kind, ((members, rows), F32)],
        (own, from_off, grad_weights, total, mate_total, grad_ens),
        0,
        [half, sem((4,))],
        far=1,
        alias={5: 0},
        near=False,
        far_outs=1,
        count=rows * tiles,
    )
    return (grad_ens, direction)


def solution(mesh):
    placed = (
        P("members", "space"),
        P("space", None, None, None),
        P("space", None),
        P("members", "space"),
        P(None, "space"),
        P(None, "space"),
    )
    return jax.shard_map(
        on_device,
        mesh=mesh,
        in_specs=placed,
        out_specs=(P("members", "space"), P("members", "space")),
        check_vma=False,
    )
```

```python
import functools

import jax
import jax.numpy as jnp
from jax import lax
from jax.experimental import pallas as pl
from jax.experimental.pallas import tpu as pltpu
from jax.sharding import PartitionSpec as P

MEMBERS = 128
REACH = 32
SCALE = (MEMBERS - 1) ** (-0.5)
F32 = jnp.float32
BF16 = jnp.bfloat16
I32 = jnp.int32
UNROLL = 32


def dot_t(x, a):
    return lax.dot_general(x, a, (((1,), (1,)), ((), ())), preferred_element_type=F32)


def dot_n(x, a):
    return lax.dot_general(x, a, (((1,), (0,)), ((), ())), preferred_element_type=F32)


class Sides:
    def __init__(self, rows):
        place = lax.axis_index("space")
        self.even = place % 2 == 0
        self.base = place * rows
        self.flip = jnp.where(self.even, 0, 3 * REACH)
        self.off_row = jnp.where(self.even, 0, REACH)
        self.mate_row = REACH - self.off_row
        self.off_k = jnp.where(self.even, 1, 2)
        self.mate_k = 3 - self.off_k

    def place(self, col):
        return (col - self.base + REACH) ^ self.flip

    def pick(self, first, last):
        return jnp.where(self.even, first, last), jnp.where(self.even, last, first)


def lanes(ref, index, size):
    return ref.at[:, pl.ds(index * size if isinstance(index, int) else pl.multiple_of(index * size, size), size)]


def chunks(total, body):
    unroll = min(total, UNROLL)

    def step(i, carry):
        body([i * unroll + u for u in range(unroll)])
        return carry

    if total == unroll:
        body(list(range(total)))
    else:
        lax.fori_loop(0, total // unroll, step, 0)


def split_terms(value):
    high = value.astype(BF16)
    return high, (value - high.astype(F32)).astype(BF16)


def as_column(row):
    count = row.shape[1]
    shape = (count, count)
    on = lax.broadcasted_iota(I32, shape, 0) == lax.broadcasted_iota(I32, shape, 1)
    return jnp.sum(jnp.where(on, jnp.broadcast_to(row.astype(F32), shape), 0.0), axis=1, keepdims=True)


def load(ens, w_far, cols_far, off, mate, w, cols, sems):
    size = ens.shape[1] // (2 * REACH)
    sides = Sides(2 * REACH)
    width = REACH * size
    small = [pltpu.make_async_copy(w_far, w, sems.at[0]), pltpu.make_async_copy(cols_far, cols, sems.at[1])]
    large = []
    step = 16
    for row, out in ((sides.off_row, off), (sides.mate_row, mate)):
        for m in range(0, ens.shape[0], step):
            source = ens.at[m : m + step, pl.ds(pl.multiple_of(row * size, size), width)]
            large.append(pltpu.make_async_copy(source, out.at[m : m + step, :width], sems.at[2 + len(large)]))
    for copy in small + large:
        copy.start()
    for copy in small:
        copy.wait()
    high, low = split_terms(sides.pick(w[:, :REACH], w[:, REACH:])[0])
    col = sides.pick(cols[:1, :REACH], cols[1:, REACH:])[0]
    spread = [jnp.broadcast_to(part.astype(F32), high.shape).astype(BF16) for part in (col >> 8, col & 255)]
    off[:, width:] = jnp.concatenate([high, low] + spread, 1)
    for copy in large:
        copy.wait()


def inner(cols, wide, ops, acc, sides, ready=None):
    size = ops.shape[2]
    for row, k, q in ((sides.off_row, sides.mate_k, 0), (sides.mate_row, sides.off_k, REACH)):
        step = REACH if ready is None else REACH // 2
        for low in range(0, REACH, step):
            if ready is not None:
                ready((q + low) // step)

            def some(ids, row=row, k=k, q=q, low=low):
                outs = []
                for i in ids:
                    r = row + low + i
                    e = sides.place(cols[k - 1, r])
                    x = [lanes(wide, REACH + q + low + i, size)[...], lanes(wide, e, size)[...]]
                    outs.append((q + low + i, dot_t(jnp.concatenate(x, 1), jnp.concatenate([ops[r, 0], ops[r, k]], 1))))
                for place, o in outs:
                    acc[place] = o

            chunks(step, some)


def first_inner(cols_in, off, mate, ops_far, acc, wide, ops, cols, sems):
    rows, _, size, _ = ops.shape
    sides = Sides(rows)
    step = REACH // 2
    copies = []
    for part in range(2 * REACH // step):
        start = (sides.off_row if part * step < REACH else sides.mate_row) + part * step % REACH
        where = pl.ds(start, step)
        copies.append(pltpu.make_async_copy(ops_far.at[where], ops.at[where], sems.at[part]))
        copies[-1].start()
    for k in range(cols.shape[0]):
        for r in range(rows):
            cols[k, r] = cols_in[k, r]
    wide[:, REACH * size : 2 * REACH * size] = off[:, : REACH * size]
    wide[:, 2 * REACH * size : 3 * REACH * size] = mate[...]
    inner(cols, wide, ops, acc, sides, lambda part: copies[part].wait())


def rim(cols, acc, wide, ops, sides, near, store):
    size = ops.shape[2]
    row, k, q = (sides.mate_row, sides.mate_k, REACH) if near else (sides.off_row, sides.off_k, 0)

    def some(ids):
        outs = []
        for i in ids:
            e = sides.place(cols[k - 1, row + i])
            outs.append((i, acc[q + i] + dot_t(lanes(wide, e, size)[...], ops[row + i, k])))
        for i, o in outs:
            store(i, o.astype(BF16))

    chunks(REACH, some)


def first_mate(cols, acc, wide_in, halo, ops, wide, out, send):
    size = ops.shape[2]
    out[:, : REACH * size] = jnp.zeros_like(halo)
    wide[:, 3 * REACH * size :] = halo[...]

    def store(i, o):
        lanes(out, 2 * REACH + i, size)[...] = o
        lanes(send, i, size)[...] = o

    rim(cols, acc, wide, ops, Sides(ops.shape[0]), True, store)


def first_off(cols, acc, wide_in, out_in, halo, ops, wide, out, send, slot, near_w, near_at, sums):
    size = ops.shape[2]
    width = REACH * size
    sides = Sides(ops.shape[0])
    wide[:, :width] = halo[:, :width]
    facts = halo[:, width:].astype(F32)
    weights = facts[:, :REACH] + facts[:, REACH : 2 * REACH]
    col = facts[:1, 2 * REACH : 3 * REACH] * 256.0 + facts[:1, 3 * REACH : 4 * REACH]
    near_w[...] = weights
    near_at[...] = sides.place(col.astype(I32))
    place = sides.place(as_column(col).astype(I32)) - REACH
    place = jnp.where((place >= 0) & (place < REACH), place, -1)
    slot[...] = jnp.broadcast_to(place, slot.shape)

    def store(i, o):
        lanes(out, REACH + i, size)[...] = o

    rim(cols, acc, wide, ops, sides, False, store)
    for p in range(REACH):
        at = slot[p, 0]
        x = lanes(out, REACH + jnp.maximum(at, 0), size)[...].astype(F32)
        part = jnp.sum(x * weights[:, p : p + 1], axis=0, keepdims=True)
        sums[p : p + 1, :] = jnp.where(at >= 0, part, 0.0)
    send[...] = sums[...].astype(BF16)


def turned(sides, w):
    swapped = jnp.concatenate([w[:, REACH:], w[:, :REACH]], 1)
    return jnp.where(sides.even, w, swapped)


def member_sums(value, start, w, first, count, size, store):
    for i in range(count):
        x = value[:, (start + i) * size : (start + i + 1) * size].astype(F32)
        store(i, jnp.sum(x * w[:, first + i : first + i + 1], axis=0, keepdims=True))


def second_inner(cols, wide, ops, w, innov, prec, acc, inc, innov_rows, prec_rows, w_turned, two_off, inc_off):
    rows, _, size, _ = ops.shape
    sides = Sides(rows)
    inner(cols, wide, ops, acc, sides)
    weights = turned(sides, w[...])
    w_turned[...] = weights
    for q in range(rows):
        r = q + (sides.off_row if q < REACH else sides.mate_row - REACH)
        for time in range(2):
            place = slice(time * rows + q, time * rows + q + 1)
            innov_rows[place, :] = lanes(innov, r, size)[time : time + 1, :]
            prec_rows[place, :] = lanes(prec, r, size)[time : time + 1, :]

    def store(i, s):
        inc[i : i + 1, :] = s

    member_sums(wide, REACH, weights, 0, rows, size, store)

    def keep_row(i, o):
        lanes(two_off, i, size)[...] = o

    rim(cols, acc, wide, ops, sides, False, keep_row)

    def keep(i, s):
        inc_off[i : i + 1, :] = s

    member_sums(two_off, 0, weights, 0, REACH, size, keep)


def second_mate(cols, acc, wide_in, halo, ops, w, wide, out, inc):
    size = ops.shape[2]
    wide[:, 3 * REACH * size :] = halo[...]

    def store(i, o):
        lanes(out, i, size)[...] = o

    rim(cols, acc, wide, ops, Sides(ops.shape[0]), True, store)

    def keep(i, s):
        inc[i : i + 1, :] = s

    member_sums(out, 0, w, REACH, REACH, size, keep)


def second_off(halo, ops, inc_one, inc_off, inc_mate, inc, send):
    rows, _, size, _ = ops.shape
    sides = Sides(rows)
    inc[:rows, :] = inc_one[...]
    inc[rows + REACH :, :] = inc_mate[...]
    parts = []
    sums = halo[...].astype(F32)
    for i in range(REACH):
        row = jnp.broadcast_to(sums[i : i + 1, :], (8, size)).astype(BF16)
        parts.append(dot_t(row, ops[sides.off_row + i, sides.off_k]))
    for i, part in enumerate(parts):
        inc[rows + i : rows + i + 1, :] = inc_off[i : i + 1, :] + part[:1]
    send[...] = inc[...].astype(BF16)


def cot_row(res, place):
    return jnp.broadcast_to(res[pl.ds(place, 1), :], (8, res.shape[1])).astype(BF16)


def rim_rows(res, ops, sides, near, out):
    rows = ops.shape[0]
    row, k, q = (sides.mate_row, sides.mate_k, REACH) if near else (sides.off_row, sides.off_k, 0)

    def some(ids):
        outs = [(i, dot_n(cot_row(res, rows + q + i), ops[row + i, k])) for i in ids]
        for i, o in outs:
            out[pl.ds(i, 1), :] = o[:1]

    chunks(REACH, some)


def residual_rim(cols, inc, innov, prec, ops, w, one, two_off, two_mate, *rest):
    received = rest[:-5]
    res, rim_off, send_off, send_mate, gw = rest[-5:]
    rows, _, size, _ = ops.shape
    members = w.shape[0]
    sides = Sides(rows)
    total = inc[...]
    for other in received:
        total = total + other[...].astype(F32)
    res[...] = prec[...] * (total * SCALE - innov[...])
    rim_rows(res, ops, sides, False, rim_off)
    rim_rows(res, ops, sides, True, send_mate)
    send_off[:REACH, :] = rim_off[...].astype(BF16)
    send_mate[REACH:, :REACH] = w[:, REACH:]
    send_mate[REACH : REACH + 1, REACH : 2 * REACH] = sides.pick(cols[:1, :REACH], cols[1:, REACH:])[1].astype(F32)
    index = lax.broadcasted_iota(I32, (members, rows), 1)
    grown = jnp.zeros((members, rows), F32)
    for q in range(rows):
        two, place = (two_off, q) if q < REACH else (two_mate, q - REACH)
        prod = one[:, (REACH + q) * size : (REACH + q + 1) * size].astype(F32) * res[q : q + 1, :]
        prod = prod + two[:, place * size : (place + 1) * size].astype(F32) * res[rows + q : rows + q + 1, :]
        grown = jnp.where(index == q, jnp.sum(prod, axis=1, keepdims=True), grown)
    grown = w[...] + SCALE * grown
    gw[...] = grown
    high, low = split_terms(grown[:, :REACH])
    send_off[REACH:, :] = jnp.concatenate([high, low, jnp.zeros((members, size - 2 * REACH), BF16)], 1)


def residual_inner(res, ops, w, cols, rim_off, own_mate, near_w, near_at, vals, wp, tgt, y):
    rows, _, size, _ = ops.shape
    sides = Sides(rows)
    for row, k, q in ((sides.off_row, sides.mate_k, 0), (sides.mate_row, sides.off_k, REACH)):

        def some(ids, row=row, k=k, q=q):
            outs = []
            for i in ids:
                r = row + i
                o = dot_n(cot_row(res, rows + q + i), jnp.concatenate([ops[r, 0], ops[r, k]], 1))
                outs.append((q + i, o))
            for place, o in outs:
                y[pl.ds(place, 1), :] = o[:1, :size] + res[pl.ds(place, 1), :]
                y[pl.ds(rows + place, 1), :] = o[:1, size:]

        chunks(REACH, some)
    vals[:rows, :] = y[:rows, :].astype(BF16)
    vals[2 * rows : 3 * rows, :] = y[rows:, :].astype(BF16)
    for n, part in enumerate((rim_off, own_mate)):
        vals[rows + n * REACH : rows + (n + 1) * REACH, :] = part[:REACH, :].astype(BF16)
    for k in range(3):
        wp[:, k * rows : (k + 1) * rows] = w[...] * SCALE
    col = cols[...]
    rims = sides.pick(col[:1, :REACH], col[1:, REACH:])
    inners = sides.pick(col[1:, :REACH], col[:1, REACH:])
    tgt[:, :rows] = lax.broadcasted_iota(I32, (1, rows), 1) + REACH
    for n, part in enumerate(rims + inners):
        tgt[:, rows + n * REACH : rows + (n + 1) * REACH] = sides.place(part)
    wp[:, 3 * rows : 3 * rows + REACH] = near_w[...] * SCALE
    tgt[:, 3 * rows : 3 * rows + REACH] = near_at[...]


def middle(weights, target, vals, q, mid):
    members = weights.shape[0]
    group = 8
    for g in range(REACH // group):
        place = REACH + q + g * group
        picked = [jnp.where(target == place + c, weights, 0.0).astype(BF16) for c in range(group)]
        mid[g * group * members : (g + 1) * group * members, :] = dot_n(jnp.concatenate(picked, 0), vals).astype(BF16)


def adjoint_side(cols, mid, ops, sides, near, sums):
    members = mid.shape[0] // REACH
    row, k, low = (sides.mate_row, sides.mate_k, 2 * REACH) if near else (sides.off_row, sides.off_k, 0)
    sums[...] = jnp.zeros_like(sums)

    def some(ids):
        outs = []
        for i in ids:
            x = mid[pl.ds(pl.multiple_of(i * members, members), members), :]
            outs.append((sides.place(cols[k - 1, row + i]) - low, dot_n(x, ops[row + i, k])))
        for place, o in outs:
            sums[place] = sums[place] + o

    chunks(REACH, some)


def adjoint_off(
    cols, vals_in, wp_in, tgt_in, off, mate, ops, one, gw, slot, mid, sums, send, vals, wp, tgt, squares
):
    rows, _, size, _ = ops.shape
    members = gw.shape[0]
    sides = Sides(rows)
    vals[3 * rows : 3 * rows + REACH, :] = off[:REACH, :]
    where = slice(3 * rows + REACH, 3 * rows + 2 * REACH)
    vals[where, :] = mate[:REACH, :].astype(BF16)
    wp[:, where] = mate[REACH:, :REACH] * SCALE
    tgt[:, where] = sides.place(mate[REACH : REACH + 1, REACH : 2 * REACH].astype(I32))
    middle(wp[...], tgt[...], vals[...], 0, mid)
    adjoint_side(cols, mid, ops, sides, False, sums)
    send[:REACH] = sums[:REACH].astype(BF16)
    index = lax.broadcasted_iota(I32, (members, REACH), 1)
    drawn = jnp.zeros((members, REACH), F32)
    for p in range(REACH):
        at = slot[p, 0]
        x = lanes(one, REACH + jnp.maximum(at, 0), size)[...].astype(F32) * off[p : p + 1, :].astype(F32)
        part = jnp.where(at >= 0, jnp.sum(x, axis=1, keepdims=True), 0.0)
        drawn = jnp.where(index == p, part, drawn)
    drawn = drawn * SCALE
    high, low = split_terms(drawn)
    send[REACH] = jnp.concatenate([high, low, jnp.zeros((members, size - 2 * REACH), BF16)], 1)
    theirs = off[REACH:, :REACH].astype(F32) + off[REACH:, REACH : 2 * REACH].astype(F32)
    grown = gw[...]
    total = jnp.sum(grown * grown, axis=1, keepdims=True)
    total = total + jnp.sum((2.0 * theirs + drawn) * drawn, axis=1, keepdims=True)
    squares[...] = jnp.broadcast_to(total, squares.shape)


def adjoint_mate(cols, wp, tgt, vals, ops, mid, sums, send):
    sides = Sides(ops.shape[0])
    middle(wp[...], tgt[...], vals[...], REACH, mid)
    adjoint_side(cols, mid, ops, sides, True, sums)
    send[...] = sums[REACH:].astype(BF16)


def adjoint_inner(cols, mid_off, mid_mate, sums_off, sums_mate, ops, out):
    rows, _, size, _ = ops.shape
    members = sums_off.shape[1]
    sides = Sides(rows)
    out[:REACH] = sums_off[REACH:]
    out[REACH:] = sums_mate[:REACH]
    for row, k, q, mid in ((sides.off_row, sides.mate_k, 0, mid_off), (sides.mate_row, sides.off_k, REACH, mid_mate)):

        def some(ids, row=row, k=k, q=q, mid=mid):
            outs = []
            for i in ids:
                r = row + i
                x = mid[pl.ds(pl.multiple_of(i * members, members), members), :]
                o = dot_n(x, jnp.concatenate([ops[r, 0], ops[r, k]], 1))
                outs.append((q + i, o[:, :size]))
                outs.append((sides.place(cols[k - 1, r]) - REACH, o[:, size:]))
            for place, o in outs:
                out[place] = out[place] + o

        chunks(REACH, some)


def write_side(own, q, halos, row, out, half, sems):
    size = own.shape[2]
    groups = sems.shape[0]
    step = REACH // groups
    copies = []
    for g in range(groups):
        for i in range(g * step, (g + 1) * step):
            value = own[q + i]
            for halo in halos:
                value = value + halo[i].astype(F32)
            half[:, i * size : (i + 1) * size] = value
        part = half.at[:, g * step * size : (g + 1) * step * size]
        place = out.at[:, pl.ds(pl.multiple_of((row + g * step) * size, size), step * size)]
        copies.append(pltpu.make_async_copy(part, place, sems.at[g]))
        copies[-1].start()
    return copies


def finish_mate(own, mate, out, half, sems):
    sides = Sides(own.shape[0])
    for copy in write_side(own, REACH, [mate], sides.mate_row, out, half, sems):
        copy.wait()


def finish_off(own, far, near, gw, total, mate_total, out_in, out, direction, half, normal, sems, sem, *, count):
    sides = Sides(own.shape[0])
    copies = write_side(own, 0, [far, near], sides.off_row, out, half, sems)
    drawn = far[REACH].astype(F32) + near[REACH].astype(F32)
    drawn = drawn[:, :REACH] + drawn[:, REACH : 2 * REACH]
    grown = gw[...]
    grown = jnp.concatenate([grown[:, :REACH] + drawn, grown[:, REACH:]], 1)
    mean = (total[:, :1] + mate_total[:, :1]) / count
    normal[...] = turned(sides, grown / jnp.sqrt(mean + 1e-06))
    copies.append(pltpu.make_async_copy(normal, direction, sem))
    copies[-1].start()
    for copy in copies:
        copy.wait()


SMEM = pl.BlockSpec(memory_space=pltpu.SMEM)
VMEM = pl.BlockSpec(memory_space=pltpu.VMEM)
FAR = pl.BlockSpec(memory_space=pltpu.HBM)


def run(body, outs, args, scalars=0, scratch=(), far=0, alias=None, near=True, far_outs=0, table=None, **fixed):
    kind_of = pltpu.VMEM if near else jax.ShapeDtypeStruct
    shapes = [kind_of(shape, kind) for shape, kind in outs]
    places = [FAR] * far_outs + [VMEM] * (len(outs) - far_outs)
    if table is not None:
        shapes.append(pltpu.SMEM(table, I32))
        places.append(SMEM)
    return pl.pallas_call(
        functools.partial(body, **fixed) if fixed else body,
        out_shape=shapes,
        in_specs=[SMEM] * scalars + [VMEM] * (len(args) - scalars - far) + [FAR] * far,
        out_specs=places,
        scratch_shapes=list(scratch),
        input_output_aliases=alias or {},
        compiler_params=pltpu.CompilerParams(vmem_limit_bytes=12 * 1024 * 1024),
        name=body.__name__,
    )(*args)


def on_device(ensemble, op_blocks, col_index, weights, innovations, obs_precision):
    members = ensemble.shape[0]
    rows, per_row, size, _ = op_blocks.shape
    assert rows == 2 * REACH and per_row == 3
    length = rows * size
    halo = REACH * size
    tiles = lax.axis_size("space")
    groups = lax.axis_size("members")
    mates = [(i, i ^ 1) for i in range(tiles)]
    far_edges, near_edges = [], []
    for i in range(1, tiles - 1, 2):
        edges = near_edges if i % 4 == 1 else far_edges
        edges += [(i, i + 1), (i + 1, i)]
    sem = pltpu.SemaphoreType.DMA

    def far(value):
        return pltpu.with_memory_space_constraint(value, pltpu.HBM)

    def to_mate(value):
        return lax.ppermute(value, "space", mates)

    def to_off(value):
        return lax.ppermute(value, "space", far_edges + near_edges)

    def to_far(value):
        return lax.ppermute(value, "space", far_edges)

    def to_near(value):
        return lax.ppermute(value, "space", near_edges)

    def partner(value, stride):
        return lax.ppermute(value, "space", [(i, i ^ stride) for i in range(tiles)])

    cols = col_index.T
    acc_kind = ((rows, members, size), F32)
    wide_kind = ((members, length + 2 * halo), BF16)
    side_kind = ((members, halo), BF16)
    part_kind = ((REACH, size), F32)
    row_kind = ((2 * rows, size), F32)

    off, mate = run(
        load,
        [((members, halo + 4 * REACH), BF16), side_kind],
        (far(ensemble), far(weights), far(cols)),
        0,
        [pltpu.VMEM((members, rows), F32), pltpu.VMEM(cols.shape, I32), sem((2 + members // 8,))],
        far=3,
    )
    from_off, from_mate = to_off(off), to_mate(mate)
    acc, wide, ops, table = run(
        first_inner,
        [acc_kind, wide_kind, (op_blocks.shape, BF16)],
        (cols, off, mate, far(op_blocks)),
        1,
        [sem((4,))],
        far=1,
        table=cols.shape,
    )
    wide, one, send = run(
        first_mate, [wide_kind, wide_kind, side_kind], (table, acc, wide, from_mate, ops), 1, alias={2: 0}
    )
    from_mate = to_mate(send)
    wide, one, send, slot, near_w, near_at = run(
        first_off,
        [
            wide_kind,
            wide_kind,
            ((REACH, size), BF16),
            ((REACH, size), I32),
            ((members, REACH), F32),
            ((1, REACH), I32),
        ],
        (table, acc, wide, one, from_off, ops),
        1,
        [pltpu.VMEM((REACH, size), F32)],
        alias={2: 0, 3: 1},
    )
    from_off = to_off(send)
    acc, inc_one, innov, prec, w, two_off, inc_off = run(
        second_inner,
        [acc_kind, ((rows, size), F32), row_kind, row_kind, ((members, rows), F32), side_kind, part_kind],
        (table, one, ops, weights, innovations, obs_precision),
        1,
    )
    one, two_mate, inc_mate = run(
        second_mate, [wide_kind, side_kind, part_kind], (table, acc, one, from_mate, ops, w), 1, alias={2: 0}
    )
    inc, send = run(second_off, [row_kind, (row_kind[0], BF16)], (from_off, ops, inc_one, inc_off, inc_mate))
    received = [lax.ppermute(send, "members", [(i, i ^ step) for i in range(groups)]) for step in range(1, groups)]
    pay_kind = ((REACH + members, size), F32)
    res, rim_off, own_off, own_mate, grad_weights = run(
        residual_rim,
        [row_kind, part_kind, (pay_kind[0], BF16), pay_kind, ((members, rows), F32)],
        (cols, inc, innov, prec, ops, w, one, two_off, two_mate, *received),
    )
    from_off, from_mate = to_off(own_off), to_mate(own_mate)
    pairs = 3 * rows + 2 * REACH
    pair_kinds = [((pairs, size), BF16), ((members, pairs), F32), ((1, pairs), I32)]
    vals, wp, tgt = run(
        residual_inner,
        pair_kinds,
        (res, ops, w, cols, rim_off, own_mate, near_w, near_at),
        0,
        [pltpu.VMEM(*row_kind)],
    )
    mid_kind = ((REACH * members, size), BF16)
    sums_kind = ((2 * REACH, members, size), F32)
    send_kind = ((REACH, members, size), BF16)
    mid_off, sums_off, send, vals, wp, tgt, total = run(
        adjoint_off,
        [mid_kind, sums_kind, ((REACH + 1, members, size), BF16), *pair_kinds, ((members, size), F32)],
        (table, vals, wp, tgt, from_off, from_mate, ops, one, grad_weights, slot),
        1,
        alias={1: 3, 2: 4, 3: 5},
    )
    from_near, from_far = to_near(send), to_far(send)
    total = total + partner(total, 2)
    mid_mate, sums_mate, send = run(
        adjoint_mate, [mid_kind, sums_kind, send_kind], (table, wp, tgt, vals, ops), 1
    )
    send, total = lax.optimization_barrier((send, total))
    from_mate = to_mate(send)
    stride = 4
    while stride < tiles:
        total = total + partner(total, stride)
        stride *= 2
    (own,) = run(adjoint_inner, [acc_kind], (table, mid_off, mid_mate, sums_off, sums_mate, ops), 1)
    total, own = lax.optimization_barrier((total, own))
    mate_total = to_mate(total)
    half = pltpu.VMEM((members, halo), F32)
    grad_kind = ((members, length), F32)
    (grad_ens,) = run(finish_mate, [grad_kind], (own, from_mate), 0, [half, sem((2,))], near=False, far_outs=1)
    grad_ens, direction = run(
        finish_off,
        [grad_kind, ((members, rows), F32)],
        (own, from_far, from_near, grad_weights, total, mate_total, grad_ens),
        0,
        [half, pltpu.VMEM((members, rows), F32), sem((2,)), sem(())],
        far=1,
        alias={6: 0},
        near=False,
        far_outs=2,
        count=rows * tiles,
    )
    return (grad_ens, direction)


def solution(mesh):
    placed = (
        P("members", "space"),
        P("space", None, None, None),
        P("space", None),
        P("members", "space"),
        P(None, "space"),
        P(None, "space"),
    )
    return jax.shard_map(
        on_device,
        mesh=mesh,
        in_specs=placed,
        out_specs=(P("members", "space"), P("members", "space")),
        check_vma=False,
    )
```
